128 devices in a mesh: mem: 4 (over x), space: 32 (over y, z, core).
Axes of the slice: x: 4, y: 4, z: 4, core: 2. Of those that a mesh axis runs over, the one named last changes fastest.
Arguments:
- log_perm: float32 [8, 128, 128, 128], P('mem', 'space'), may hold values from -4 to 4
- saturation: float32 [128, 128, 128], P('space'), may hold values from 0.1 to 0.9
- pressure_init: float32 [128, 128, 128], P('space'), may hold values from -3 to 3
- wells: int32 [64], replicated, may hold values from 0 to 2097151
- well_rate: float32 [64], replicated, may hold values from -4 to 4
- obs_index: int32 [512, 8], replicated, may hold values from 0 to 2097151, as said below
- obs_weight: float32 [512, 8], replicated, may hold values from -2 to 2
- obs_value: float32 [512], replicated, may hold values from -5 to 5
- obs_var: float32 [512], replicated, may hold values from 0.1 to 1
- noise: float32 [8, 512], replicated, may hold values from -5 to 5
Outputs:
- updated_perm: float32 [8, 128, 128, 128], P(None, 'space', 'mem')
The draws below stay inside these ranges and needn't reach their ends.
Inputs may be any that keep to these rules, and one draw needn't show every extreme that they name: `obs_index`: observation o reads only cells of the grid row o % 128 along the first dimension.
All inputs are finite; a program needn't handle non-finite values.
Results may differ from the reference program's by a relative error of at most 0.00007.
Values sent between devices are 32-bit elements; how exact they have to be, the bound alone decides.
No kernel may reach another device: no remote copies, remote signals or barrier semaphores. Data moves between devices by JAX's collectives and lax.ppermute only.
A program may use at most 128 MiB of HBM per device.

```python
import math
import jax
import jax.numpy as jnp
from jax import lax

NY = 128
NZ = 128
SWEEPS = 6
NOBS = 512
TAPS = 8
WELLS = 64
ENS = 8
NX = 128


def well_cells(key):
    first = jax.random.randint(jax.random.fold_in(key, 11), (WELLS,), 0, NX)
    second = jax.random.randint(jax.random.fold_in(key, 12), (WELLS,), 0, NY)
    third = jax.random.randint(jax.random.fold_in(key, 13), (WELLS,), 0, NZ)
    return (first, second, third)


def draw_wells(key, part):
    first, second, third = well_cells(key)
    return ((first * NY + second) * NZ + third).astype(jnp.int32)


def draw_obs_index(key, part):
    row = (jnp.arange(NOBS) % NX).astype(jnp.int32)
    centre_y = jax.random.randint(jax.random.fold_in(key, 21), (NOBS,), 0, NY)
    centre_z = jax.random.randint(jax.random.fold_in(key, 22), (NOBS,), 0, NZ)
    offsets = jax.random.randint(jax.random.fold_in(key, 23), (NOBS, TAPS, 2), -2, 3)
    cell_y = jnp.clip(centre_y[:, None] + offsets[:, :, 0], 0, NY - 1)
    cell_z = jnp.clip(centre_z[:, None] + offsets[:, :, 1], 0, NZ - 1)
    return ((row[:, None] * NY + cell_y) * NZ + cell_z).astype(jnp.int32)


def block_levels(key, dims, pieces, least, high):
    level, own = 1.0, jax.random.fold_in(key, 6)
    for position, parts in pieces:
        draws = jnp.exp(jax.random.uniform(jax.random.fold_in(own, position), (parts,), jnp.float32, least / len(pieces), high / len(pieces)))
        level = level * jnp.repeat(draws, dims[position] // parts).reshape([-1 if axis == position else 1 for axis in range(len(dims))])
    return level


def gaussian(stream_key, extent, width, most, pieces=(), dtype=jnp.bfloat16):
    result = width * jax.random.normal(stream_key, extent, jnp.float32)
    if pieces:
        result = result * block_levels(stream_key, extent, pieces, -0.22, 0.18)
    return jnp.clip(result, -most, most).astype(dtype)


def setup_inputs(seed: int = 0) -> dict:
    key_of = jax.random.split(jax.random.key(seed), 11)
    log_perm = gaussian(key_of[0], (ENS, NX, NY, NZ), 1.0, 4.0, ((0, 4), (1, 32)), jnp.float32)
    saturation = jnp.clip(0.1 + 0.79999997 * jax.random.uniform(key_of[1], (NX, NY, NZ), jnp.float32) ** block_levels(key_of[1], (NX, NY, NZ), ((0, 32),), -0.2, 0.2), 0.1, 0.9)
    pressure_init = gaussian(key_of[2], (NX, NY, NZ), 0.5, 3.0, ((0, 32),), jnp.float32)
    wells = draw_wells(jax.random.fold_in(key_of[10], 71), 0)
    well_rate = jnp.clip(jax.random.uniform(key_of[4], (WELLS,), jnp.float32, -4.0, 4.0), -4.0, 4.0)
    obs_index = draw_obs_index(jax.random.fold_in(key_of[10], 71), 0)
    obs_weight = gaussian(key_of[6], (NOBS, TAPS), TAPS ** -0.5, 2.0, (), jnp.float32)
    obs_value = gaussian(key_of[7], (NOBS,), 1.0, 5.0, (), jnp.float32)
    obs_var = jnp.clip(jnp.exp(jax.random.uniform(key_of[8], (NOBS,), jnp.float32, math.log(0.1), math.log(1.0))), 0.1, 1.0)
    noise = gaussian(key_of[9], (ENS, NOBS), 1.0, 5.0, (), jnp.float32)
    return dict(log_perm=log_perm, saturation=saturation, pressure_init=pressure_init, wells=wells, well_rate=well_rate, obs_index=obs_index, obs_weight=obs_weight, obs_value=obs_value, obs_var=obs_var, noise=noise)


water_visc = 1.0
oil_visc = 4.0
time_step = 0.1
storage = 1.0
inflation = 4.0

def pad_cells(field):
    return jnp.pad(field, ((1, 1), (1, 1), (1, 1)))

def beside_all(field):
    return [field[2:, 1:-1, 1:-1], field[:-2, 1:-1, 1:-1], field[1:-1, 2:, 1:-1], field[1:-1, :-2, 1:-1], field[1:-1, 1:-1, 2:], field[1:-1, 1:-1, :-2]]

def middle(field):
    return field[1:-1, 1:-1, 1:-1]

def props(perm, sat):
    water = sat * sat / water_visc
    oil = (1.0 - sat) * (1.0 - sat) / oil_visc
    total = water + oil
    return (perm * total, water / total)

def saturate(perm_pad, sat_pad, press_pad, source):
    lam, frac = props(perm_pad, sat_pad)
    lam_mid, frac_mid, press_mid = (middle(lam), middle(frac), middle(press_pad))
    outflow = jnp.zeros_like(lam_mid)
    for lam_next, frac_next, press_next in zip(beside_all(lam), beside_all(frac), beside_all(press_pad)):
        flux = 0.5 * (lam_mid + lam_next) * (press_mid - press_next)
        outflow = outflow + jnp.maximum(flux, 0.0) * frac_mid + jnp.minimum(flux, 0.0) * frac_next
    water = jnp.maximum(source, 0.0) + jnp.minimum(source, 0.0) * frac_mid
    return jnp.clip(middle(sat_pad) + time_step * (water - outflow), 0.0, 1.0)

def pressure(perm_pad, sat_pad, press_pad, source):
    lam, frac = props(perm_pad, sat_pad)
    lam_mid = middle(lam)
    numer = storage * middle(press_pad) + source
    denom = storage + jnp.zeros_like(lam_mid)
    for lam_next, press_next in zip(beside_all(lam), beside_all(press_pad)):
        trans = 0.5 * (lam_mid + lam_next)
        numer = numer + trans * press_next
        denom = denom + trans
    return numer / denom

def reference(log_perm, saturation, pressure_init, wells, well_rate, obs_index, obs_weight, obs_value, obs_var, noise):
    source = jnp.zeros((NX * NY * NZ,), jnp.float32).at[wells].add(well_rate).reshape(NX, NY, NZ)

    def member(member_log):
        perm_pad = pad_cells(jnp.exp(member_log))
        sat, press = (saturation, pressure_init)
        for sweep in range(SWEEPS):
            sat = saturate(perm_pad, pad_cells(sat), pad_cells(press), source)
            press = pressure(perm_pad, pad_cells(sat), pad_cells(press), source)
        flat = press.reshape(-1)
        return lax.optimization_barrier(jnp.sum(obs_weight * flat[obs_index], axis=1))
    predicted = lax.map(member, log_perm)
    high = lax.Precision.HIGHEST
    dev = predicted - lax.optimization_barrier(jnp.mean(predicted, axis=0, keepdims=True))
    cov = jnp.dot(dev.T, dev, precision=high) / (ENS - 1) + inflation * jnp.diag(obs_var)
    resid = obs_value[None, :] + jnp.sqrt(inflation * obs_var)[None, :] * noise - predicted
    factor = jnp.linalg.cholesky(cov)
    half = lax.linalg.triangular_solve(factor, resid.T, left_side=True, lower=True)
    solved = lax.linalg.triangular_solve(factor, half, left_side=True, lower=True, transpose_a=True)
    weights = jnp.dot(dev, solved, precision=high) / (ENS - 1)
    spread = log_perm - lax.optimization_barrier(jnp.mean(log_perm, axis=0, keepdims=True))
    return log_perm + jnp.tensordot(weights.T, spread, axes=1, precision=high)
```

```python
import functools

import jax
import jax.numpy as jnp
from jax import lax
from jax.experimental import pallas as pl
from jax.experimental.pallas import tpu as pltpu
from jax.sharding import PartitionSpec as P


INFLATION = 4.0
STEP = 0.1
PAD = 8
CHUNK = 32
HIGH = lax.Precision.HIGHEST
ANY = pl.BlockSpec(memory_space=pl.ANY)
SMEM = pl.BlockSpec(memory_space=pltpu.SMEM)
VMEM = pl.BlockSpec(memory_space=pltpu.VMEM)

S0, P0, S1, P1, S2, L2 = (0, 1), (2, 3, 4), (5, 6, 7), (8, 9, 10), 11, 12
PLANES = 13


def spot(row):
    return row + 1 + (row >= 4)


class Tile:
    def __init__(self, lam_a, lam_b, frac_a, frac_b, p_a, p_b, s_a, s_b, perm, q, ny, cut):
        self.lam = (lam_a, lam_b)
        self.frac = (frac_a, frac_b)
        self.p = (p_a, p_b)
        self.s = (s_a, s_b)
        self.perm = perm
        self.q = q
        self.ny = ny
        self.cut = cut

    def clear(self):
        for ref in self.lam + self.frac + self.p:
            wide = ref.shape[2]
            edge = jnp.zeros((PAD, wide), jnp.float32)

            def one(r, carry, ref=ref, edge=edge):
                ref[r, 0:PAD, :] = edge
                ref[r, PAD + self.ny : PAD + self.ny + PAD, :] = edge
                return carry

            lax.fori_loop(0, ref.shape[0], one, 0)
            ref[5, :, :] = jnp.zeros(ref.shape[1:], jnp.float32)

    def rows(self, first, last, fn):
        def one(row, carry):
            far = row >= 4
            st = row + 1 + far.astype(jnp.int32)
            joined = 1 - self.cut
            up = st + 1 + jnp.where(row == 3, joined, 0)
            down = st - 1 - jnp.where(row == 4, joined, 0)
            for y0 in range(0, self.ny, CHUNK):
                fn(row, st, up, down, y0)
            return carry

        lax.fori_loop(first, last + 1, one, 0)

    def props(self, level, first, last):
        def fn(row, st, up, down, y0):
            inner = pl.ds(y0, CHUNK)
            sat = self.s[level][st, inner, :]
            lam, frac = props(self.perm[row, inner, :], sat)
            self.lam[level][st, pl.ds(PAD + y0, CHUNK), :] = lam
            self.frac[level][st, pl.ds(PAD + y0, CHUNK), :] = frac

        self.rows(first, last, fn)

    def saturate(self, level, first, last):
        lam_r, frac_r, p_r = self.lam[level], self.frac[level], self.p[level]
        new = 1 - level
        lanes = lam_r.shape[2]
        lane = lax.broadcasted_iota(jnp.int32, (CHUNK, lanes), 1)
        is_first, is_last = lane == 0, lane == lanes - 1

        def fn(row, st, up, down, y0):
            inner = pl.ds(PAD + y0, CHUNK)
            lam, frac, press = lam_r[st, inner, :], frac_r[st, inner, :], p_r[st, inner, :]

            def face(index, where):
                flux = (lam + lam_r[index, where, :]) * (press - p_r[index, where, :])
                return flux * jnp.where(flux > 0.0, frac, frac_r[index, where, :])

            out = face(up, inner) + face(down, inner)
            out = out + face(st, pl.ds(PAD + y0 + 1, CHUNK))
            out = out + face(st, pl.ds(PAD + y0 - 1, CHUNK))
            flux = (lam + pltpu.roll(lam, lanes - 1, 1)) * (press - pltpu.roll(press, lanes - 1, 1))
            moved = flux * jnp.where(flux > 0.0, frac, pltpu.roll(frac, lanes - 1, 1))
            edge = jnp.maximum(lam * press, 0.0) * frac
            out = out + jnp.where(is_last, edge, moved)
            out = out + jnp.where(is_first, edge, pltpu.roll(-moved, 1, 1))
            q = self.q[row, pl.ds(y0, CHUNK), :]
            water = jnp.maximum(q, 0.0) + jnp.minimum(q, 0.0) * frac
            sat = self.s[level][st, pl.ds(y0, CHUNK), :]
            sat = jnp.clip(sat + STEP * (water - out), 0.0, 1.0)
            self.s[new][st, pl.ds(y0, CHUNK), :] = sat
            lam, frac = props(self.perm[row, pl.ds(y0, CHUNK), :], sat)
            self.lam[new][st, inner, :] = lam
            self.frac[new][st, inner, :] = frac

        self.rows(first, last, fn)

    def pressure(self, level, first, last):
        new = 1 - level
        lam_r, p_r, out_r = self.lam[new], self.p[level], self.p[new]
        lanes = lam_r.shape[2]
        lane = lax.broadcasted_iota(jnp.int32, (CHUNK, lanes), 1)
        not_first, not_last = lane > 0, lane < lanes - 1

        def fn(row, st, up, down, y0):
            inner = pl.ds(PAD + y0, CHUNK)
            lam, press = lam_r[st, inner, :], p_r[st, inner, :]
            numer = press + self.q[row, pl.ds(y0, CHUNK), :]
            denom = jnp.ones_like(lam)
            for index, where in (
                (up, inner),
                (down, inner),
                (st, pl.ds(PAD + y0 + 1, CHUNK)),
                (st, pl.ds(PAD + y0 - 1, CHUNK)),
            ):
                trans = lam + lam_r[index, where, :]
                numer = numer + trans * p_r[index, where, :]
                denom = denom + trans
            for shift, mask in ((lanes - 1, not_last), (1, not_first)):
                trans = lam + jnp.where(mask, pltpu.roll(lam, shift, 1), 0.0)
                numer = numer + trans * jnp.where(mask, pltpu.roll(press, shift, 1), 0.0)
                denom = denom + trans
            out_r[st, inner, :] = numer / denom

        self.rows(first, last, fn)

    def expand(self):
        self.props(0, 2, 5)
        self.props(1, 0, 2)
        self.props(1, 5, 7)
        self.saturate(0, 3, 4)
        self.pressure(0, 2, 5)
        self.saturate(1, 1, 6)
        self.pressure(1, 0, 7)

    def shrink(self):
        self.saturate(0, 1, 6)
        self.pressure(0, 2, 5)
        self.saturate(1, 3, 4)


def props(perm_half, sat):
    water = sat * sat
    oil = (1.0 - sat) * (1.0 - sat) * 0.25
    total = water + oil
    return perm_half * total, water / total


def tile_scratch(ny, nz):
    tall = ny + 2 * PAD
    wide = [pltpu.VMEM((11, tall, nz), jnp.float32) for _ in range(6)]
    flat = [pltpu.VMEM((11, ny, nz), jnp.float32) for _ in range(2)]
    own = [pltpu.VMEM((8, ny, nz), jnp.float32) for _ in range(2)]
    return wide + flat + own


def issue(pairs, sems, first):
    copies = []
    for n, (src, dst) in enumerate(pairs):
        copy = pltpu.make_async_copy(src, dst, sems.at[first + n])
        copy.start()
        copies.append(copy)
    return copies


def drain(copies):
    for copy in copies:
        copy.wait()


def beyond(tile, row):
    return jnp.where(tile.cut == 1, 5, spot(row))


def give_early(tile, keep, send, send_early):
    pairs = []
    inner = pl.ds(PAD, tile.ny)
    for d in range(2):
        pairs.append((tile.s[0].at[spot(d)], keep.at[S0[d]]))
    for d in range(3):
        pairs.append((tile.p[0].at[spot(d), inner], keep.at[P0[d]]))
    if send_early:
        for d in range(2):
            pairs.append((tile.s[0].at[spot(7 - d)], send.at[S0[d]]))
        for d in range(3):
            pairs.append((tile.p[0].at[spot(7 - d), inner], send.at[P0[d]]))
    return pairs


def give_late(tile, out, near, base):
    row, step = near
    inner = pl.ds(PAD, tile.ny)
    pairs = []
    for n, d in enumerate((1, 2, 3)):
        pairs.append((tile.s[1].at[spot(row + step * d)], out.at[S1[n] - base]))
    for n, d in enumerate((2, 3, 4)):
        st = beyond(tile, row + step * d) if d == 4 else spot(row + step * d)
        pairs.append((tile.p[1].at[st, inner], out.at[P1[n] - base]))
    return pairs


def give_last(tile, out, near, base):
    row, step = near
    inner = pl.ds(PAD, tile.ny)
    return [
        (tile.s[0].at[spot(row + step * 3)], out.at[S2 - base]),
        (tile.lam[0].at[beyond(tile, row + step * 4), inner], out.at[L2 - base]),
    ]


def take_side(tile, src, early, late, base_row, step):
    del src
    inner = pl.ds(PAD, tile.ny)
    pairs = []
    for d in range(2):
        pairs.append((early(S0[d]), tile.s[0].at[base_row + step * d]))
    for d in range(3):
        pairs.append((early(P0[d]), tile.p[0].at[base_row + step * d, inner]))
    for n, d in enumerate((1, 2, 3)):
        pairs.append((late(S1[n]), tile.s[1].at[base_row + step * d]))
    for n, d in enumerate((2, 3, 4)):
        pairs.append((late(P1[n]), tile.p[1].at[base_row + step * d, inner]))
    return pairs


def take_last(tile, late, base_row, step):
    inner = pl.ds(PAD, tile.ny)
    return [
        (late(S2), tile.s[0].at[base_row + step * 3]),
        (late(L2), tile.lam[0].at[base_row + step * 4, inner]),
    ]


def advance(tile, keep, send, sems, first, send_early):
    base = 0 if send_early else S1[0]
    early = issue(give_early(tile, keep, send, send_early), sems, first)
    first += len(early)
    tile.saturate(0, 1, 6)
    tile.pressure(0, 2, 5)
    late = issue(
        give_late(tile, send, (7, -1), base) + give_late(tile, keep, (0, 1), 0), sems, first
    )
    first += len(late)
    drain(early)
    tile.saturate(1, 3, 4)
    last = issue(
        give_last(tile, send, (7, -1), base) + give_last(tile, keep, (0, 1), 0), sems, first
    )
    drain(late)
    drain(last)


def first_kernel(flags, own_log, own_sat, own_press, swapped, q, keep, send, perm_out, *refs):
    tile = Tile(*refs[:10], own_log.shape[1], jnp.int32(0))
    raw, sems = refs[10], refs[11]
    odd = flags[0]
    inner = pl.ds(PAD, tile.ny)

    def place(n):
        return jnp.where(odd == 1, 3 - n, n)

    pairs = [(own_log, raw.at[pl.ds(0, 4)]), (swapped.at[pl.ds(0, 4)], raw.at[pl.ds(4, 4)])]
    pairs.append((q, tile.q))
    for n in range(4):
        pairs.append((own_sat.at[place(n)], tile.s[0].at[spot(n)]))
        pairs.append((own_press.at[place(n)], tile.p[0].at[spot(n), inner]))
        pairs.append((swapped.at[4 + place(n)], tile.s[0].at[spot(4 + n)]))
        pairs.append((swapped.at[8 + place(n)], tile.p[0].at[spot(4 + n), inner]))
    copies = issue(pairs, sems, 0)
    tile.clear()
    drain(copies)

    def halve(row, carry):
        at = row - (row & 3) + place(row & 3)
        for y0 in range(0, tile.ny, CHUNK):
            tile.perm[row, pl.ds(y0, CHUNK), :] = 0.5 * jnp.exp(raw[at, pl.ds(y0, CHUNK), :])
        return carry

    lax.fori_loop(0, 8, halve, 0)
    perm_copy = issue([(tile.perm, perm_out)], sems, len(pairs))
    tile.props(0, 0, 7)
    advance(tile, keep, send, sems, len(pairs) + 1, False)
    drain(perm_copy)


def second_kernel(flags, kept, raw_in, late_in, perm_own, q, keep, send, perm_out, *refs):
    tile = Tile(*refs[:10], kept.shape[1], flags[1])
    raw, sems = refs[10], refs[11]
    odd = flags[0]

    def place(n, count):
        return jnp.where(odd == 1, n, count - 1 - n)

    def early(plane):
        if plane in S0:
            return raw_in.at[4 + place(plane, 2)]
        return raw_in.at[6 + place(plane - 2, 3)]

    pairs = [(raw_in.at[pl.ds(0, 4)], raw), (q, tile.q)]
    for d in range(4):
        pairs.append((perm_own.at[d], tile.perm.at[3 - d]))
    pairs += take_side(tile, None, lambda n: kept.at[n], lambda n: kept.at[n], 4, -1)
    pairs += take_side(tile, None, early, lambda n: late_in.at[n - S1[0]], 6, 1)
    last = take_last(tile, lambda n: kept.at[n], 4, -1)
    last += take_last(tile, lambda n: late_in.at[n - S1[0]], 6, 1)
    copies = issue(pairs, sems, 0)
    tile.clear()
    drain(copies)

    def halve(d, carry):
        for y0 in range(0, tile.ny, CHUNK):
            where = pl.ds(y0, CHUNK)
            tile.perm[4 + d, where, :] = 0.5 * jnp.exp(raw[place(d, 4), where, :])
        return carry

    lax.fori_loop(0, 4, halve, 0)
    first = len(pairs)
    perm_copy = issue([(tile.perm, perm_out)], sems, first)
    first = fill(tile, last, sems, first + 1)
    advance(tile, keep, send, sems, first, True)
    drain(perm_copy)


def fill(tile, last, sems, first):
    tile.props(0, 2, 5)
    tile.props(1, 0, 2)
    tile.props(1, 5, 7)
    tile.saturate(0, 3, 4)
    tile.pressure(0, 2, 5)
    copies = issue(last, sems, first)
    drain(copies)
    tile.props(0, 0, 0)
    tile.props(0, 7, 7)
    tile.saturate(1, 1, 6)
    tile.pressure(1, 0, 7)
    return first + len(copies)


def load_both(tile, kept, got, perm, q, sems):
    pairs = [(perm, tile.perm), (q, tile.q)]
    pairs += take_side(tile, None, lambda n: kept.at[n], lambda n: kept.at[n], 4, -1)
    pairs += take_side(tile, None, lambda n: got.at[n], lambda n: got.at[n], 6, 1)
    last = take_last(tile, lambda n: kept.at[n], 4, -1)
    last += take_last(tile, lambda n: got.at[n], 6, 1)
    copies = issue(pairs, sems, 0)
    tile.clear()
    drain(copies)
    return fill(tile, last, sems, len(pairs))


def third_kernel(flags, kept, got, perm, q, keep, send, *refs):
    tile = Tile(*refs[:10], kept.shape[1], jnp.int32(0))
    first = load_both(tile, kept, got, perm, q, refs[10])
    advance(tile, keep, send, refs[10], first, True)


def last_kernel(flags, index, weight, kept, got, perm, q, values, *refs):
    tile = Tile(*refs[:10], kept.shape[1], flags[1])
    sems, picked = refs[10], refs[11]
    load_both(tile, kept, got, perm, q, sems)
    odd, offset = flags[0], flags[2]
    lanes = kept.shape[2]
    lane = lax.broadcasted_iota(jnp.int32, (1, lanes), 1)
    picked[...] = jnp.zeros_like(picked)
    count = index.shape[0] // 8

    def one(n, carry):
        slot = n & 7
        row = jnp.where(odd == 1, slot, 7 - slot)
        st = row + 1 + (row >= 4).astype(jnp.int32)
        total = jnp.zeros((1, lanes), jnp.float32)
        for t in range(8):
            cell = index[n * 8 + t]
            y = lax.shift_right_logical(cell, 7) & (tile.ny - 1)
            values_row = tile.p[0][st, pl.ds(PAD + y, 1), :]
            total = total + jnp.where(lane == (cell & (lanes - 1)), values_row, 0.0) * weight[n * 8 + t]
        picked[pl.ds(offset + n, 1), :] = total
        return carry

    lax.fori_loop(0, count, one, 0)
    ones = jnp.ones((values.shape[0], lanes), jnp.float32)
    values[...] = lax.dot_general(
        ones, picked[...], (((1,), (1,)), ((), ())), precision=HIGH, preferred_element_type=jnp.float32
    )


def source_kernel(flags, wells, rate, whole, edge):
    ny, nz = whole.shape[1], whole.shape[2]
    odd, chip = flags[0], flags[3]
    lane = lax.broadcasted_iota(jnp.int32, (1, nz), 1)
    whole[...] = jnp.zeros_like(whole)
    edge[...] = jnp.zeros_like(edge)
    total = flags[4]

    def one(n, carry):
        cell = wells[n]
        x = lax.shift_right_logical(cell, 14)
        y = lax.shift_right_logical(cell, 7) & (ny - 1)
        add = jnp.where(lane == (cell & (nz - 1)), rate[n], 0.0)
        behind = jnp.where(odd == 1, chip * 8 + 11 - x, x - chip * 8 + 4) & (total - 1)
        inside = behind - 4

        @pl.when((inside >= 0) & (inside < 8))
        def _():
            where = (inside, pl.ds(y, 1), slice(None))
            whole[where] = whole[where] + add

        @pl.when(behind < 8)
        def _():
            where = (7 - behind, pl.ds(y, 1), slice(None))
            edge[where] = edge[where] + add

        return carry

    lax.fori_loop(0, wells.shape[0], one, 0)


def solve_kernel(values, obs, var, noise, columns, out, coef):
    groups = obs.shape[0]
    ens = noise.shape[1]
    half = ens // 2
    spaces = groups * 8
    parts = []
    for g in range(groups):
        sides = []
        for core in range(2):
            total = None
            for near in range(4):
                chip = (4 * g + near - core) % (4 * groups)
                row = values[pl.ds(2 * chip + core, half, stride=spaces), :]
                total = row if total is None else total + row
            sides.append(total)
        parts.append(jnp.concatenate(sides, axis=0))
    small = jnp.zeros((ens, ens), jnp.float32)
    right = jnp.zeros((ens, ens), jnp.float32)
    dims = (((1,), (1,)), ((), ()))
    for g in range(groups):
        predicted = parts[g]
        dev = predicted - jnp.mean(predicted, axis=0, keepdims=True)
        spread = INFLATION * var[pl.ds(g, 1), :]
        resid = obs[pl.ds(g, 1), :] + jnp.sqrt(spread) * noise[g] - predicted
        scaled = dev / spread
        small = small + lax.dot_general(
            scaled, dev, dims, precision=HIGH, preferred_element_type=jnp.float32
        )
        right = right + lax.dot_general(
            scaled, resid, dims, precision=HIGH, preferred_element_type=jnp.float32
        )
    row = lax.broadcasted_iota(jnp.int32, (ens, ens), 0)
    col = lax.broadcasted_iota(jnp.int32, (ens, ens), 1)
    left = small + jnp.where(row == col, ens - 1.0, 0.0)
    for k in range(ens):
        pivot = left[k : k + 1, k : k + 1]
        left_row = left[k : k + 1, :] / pivot
        right_row = right[k : k + 1, :] / pivot
        factor = left[:, k : k + 1]
        here = row == k
        left = jnp.where(here, left_row, left - factor * left_row)
        right = jnp.where(here, right_row, right - factor * right_row)
    mixing = right - jnp.mean(right, axis=0, keepdims=True) + jnp.where(row == col, 1.0, 0.0)
    rows, wide = columns.shape[2], columns.shape[3]

    def natural(place):
        return 2 * place if place < half else 2 * (place - half) + 1

    for j in range(ens):
        for m in range(ens):
            at = natural(j) * ens + natural(m)
            coef[at] = jnp.broadcast_to(mixing[j : j + 1, m : m + 1], (8, wide))

    def one(n, carry):
        part = [columns[j, n] for j in range(ens)]
        for m in range(ens):
            for r0 in range(0, rows, 8):
                total = coef[m] * part[0][r0 : r0 + 8]
                for j in range(1, ens):
                    total = total + coef[j * ens + m] * part[j][r0 : r0 + 8]
                out[m, n, r0 : r0 + 8, :] = total
        return carry

    lax.fori_loop(0, columns.shape[1], one, 0)


def body(
    log_perm,
    saturation,
    pressure_init,
    wells,
    well_rate,
    obs_index,
    obs_weight,
    obs_value,
    obs_var,
    noise,
):
    width, ny, nz = log_perm.shape[1:]
    spaces = lax.axis_size("space")
    mems = lax.axis_size("mem")
    place = lax.axis_index("space")
    odd = place % 2
    chip = place // 2
    chips = spaces // 2
    rows = spaces * width
    around = (chip + odd) % chips
    cut = jnp.where(odd == 1, chip == chips - 1, chip == 0).astype(jnp.int32)
    per = obs_index.shape[0] // rows
    slots = 8 * per
    flags = jnp.stack([odd, cut, (around % 4) * slots, chip, jnp.int32(rows)]).astype(jnp.int32)

    def take(field, start, size):
        return lax.dynamic_slice_in_dim(field, start, size, axis=0)

    other = take(log_perm, 1 - odd, 1)[0]
    mine = take(log_perm, odd, 1)[0]
    swap_out = jnp.concatenate([other, saturation, pressure_init])
    edge_out = jnp.concatenate([other, take(saturation, odd * 2, 2), take(pressure_init, odd, 3)])
    swapped = lax.ppermute(swap_out, "space", [(i, i ^ 1) for i in range(spaces)])
    edge_in = lax.ppermute(
        edge_out,
        "space",
        [(i, (i + 1) % spaces if i % 2 else (i - 1) % spaces) for i in range(spaces)],
    )
    plane = functools.partial(jax.ShapeDtypeStruct, dtype=jnp.float32)
    grid = (ny, nz)
    sems = pltpu.SemaphoreType.DMA((96,))
    q_tile, q_edge = pl.pallas_call(
        source_kernel,
        out_shape=(plane((8,) + grid), plane((8,) + grid)),
        in_specs=[SMEM, SMEM, SMEM],
        out_specs=(VMEM, VMEM),
        name="sources",
    )(flags, wells, well_rate)
    keep, send, perm_tile = pl.pallas_call(
        first_kernel,
        out_shape=(plane((PLANES,) + grid), plane((8,) + grid), plane((8,) + grid)),
        in_specs=[SMEM] + [ANY] * 5,
        out_specs=(ANY,) * 3,
        scratch_shapes=tile_scratch(ny, nz) + [pltpu.VMEM((8,) + grid, jnp.float32), sems],
        name="first",
    )(flags, mine, saturation, pressure_init, swapped, q_tile)
    onward = [(i, (i + (-2 if i % 2 else 2)) % spaces) for i in range(spaces)]
    back = [(b, a) for a, b in onward]
    got = lax.ppermute(send, "space", onward)
    keep, send, perm_edge = pl.pallas_call(
        second_kernel,
        out_shape=(plane((PLANES,) + grid), plane((PLANES,) + grid), plane((8,) + grid)),
        in_specs=[SMEM] + [ANY] * 5,
        out_specs=(ANY,) * 3,
        scratch_shapes=tile_scratch(ny, nz) + [pltpu.VMEM((4,) + grid, jnp.float32), sems],
        name="second",
    )(flags, keep, edge_in, got, perm_tile, q_edge)
    got = lax.ppermute(send, "space", back)
    keep, send = pl.pallas_call(
        third_kernel,
        out_shape=(plane((PLANES,) + grid), plane((PLANES,) + grid)),
        in_specs=[SMEM] + [ANY] * 4,
        out_specs=(ANY,) * 2,
        scratch_shapes=tile_scratch(ny, nz) + [sems],
        name="third",
    )(flags, keep, got, perm_tile, q_tile)
    got = lax.ppermute(send, "space", onward)

    def local(table):
        table = jnp.roll(table.reshape(per, rows, -1), 4, axis=1)
        return lax.dynamic_slice_in_dim(table, around * 8, 8, axis=1).reshape(-1)

    devices = mems * spaces
    values = pl.pallas_call(
        last_kernel,
        out_shape=plane((devices, nz)),
        in_specs=[SMEM] * 3 + [ANY] * 4,
        out_specs=VMEM,
        scratch_shapes=tile_scratch(ny, nz) + [sems, pltpu.VMEM((nz, nz), jnp.float32)],
        name="last",
    )(flags, local(obs_index), local(obs_weight), keep, got, perm_edge, q_edge)
    values = lax.all_to_all(
        values.reshape(devices, 1, nz), ("mem", "space"), 0, 0, tiled=True
    ).reshape(devices, nz)

    def ordered(table):
        table = jnp.roll(table.reshape(-1, per, rows), 4, axis=2)
        table = table.reshape(-1, per, chips // 4, 4, 8).transpose(2, 0, 3, 1, 4)
        return table.reshape(chips // 4, -1, 4 * slots)

    columns = lax.all_to_all(log_perm, "mem", split_axis=2, concat_axis=0, tiled=True)
    mixed_noise = ordered(jnp.concatenate([noise[0::2], noise[1::2]]))
    return pl.pallas_call(
        solve_kernel,
        out_shape=plane(columns.shape),
        in_specs=[VMEM] * 5,
        out_specs=VMEM,
        scratch_shapes=[pltpu.VMEM((noise.shape[0] ** 2, 8, nz), jnp.float32)],
        name="solve",
    )(values, ordered(obs_value)[:, 0], ordered(obs_var)[:, 0], mixed_noise, columns)


def solution(mesh):
    placed = (
        P("mem", "space", None, None),
        P("space", None, None),
        P("space", None, None),
        P(),
        P(),
        P(),
        P(),
        P(),
        P(),
        P(),
    )
    return jax.shard_map(
        body, mesh=mesh, in_specs=placed, out_specs=P(None, "space", "mem", None), check_vma=False
    )
```

```python
import jax
import jax.numpy as jnp
from jax import lax
from jax.experimental import pallas as pl
from jax.experimental.pallas import tpu as pltpu
from jax.sharding import PartitionSpec as P


INFLATION = 4.0
STEP = 0.1
PAD = 8
CHUNK = 32
HIGH = lax.Precision.HIGHEST
FAR = pl.BlockSpec(memory_space=pltpu.HBM)
SMEM = pl.BlockSpec(memory_space=pltpu.SMEM)
VMEM = pl.BlockSpec(memory_space=pltpu.VMEM)

S0, P0, S1, P1, S2, L2 = (0, 1), (2, 3, 4), (5, 6, 7), (8, 9, 10), 11, 12
PLANES = 13
TABLES = 5
PARAMS = pltpu.CompilerParams(vmem_limit_bytes=12 << 20)


def spot(row):
    return row + 1 + (row >= 4)


class Tile:
    def __init__(self, lam_a, lam_b, frac_a, frac_b, p_a, p_b, s_a, s_b, perm, q, q_row, cut):
        self.lam = (lam_a, lam_b)
        self.frac = (frac_a, frac_b)
        self.p = (p_a, p_b)
        self.s = (s_a, s_b)
        self.perm = perm
        self.q = q
        self.q_row = q_row
        self.ny = perm.shape[1]
        self.cut = cut

    def clear(self):
        for ref in self.lam + self.frac + self.p:
            tall, wide = ref.shape[1:]
            edge = jnp.zeros((PAD, wide), jnp.float32)
            for r in range(ref.shape[0]):
                ref[r, 0:PAD, :] = edge
                ref[r, tall - PAD : tall, :] = edge
            ref[5, :, :] = jnp.zeros((tall, wide), jnp.float32)

    def rows(self, first, last, fn):
        def one(row, carry):
            far = row >= 4
            st = row + 1 + far.astype(jnp.int32)
            joined = 1 - self.cut
            up = st + 1 + jnp.where(row == 3, joined, 0)
            down = st - 1 - jnp.where(row == 4, joined, 0)
            for y0 in range(0, self.ny, CHUNK):
                fn(row, st, up, down, y0)
            return carry

        lax.fori_loop(first, last + 1, one, 0)

    def props(self, level, first, last):
        def fn(row, st, up, down, y0):
            inner = pl.ds(y0, CHUNK)
            sat = self.s[level][st, inner, :]
            lam, frac = props(self.perm[row, inner, :], sat)
            self.lam[level][st, pl.ds(PAD + y0, CHUNK), :] = lam
            self.frac[level][st, pl.ds(PAD + y0, CHUNK), :] = frac

        self.rows(first, last, fn)

    def saturate(self, level, first, last):
        lam_r, frac_r, p_r = self.lam[level], self.frac[level], self.p[level]
        new = 1 - level
        lanes = lam_r.shape[2]
        lane = lax.broadcasted_iota(jnp.int32, (CHUNK, lanes), 1)
        is_first, is_last = lane == 0, lane == lanes - 1

        def fn(row, st, up, down, y0):
            inner = pl.ds(PAD + y0, CHUNK)
            lam, frac, press = lam_r[st, inner, :], frac_r[st, inner, :], p_r[st, inner, :]

            def face(index, where):
                flux = (lam + lam_r[index, where, :]) * (press - p_r[index, where, :])
                return flux * jnp.where(flux > 0.0, frac, frac_r[index, where, :])

            out = face(up, inner) + face(down, inner)
            out = out + face(st, pl.ds(PAD + y0 + 1, CHUNK))
            out = out + face(st, pl.ds(PAD + y0 - 1, CHUNK))
            flux = (lam + pltpu.roll(lam, lanes - 1, 1)) * (press - pltpu.roll(press, lanes - 1, 1))
            moved = flux * jnp.where(flux > 0.0, frac, pltpu.roll(frac, lanes - 1, 1))
            edge = jnp.maximum(lam * press, 0.0) * frac
            out = out + jnp.where(is_last, edge, moved)
            out = out + jnp.where(is_first, edge, pltpu.roll(-moved, 1, 1))
            q = self.q[self.q_row(row), pl.ds(y0, CHUNK), :]
            water = q * jnp.where(q > 0.0, 1.0, frac)
            sat = self.s[level][st, pl.ds(y0, CHUNK), :]
            sat = jnp.clip(sat + STEP * (water - out), 0.0, 1.0)
            self.s[new][st, pl.ds(y0, CHUNK), :] = sat
            lam, frac = props(self.perm[row, pl.ds(y0, CHUNK), :], sat)
            self.lam[new][st, inner, :] = lam
            self.frac[new][st, inner, :] = frac

        self.rows(first, last, fn)

    def pressure(self, level, first, last):
        new = 1 - level
        lam_r, p_r, out_r = self.lam[new], self.p[level], self.p[new]
        lanes = lam_r.shape[2]
        lane = lax.broadcasted_iota(jnp.int32, (CHUNK, lanes), 1)
        not_first, not_last = lane > 0, lane < lanes - 1

        def fn(row, st, up, down, y0):
            inner = pl.ds(PAD + y0, CHUNK)
            lam, press = lam_r[st, inner, :], p_r[st, inner, :]
            numer = press + self.q[self.q_row(row), pl.ds(y0, CHUNK), :]
            denom = jnp.ones_like(lam)
            for index, where in (
                (up, inner),
                (down, inner),
                (st, pl.ds(PAD + y0 + 1, CHUNK)),
                (st, pl.ds(PAD + y0 - 1, CHUNK)),
            ):
                trans = lam + lam_r[index, where, :]
                numer = numer + trans * p_r[index, where, :]
                denom = denom + trans
            for shift, mask in ((lanes - 1, not_last), (1, not_first)):
                trans = lam + jnp.where(mask, pltpu.roll(lam, shift, 1), 0.0)
                numer = numer + trans * jnp.where(mask, pltpu.roll(press, shift, 1), 0.0)
                denom = denom + trans
            out_r[st, inner, :] = numer / denom

        self.rows(first, last, fn)


def props(perm_half, sat):
    water = sat * sat
    oil = (1.0 - sat) * (1.0 - sat) * 0.25
    total = water + oil
    return perm_half * total, water / total


def near(array):
    return pltpu.with_memory_space_constraint(array, pltpu.VMEM)


def tile_scratch(ny, nz):
    tall = ny + 2 * PAD
    wide = [pltpu.VMEM((11, tall, nz), jnp.float32) for _ in range(6)]
    flat = [pltpu.VMEM((count, ny, nz), jnp.float32) for count in (11, 11, 13)]
    return wide + flat


def issue(pairs, sems, first):
    copies = []
    for n, (src, dst) in enumerate(pairs):
        copy = pltpu.make_async_copy(src, dst, sems.at[first + n])
        copy.start()
        copies.append(copy)
    return copies


def drain(copies):
    for copy in copies:
        copy.wait()


def beyond(tile, row):
    return jnp.where(tile.cut == 1, 5, spot(row))


def give_early(tile, keep, send, send_early):
    pairs = []
    inner = pl.ds(PAD, tile.ny)
    for d in range(2):
        pairs.append((tile.s[0].at[spot(d)], keep.at[S0[d]]))
    for d in range(3):
        pairs.append((tile.p[0].at[spot(d), inner], keep.at[P0[d]]))
    if send_early:
        for d in range(2):
            pairs.append((tile.s[0].at[spot(7 - d)], send.at[S0[d]]))
        for d in range(3):
            pairs.append((tile.p[0].at[spot(7 - d), inner], send.at[P0[d]]))
    return pairs


def give_late(tile, out, near, base):
    row, step = near
    inner = pl.ds(PAD, tile.ny)
    pairs = []
    for n, d in enumerate((1, 2, 3)):
        pairs.append((tile.s[1].at[spot(row + step * d)], out.at[S1[n] - base]))
    for n, d in enumerate((2, 3, 4)):
        st = beyond(tile, row + step * d) if d == 4 else spot(row + step * d)
        pairs.append((tile.p[1].at[st, inner], out.at[P1[n] - base]))
    return pairs


def give_last(tile, out, near, base):
    row, step = near
    inner = pl.ds(PAD, tile.ny)
    return [
        (tile.s[0].at[spot(row + step * 3)], out.at[S2 - base]),
        (tile.lam[0].at[beyond(tile, row + step * 4), inner], out.at[L2 - base]),
    ]


def take(tile, early, late, base_row, step):
    inner = pl.ds(PAD, tile.ny)
    start, s_next, p_next, last = [], [], [], []
    for d in range(2):
        start.append((early(S0[d]), tile.s[0].at[base_row + step * d]))
    for d in range(3):
        start.append((early(P0[d]), tile.p[0].at[base_row + step * d, inner]))
    for n, d in enumerate((1, 2, 3)):
        s_next.append((late(S1[n]), tile.s[1].at[base_row + step * d]))
    for n, d in enumerate((2, 3, 4)):
        p_next.append((late(P1[n]), tile.p[1].at[base_row + step * d, inner]))
    last.append((late(S2), tile.s[0].at[base_row + step * 3]))
    last.append((late(L2), tile.lam[0].at[base_row + step * 4, inner]))
    return start, s_next, p_next, last


def advance(tile, keep, send, sems, first, send_early):
    base = 0 if send_early else S1[0]
    early = issue(give_early(tile, keep, send, send_early), sems, first)
    first += len(early)
    tile.saturate(0, 1, 6)
    tile.pressure(0, 2, 5)
    late = issue(
        give_late(tile, send, (7, -1), base) + give_late(tile, keep, (0, 1), 0), sems, first
    )
    first += len(late)
    drain(early)
    tile.saturate(1, 3, 4)
    last = issue(
        give_last(tile, send, (7, -1), base) + give_last(tile, keep, (0, 1), 0), sems, first
    )
    drain(late)
    drain(last)


def first_kernel(flags, log_perm, own_sat, own_press, swapped, q, keep, send, perm, *refs):
    tile = Tile(*refs[:8], perm, refs[8], lambda row: row + 4, jnp.int32(0))
    raw, sems = refs[9], refs[10]
    odd = flags[0]
    inner = pl.ds(PAD, tile.ny)

    def place(n):
        return jnp.where(odd == 1, 3 - n, n)

    pairs = [(q, tile.q), (log_perm.at[odd], raw)]
    for n in range(4):
        pairs.append((own_sat.at[place(n)], tile.s[0].at[spot(n)]))
        pairs.append((own_press.at[place(n)], tile.p[0].at[spot(n), inner]))
        pairs.append((swapped.at[4 + place(n)], tile.s[0].at[spot(4 + n)]))
        pairs.append((swapped.at[8 + place(n)], tile.p[0].at[spot(4 + n), inner]))
    copies = issue(pairs, sems, 0)
    tile.clear()

    def halve(n, carry):
        for y0 in range(0, tile.ny, CHUNK):
            where = pl.ds(y0, CHUNK)
            perm[4 + n, where, :] = 0.5 * jnp.exp(swapped[place(n), where, :])
        return carry

    lax.fori_loop(0, 4, halve, 0)
    drain(copies)

    def halve_own(n, carry):
        for y0 in range(0, tile.ny, CHUNK):
            where = pl.ds(y0, CHUNK)
            perm[n, where, :] = 0.5 * jnp.exp(raw[place(n), where, :])
        return carry

    lax.fori_loop(0, 4, halve_own, 0)
    tile.props(0, 0, 7)
    advance(tile, keep, send, sems, len(pairs), False)


def fill(tile, q, sides, sems):
    groups = [sum((side[n] for side in sides), []) for n in range(4)]
    groups[0].append((q, tile.q))
    first, copies = 0, []
    for group in groups[:3]:
        copies.append(issue(group, sems, first))
        first += len(group)
    tile.clear()
    drain(copies[0])
    tile.props(0, 2, 5)
    tile.saturate(0, 3, 4)
    drain(copies[1])
    tile.props(1, 0, 2)
    tile.props(1, 5, 7)
    tile.pressure(0, 2, 5)
    drain(copies[2])
    last = issue(groups[3], sems, first)
    drain(last)
    tile.props(0, 0, 0)
    tile.props(0, 7, 7)
    tile.saturate(1, 1, 6)
    tile.pressure(1, 0, 7)
    return first + len(last)


def edge_q(cut):
    return lambda row: jnp.where((cut == 1) & (row >= 4), row, 7 - row)


def second_kernel(flags, kept, raw_in, late_in, perm_own, q, *refs):
    keep, send, perm = refs[TABLES : TABLES + 3]
    refs = refs[TABLES + 3 :]
    tile = Tile(*refs[:8], perm, refs[8], edge_q(flags[1]), flags[1])
    sems = refs[9]
    straight = flags[0] ^ flags[1]

    def place(n, count):
        return jnp.where(straight == 1, n, count - 1 - n)

    def early(plane):
        if plane in S0:
            return raw_in.at[4 + place(plane, 2)]
        return raw_in.at[6 + place(plane - 2, 3)]

    def permeability(d, carry):
        for y0 in range(0, tile.ny, CHUNK):
            where = pl.ds(y0, CHUNK)
            perm[3 - d, where, :] = perm_own[d, where, :]
            perm[4 + d, where, :] = 0.5 * jnp.exp(raw_in[place(d, 4), where, :])
        return carry

    lax.fori_loop(0, 4, permeability, 0)
    sides = (
        take(tile, lambda n: kept.at[n], lambda n: kept.at[n], 4, -1),
        take(tile, early, lambda n: late_in.at[n - S1[0]], 6, 1),
    )
    first = fill(tile, q, sides, sems)
    advance(tile, keep, send, sems, first, True)


def both_sides(tile, kept, got):
    return (
        take(tile, lambda n: kept.at[n], lambda n: kept.at[n], 4, -1),
        take(tile, lambda n: got.at[n], lambda n: got.at[n], 6, 1),
    )


def third_kernel(flags, kept, got, perm, q, columns, keep, send, *refs):
    del columns
    tile = Tile(*refs[:8], perm, refs[8], lambda row: row + 4, jnp.int32(0))
    first = fill(tile, q, both_sides(tile, kept, got), refs[9])
    advance(tile, keep, send, refs[9], first, True)


def last_kernel(flags, index, weight, kept, got, perm, q, values, *refs):
    tile = Tile(*refs[:8], perm, refs[8], edge_q(flags[1]), flags[1])
    sems, picked = refs[9], refs[10]
    fill(tile, q, both_sides(tile, kept, got), sems)
    odd, cut, offset = flags[0], flags[1], flags[2]
    lanes = kept.shape[2]
    lane = lax.broadcasted_iota(jnp.int32, (1, lanes), 1)
    picked[...] = jnp.zeros_like(picked)
    count = index.shape[0] // 8

    def one(n, carry):
        slot = n & 7
        row = jnp.where(odd == 1, slot, 7 - slot)
        st = row + 1 + (row >= 4).astype(jnp.int32)
        other = cut * (row >= 4).astype(jnp.int32)
        at = n - slot + jnp.where(other == 1, 7 - slot, slot)
        total = jnp.zeros((1, lanes), jnp.float32)
        for t in range(8):
            cell = index[at * 8 + t]
            y = lax.shift_right_logical(cell, 7) & (tile.ny - 1)
            values_row = tile.p[0][st, pl.ds(PAD + y, 1), :]
            total = total + jnp.where(lane == (cell & (lanes - 1)), values_row, 0.0) * weight[at * 8 + t]
        picked[pl.ds(offset + at + other * count, 1), :] = total
        return carry

    lax.fori_loop(0, count, one, 0)
    ones = jnp.ones((values.shape[0], lanes), jnp.float32)
    values[...] = lax.dot_general(
        ones, picked[...], (((1,), (1,)), ((), ())), precision=HIGH, preferred_element_type=jnp.float32
    )


def source_kernel(flags, wells, rate, out, q, sem):
    ny, nz = q.shape[1], q.shape[2]
    odd, chip = flags[0], flags[3]
    last = q.shape[0] - 1
    lane = lax.broadcasted_iota(jnp.int32, (1, nz), 1)
    q[...] = jnp.zeros_like(q)
    total = flags[4]

    def one(n, carry):
        cell = wells[n]
        x = lax.shift_right_logical(cell, 14)
        y = lax.shift_right_logical(cell, 7) & (ny - 1)
        behind = jnp.where(odd == 1, chip * 8 + 11 - x, x - chip * 8 + 4) & (total - 1)
        where = (jnp.minimum(behind, last), pl.ds(y, 1), slice(None))
        q[where] = q[where] + jnp.where(lane == (cell & (nz - 1)), rate[n], 0.0)
        return carry

    lax.fori_loop(0, wells.shape[0], one, 0, unroll=4)
    copy = pltpu.make_async_copy(q, out, sem)
    copy.start()
    copy.wait()


def solve_kernel(values, obs, var, noise, columns, out, coef):
    groups = obs.shape[0]
    ens = noise.shape[1]
    half = ens // 2
    spaces = groups * 8
    parts = []
    for g in range(groups):
        sides = []
        for core in range(2):
            total = None
            for near in range(4):
                chip = (4 * g + near - core) % (4 * groups)
                row = values[pl.ds(2 * chip + core, half, stride=spaces), :]
                total = row if total is None else total + row
            sides.append(total)
        parts.append(sides)
    lanes = values.shape[1]
    count = lanes // 4
    near = lax.broadcasted_iota(jnp.int32, (half, lanes), 1) < count
    ends = [values[pl.ds(at, half, stride=spaces), :] for at in (0, spaces - 1)]
    far = [pltpu.roll(end, lanes - count, 1) for end in ends]
    for core in range(2):
        own, foreign = ends[core], far[1 - core]
        parts[0][core] = parts[0][core] - own + jnp.where(near, own + foreign, 0.0)
    parts = [jnp.concatenate(sides, axis=0) for sides in parts]
    small = jnp.zeros((ens, ens), jnp.float32)
    right = jnp.zeros((ens, ens), jnp.float32)
    dims = (((1,), (1,)), ((), ()))
    for g in range(groups):
        predicted = parts[g]
        dev = predicted - jnp.mean(predicted, axis=0, keepdims=True)
        spread = INFLATION * var[pl.ds(g, 1), :]
        resid = obs[pl.ds(g, 1), :] + jnp.sqrt(spread) * noise[g] - predicted
        scaled = dev / spread
        small = small + lax.dot_general(
            scaled, dev, dims, precision=HIGH, preferred_element_type=jnp.float32
        )
        right = right + lax.dot_general(
            scaled, resid, dims, precision=HIGH, preferred_element_type=jnp.float32
        )
    row = lax.broadcasted_iota(jnp.int32, (ens, ens), 0)
    col = lax.broadcasted_iota(jnp.int32, (ens, ens), 1)
    left = small + jnp.where(row == col, ens - 1.0, 0.0)
    for k in range(ens):
        pivot = left[k : k + 1, k : k + 1]
        left_row = left[k : k + 1, :] / pivot
        right_row = right[k : k + 1, :] / pivot
        factor = left[:, k : k + 1]
        here = row == k
        left = jnp.where(here, left_row, left - factor * left_row)
        right = jnp.where(here, right_row, right - factor * right_row)
    mixing = right - jnp.mean(right, axis=0, keepdims=True) + jnp.where(row == col, 1.0, 0.0)
    rows, wide = columns.shape[2], columns.shape[3]

    def natural(place):
        return 2 * place if place < half else 2 * (place - half) + 1

    for j in range(ens):
        for m in range(ens):
            at = natural(j) * ens + natural(m)
            coef[at] = jnp.broadcast_to(mixing[j : j + 1, m : m + 1], (8, wide))

    def one(n, carry):
        part = [columns[j, n] for j in range(ens)]
        for m in range(ens):
            for r0 in range(0, rows, 8):
                total = coef[m] * part[0][r0 : r0 + 8]
                for j in range(1, ens):
                    total = total + coef[j * ens + m] * part[j][r0 : r0 + 8]
                out[m, n, r0 : r0 + 8, :] = total
        return carry

    lax.fori_loop(0, columns.shape[1], one, 0)


def body(
    log_perm,
    saturation,
    pressure_init,
    wells,
    well_rate,
    obs_index,
    obs_weight,
    obs_value,
    obs_var,
    noise,
):
    width, ny, nz = log_perm.shape[1:]
    spaces = lax.axis_size("space")
    mems = lax.axis_size("mem")
    place = lax.axis_index("space")
    odd = place % 2
    chip = place // 2
    chips = spaces // 2
    rows = spaces * width
    around = (chip + odd) % chips
    cut = jnp.where(odd == 1, chip == chips - 1, chip == 0).astype(jnp.int32)
    per = obs_index.shape[0] // rows
    slots = 8 * per
    flags = jnp.stack([odd, cut, (around % 4) * slots, chip, jnp.int32(rows)]).astype(jnp.int32)

    def part(field, start, size):
        return lax.dynamic_slice_in_dim(field, start, size, axis=0)

    other = part(log_perm, 1 - odd, 1)[0]
    swap_out = jnp.concatenate([other, saturation, pressure_init])
    edge_out = jnp.concatenate([other, part(saturation, odd * 2, 2), part(pressure_init, odd, 3)])
    swapped = lax.ppermute(swap_out, "space", [(i, i ^ 1) for i in range(spaces)])
    ends = spaces - 1
    edge_in = lax.ppermute(
        edge_out,
        "space",
        [(0, 0), (ends, ends)] + [(i, i + 1 if i % 2 else i - 1) for i in range(1, ends)],
    )
    grid = (ny, nz)

    def plane(count):
        return pltpu.VMEM((count,) + grid, jnp.float32)

    sems = pltpu.SemaphoreType.DMA((64,))
    q = pl.pallas_call(
        source_kernel,
        out_shape=pltpu.HBM((13,) + grid, jnp.float32),
        in_specs=[SMEM, SMEM, SMEM],
        out_specs=FAR,
        scratch_shapes=[plane(13), pltpu.SemaphoreType.DMA],
        name="sources",
        compiler_params=PARAMS,
    )(flags, wells, well_rate)
    keep, send, perm_tile = pl.pallas_call(
        first_kernel,
        out_shape=(plane(PLANES), plane(8), plane(8)),
        in_specs=[SMEM] + [FAR] * 3 + [VMEM, FAR],
        out_specs=(VMEM,) * 3,
        scratch_shapes=tile_scratch(ny, nz) + [plane(4), sems],
        name="first",
        compiler_params=PARAMS,
    )(flags, log_perm, saturation, pressure_init, near(swapped), q)
    onward = [(i, i + 2) for i in range(0, ends - 1, 2)] + [(ends - 1, ends)]
    onward += [(i, i - 2) for i in range(3, spaces, 2)] + [(1, 0)]
    back = [(b, a) for a, b in onward]
    got = lax.ppermute(send, "space", onward)

    def local(table):
        table = jnp.roll(table.reshape(per, rows, -1), 4, axis=1)
        return lax.dynamic_slice_in_dim(table, around * 8, 8, axis=1).reshape(-1)

    def ordered(table):
        table = jnp.roll(table.reshape(-1, per, rows), 4, axis=2)
        table = table.reshape(-1, per, chips // 4, 4, 8).transpose(2, 0, 3, 1, 4)
        return table.reshape(chips // 4, -1, 4 * slots)

    index, weight = local(obs_index), local(obs_weight)
    value, var = ordered(obs_value)[:, 0], ordered(obs_var)[:, 0]
    mixed_noise = ordered(jnp.concatenate([noise[0::2], noise[1::2]]))
    tables = (index, weight, value, var, mixed_noise)
    keep, send, perm_edge = pl.pallas_call(
        second_kernel,
        out_shape=(plane(PLANES), plane(PLANES), plane(8)),
        in_specs=[SMEM] + [VMEM] * 4 + [FAR] * (TABLES + 1),
        out_specs=(VMEM,) * 3,
        scratch_shapes=tile_scratch(ny, nz) + [sems],
        name="second",
        compiler_params=PARAMS,
    )(flags, near(keep), near(edge_in), near(got), near(perm_tile), q, *tables)
    got = lax.ppermute(send, "space", back)
    columns = lax.all_to_all(log_perm, "mem", split_axis=2, concat_axis=0, tiled=True)
    keep, send = pl.pallas_call(
        third_kernel,
        out_shape=(plane(PLANES), plane(PLANES)),
        in_specs=[SMEM] + [VMEM] * 3 + [FAR] * 2,
        out_specs=(VMEM,) * 2,
        scratch_shapes=tile_scratch(ny, nz) + [sems],
        name="third",
        compiler_params=PARAMS,
    )(flags, near(keep), near(got), near(perm_tile), q, columns)
    got = lax.ppermute(send, "space", onward)
    devices = mems * spaces
    values = pl.pallas_call(
        last_kernel,
        out_shape=pltpu.VMEM((devices, nz), jnp.float32),
        in_specs=[SMEM] * 3 + [VMEM] * 3 + [FAR],
        out_specs=VMEM,
        scratch_shapes=tile_scratch(ny, nz) + [sems, pltpu.VMEM((nz, nz), jnp.float32)],
        name="last",
        compiler_params=PARAMS,
    )(flags, index, weight, near(keep), near(got), near(perm_edge), q)
    values = lax.all_to_all(
        values.reshape(devices, 1, nz), ("mem", "space"), 0, 0, tiled=True
    ).reshape(devices, nz)
    return pl.pallas_call(
        solve_kernel,
        out_shape=jax.ShapeDtypeStruct(columns.shape, jnp.float32),
        in_specs=[VMEM] * 5,
        out_specs=VMEM,
        scratch_shapes=[pltpu.VMEM((noise.shape[0] ** 2, 8, nz), jnp.float32)],
        name="solve",
        compiler_params=PARAMS,
    )(near(values), value, var, mixed_noise, columns)


def solution(mesh):
    placed = (
        P("mem", "space", None, None),
        P("space", None, None),
        P("space", None, None),
        P(),
        P(),
        P(),
        P(),
        P(),
        P(),
        P(),
    )
    return jax.shard_map(
        body, mesh=mesh, in_specs=placed, out_specs=P(None, "space", "mem", None), check_vma=False
    )
```

```python
import functools

import jax
import jax.numpy as jnp
from jax import lax
from jax.experimental import pallas as pl
from jax.experimental.pallas import tpu as pltpu
from jax.sharding import PartitionSpec as P


INFLATION = 4.0
STEP = 0.1
PAD = 8
CHUNK = 32
HIGH = lax.Precision.HIGHEST
FAR = pl.BlockSpec(memory_space=pltpu.HBM)
SMEM = pl.BlockSpec(memory_space=pltpu.SMEM)
VMEM = pl.BlockSpec(memory_space=pltpu.VMEM)

S0, P0, S1, P1, S2, L2 = (0, 1), (2, 3, 4), (5, 6, 7), (8, 9, 10), 11, 12
PLANES = 13
GRANT = 56 << 20


def spot(row):
    return row + 1 + (row >= 4)


class Tile:
    def __init__(self, lam_a, lam_b, frac_a, frac_b, p_a, p_b, s_a, s_b, perm, q, q_row, cut):
        self.lam = (lam_a, lam_b)
        self.frac = (frac_a, frac_b)
        self.p = (p_a, p_b)
        self.s = (s_a, s_b)
        self.perm = perm
        self.q = q
        self.q_row = q_row
        self.ny = perm.shape[1]
        self.cut = cut

    def clear(self):
        for ref in self.lam + self.frac + self.p:
            tall, wide = ref.shape[1:]
            edge = jnp.zeros((PAD, wide), jnp.float32)
            for r in range(ref.shape[0]):
                ref[r, 0:PAD, :] = edge
                ref[r, tall - PAD : tall, :] = edge
            ref[5, :, :] = jnp.zeros((tall, wide), jnp.float32)

    def rows(self, first, last, fn):
        def one(row, carry):
            far = row >= 4
            st = row + 1 + far.astype(jnp.int32)
            joined = 1 - self.cut
            up = st + 1 + jnp.where(row == 3, joined, 0)
            down = st - 1 - jnp.where(row == 4, joined, 0)
            for y0 in range(0, self.ny, CHUNK):
                fn(row, st, up, down, y0)
            return carry

        lax.fori_loop(first, last + 1, one, 0)

    def props(self, level, first, last):
        def fn(row, st, up, down, y0):
            inner = pl.ds(y0, CHUNK)
            sat = self.s[level][st, inner, :]
            lam, frac = props(self.perm[row, inner, :], sat)
            self.lam[level][st, pl.ds(PAD + y0, CHUNK), :] = lam
            self.frac[level][st, pl.ds(PAD + y0, CHUNK), :] = frac

        self.rows(first, last, fn)

    def saturate(self, level, first, last):
        lam_r, frac_r, p_r = self.lam[level], self.frac[level], self.p[level]
        new = 1 - level
        lanes = lam_r.shape[2]
        lane = lax.broadcasted_iota(jnp.int32, (CHUNK, lanes), 1)
        is_first, is_last = lane == 0, lane == lanes - 1

        def fn(row, st, up, down, y0):
            inner = pl.ds(PAD + y0, CHUNK)
            lam, frac, press = lam_r[st, inner, :], frac_r[st, inner, :], p_r[st, inner, :]

            def face(index, where):
                flux = (lam + lam_r[index, where, :]) * (press - p_r[index, where, :])
                return flux * jnp.where(flux > 0.0, frac, frac_r[index, where, :])

            out = face(up, inner) + face(down, inner)
            out = out + face(st, pl.ds(PAD + y0 + 1, CHUNK))
            out = out + face(st, pl.ds(PAD + y0 - 1, CHUNK))
            flux = (lam + pltpu.roll(lam, lanes - 1, 1)) * (press - pltpu.roll(press, lanes - 1, 1))
            moved = flux * jnp.where(flux > 0.0, frac, pltpu.roll(frac, lanes - 1, 1))
            edge = jnp.maximum(lam * press, 0.0) * frac
            out = out + jnp.where(is_last, edge, moved)
            out = out + jnp.where(is_first, edge, pltpu.roll(-moved, 1, 1))
            q = self.q[self.q_row(row), pl.ds(y0, CHUNK), :]
            water = q * jnp.where(q > 0.0, 1.0, frac)
            sat = self.s[level][st, pl.ds(y0, CHUNK), :]
            sat = jnp.clip(sat + STEP * (water - out), 0.0, 1.0)
            self.s[new][st, pl.ds(y0, CHUNK), :] = sat
            lam, frac = props(self.perm[row, pl.ds(y0, CHUNK), :], sat)
            self.lam[new][st, inner, :] = lam
            self.frac[new][st, inner, :] = frac

        self.rows(first, last, fn)

    def pressure(self, level, first, last):
        new = 1 - level
        lam_r, p_r, out_r = self.lam[new], self.p[level], self.p[new]
        lanes = lam_r.shape[2]
        lane = lax.broadcasted_iota(jnp.int32, (CHUNK, lanes), 1)
        not_first, not_last = lane > 0, lane < lanes - 1

        def fn(row, st, up, down, y0):
            inner = pl.ds(PAD + y0, CHUNK)
            lam, press = lam_r[st, inner, :], p_r[st, inner, :]
            numer = press + self.q[self.q_row(row), pl.ds(y0, CHUNK), :]
            denom = jnp.ones_like(lam)
            for index, where in (
                (up, inner),
                (down, inner),
                (st, pl.ds(PAD + y0 + 1, CHUNK)),
                (st, pl.ds(PAD + y0 - 1, CHUNK)),
            ):
                trans = lam + lam_r[index, where, :]
                numer = numer + trans * p_r[index, where, :]
                denom = denom + trans
            for shift, mask in ((lanes - 1, not_last), (1, not_first)):
                trans = lam + jnp.where(mask, pltpu.roll(lam, shift, 1), 0.0)
                numer = numer + trans * jnp.where(mask, pltpu.roll(press, shift, 1), 0.0)
                denom = denom + trans
            out_r[st, inner, :] = numer / denom

        self.rows(first, last, fn)


def props(perm_half, sat):
    water = sat * sat
    oil = (1.0 - sat) * (1.0 - sat) * 0.25
    total = water + oil
    return perm_half * total, water / total


def near(array):
    return pltpu.with_memory_space_constraint(array, pltpu.VMEM)


def tile_scratch(ny, nz):
    tall = ny + 2 * PAD
    wide = [pltpu.VMEM((11, tall, nz), jnp.float32) for _ in range(6)]
    flat = [pltpu.VMEM((count, ny, nz), jnp.float32) for count in (11, 11, 12)]
    return wide + flat


def issue(pairs, sems, first):
    copies = []
    for n, (src, dst) in enumerate(pairs):
        copy = pltpu.make_async_copy(src, dst, sems.at[first + n])
        copy.start()
        copies.append(copy)
    return copies


def drain(copies):
    for copy in copies:
        copy.wait()


def move(pairs):
    tall = min(src.shape[0] for src, _ in pairs)

    def one(n, carry):
        where = pl.ds(pl.multiple_of(n * CHUNK, CHUNK), CHUNK)
        for src, dst in pairs:
            dst[where, :] = src[where, :]
        return carry

    lax.fori_loop(0, tall // CHUNK, one, 0)


def position(chips):
    place = lax.axis_index("space")
    odd, chip = place & 1, lax.shift_right_logical(place, 1)
    end = jnp.where(odd == 1, chips - 1, 0)
    return odd, chip, (chip == end).astype(jnp.int32)


def beyond(tile, row):
    return jnp.where(tile.cut == 1, 5, spot(row))


def give_early(tile, keep, send, send_early):
    pairs = []
    inner = pl.ds(PAD, tile.ny)
    sides = [(keep, lambda d: d)] + ([(send, lambda d: 7 - d)] if send_early else [])
    for out, row in sides:
        for d in range(2):
            pairs.append((tile.s[0].at[spot(row(d))], out.at[S0[d]]))
        for d in range(3):
            pairs.append((tile.p[0].at[spot(row(d)), inner], out.at[P0[d]]))
    return pairs


def give_late(tile, out, near, base):
    row, step = near
    inner = pl.ds(PAD, tile.ny)
    pairs = []
    for n, d in enumerate((1, 2, 3)):
        pairs.append((tile.s[1].at[spot(row + step * d)], out.at[S1[n] - base]))
    for n, d in enumerate((2, 3, 4)):
        st = beyond(tile, row + step * d) if d == 4 else spot(row + step * d)
        pairs.append((tile.p[1].at[st, inner], out.at[P1[n] - base]))
    return pairs


def give_last(tile, out, near, base):
    row, step = near
    inner = pl.ds(PAD, tile.ny)
    return [
        (tile.s[0].at[spot(row + step * 3)], out.at[S2 - base]),
        (tile.lam[0].at[beyond(tile, row + step * 4), inner], out.at[L2 - base]),
    ]


def take(tile, early, late, base_row, step):
    inner = pl.ds(PAD, tile.ny)
    start, s_next, p_next, last = [], [], [], []
    for d in range(2):
        start.append((early(S0[d]), tile.s[0].at[base_row + step * d]))
    for d in range(3):
        start.append((early(P0[d]), tile.p[0].at[base_row + step * d, inner]))
    for n, d in enumerate((1, 2, 3)):
        s_next.append((late(S1[n]), tile.s[1].at[base_row + step * d]))
    for n, d in enumerate((2, 3, 4)):
        p_next.append((late(P1[n]), tile.p[1].at[base_row + step * d, inner]))
    last.append((late(S2), tile.s[0].at[base_row + step * 3]))
    last.append((late(L2), tile.lam[0].at[base_row + step * 4, inner]))
    return start, s_next, p_next, last


def advance(tile, keep, send, send_early):
    base = 0 if send_early else S1[0]
    move(give_early(tile, keep, send, send_early))
    tile.saturate(0, 1, 6)
    tile.pressure(0, 2, 5)
    tile.saturate(1, 3, 4)
    pairs = []
    for out, near_row, at in ((send, (7, -1), base), (keep, (0, 1), 0)):
        pairs += give_late(tile, out, near_row, at) + give_last(tile, out, near_row, at)
    move(pairs)


def first_kernel(chips, log_perm, own_sat, own_press, q, swapped, keep, send, perm_out, *refs):
    odd, _, _ = position(chips)
    perm, raw, sems = refs[9:]
    tile = Tile(*refs[:8], perm, refs[8], lambda row: row + 4, jnp.int32(0))
    inner = pl.ds(PAD, tile.ny)

    def place(n):
        return jnp.where(odd == 1, 3 - n, n)

    pairs = [(log_perm.at[odd], raw)]
    for n in range(4):
        pairs.append((own_sat.at[place(n)], tile.s[0].at[spot(n)]))
        pairs.append((own_press.at[place(n)], tile.p[0].at[spot(n), inner]))
    copies = issue(pairs, sems, 0)
    q_copy = issue([(q, tile.q)], sems, len(pairs))
    tile.clear()
    pairs = []
    for n in range(4):
        pairs.append((swapped.at[4 + place(n)], tile.s[0].at[spot(4 + n)]))
        pairs.append((swapped.at[8 + place(n)], tile.p[0].at[spot(4 + n), inner]))
    move(pairs)

    def halve(src, base):
        def one(n, carry):
            for y0 in range(0, tile.ny, CHUNK):
                where = pl.ds(y0, CHUNK)
                perm[base + n, where, :] = 0.5 * jnp.exp(src[place(n), where, :])
            return carry

        lax.fori_loop(0, 4, one, 0)

    halve(swapped, 4)
    drain(copies)
    halve(raw, 0)
    perm_copy = issue([(perm, perm_out)], sems, 10)
    tile.props(0, 0, 7)
    drain(q_copy)
    advance(tile, keep, send, False)
    drain(perm_copy)


def fill(tile, sides, perm_copy, q_copy):
    tile.clear()
    groups = [sum((side[n] for side in sides), []) for n in range(4)]
    move(groups[0] + groups[1] + groups[2])
    drain(perm_copy)
    tile.props(0, 2, 5)
    tile.props(1, 0, 2)
    tile.props(1, 5, 7)
    drain(q_copy)
    tile.saturate(0, 3, 4)
    tile.pressure(0, 2, 5)
    move(groups[3])
    tile.props(0, 0, 0)
    tile.props(0, 7, 7)
    tile.saturate(1, 1, 6)
    tile.pressure(1, 0, 7)


def edge_q(cut):
    return lambda row: jnp.where((cut == 1) & (row >= 4), row, 7 - row)


def second_kernel(chips, perm_own, raw_in, q, kept, late_in, keep, send, perm_out, *refs):
    odd, _, end = position(chips)
    perm, raw, sems = refs[9:]
    tile = Tile(*refs[:8], perm, refs[8], edge_q(end), end)
    straight = odd ^ end

    def place(n, count):
        return jnp.where(straight == 1, n, count - 1 - n)

    def early(plane):
        if plane in S0:
            return raw.at[4 + place(plane, 2)]
        return raw.at[6 + place(plane - 2, 3)]

    copies = issue([(raw_in, raw)] + [(perm_own.at[3 - d], perm.at[d]) for d in range(4)], sems, 0)
    q_copy = issue([(q, tile.q)], sems, 5)
    drain(copies)

    def permeability(d, carry):
        for y0 in range(0, tile.ny, CHUNK):
            where = pl.ds(y0, CHUNK)
            perm[4 + d, where, :] = 0.5 * jnp.exp(raw[place(d, 4), where, :])
        return carry

    lax.fori_loop(0, 4, permeability, 0)
    perm_copy = issue([(perm, perm_out)], sems, 6)
    sides = (
        take(tile, lambda n: kept.at[n], lambda n: kept.at[n], 4, -1),
        take(tile, early, lambda n: late_in.at[n - S1[0]], 6, 1),
    )
    fill(tile, sides, [], q_copy)
    advance(tile, keep, send, True)
    drain(perm_copy)


def both_sides(tile, kept, got):
    return (
        take(tile, lambda n: kept.at[n], lambda n: kept.at[n], 4, -1),
        take(tile, lambda n: got.at[n], lambda n: got.at[n], 6, 1),
    )


def third_kernel(perm, q, columns, kept, got, keep, send, *refs):
    del columns
    tile = Tile(*refs[:8], refs[9], refs[8], lambda row: row + 4, jnp.int32(0))
    sems = refs[10]
    perm_copy = issue([(perm, tile.perm)], sems, 0)
    q_copy = issue([(q, tile.q)], sems, 1)
    fill(tile, both_sides(tile, kept, got), perm_copy, q_copy)
    advance(tile, keep, send, True)


def last_kernel(chips, perm, q, index_in, weight_in, kept, got, values, *refs):
    odd, chip, end = position(chips)
    tile = Tile(*refs[:8], refs[9], refs[8], edge_q(end), end)
    index, weight, picked, sems = refs[10:]
    perm_copy = issue([(perm, tile.perm)], sems, 0)
    q_copy = issue([(q, tile.q)], sems, 1)
    tables = issue([(index_in, index), (weight_in, weight)], sems, 2)
    fill(tile, both_sides(tile, kept, got), perm_copy, q_copy)
    drain(tables)
    around = (chip + odd) & (chips - 1)
    total_rows = 8 * chips
    per = index.shape[1] // total_rows
    lanes = kept.shape[2]
    lane = lax.broadcasted_iota(jnp.int32, (1, lanes), 1)
    picked[...] = jnp.zeros_like(picked)

    def one(n, carry):
        slot = n & 7
        row = jnp.where(odd == 1, slot, 7 - slot)
        st = row + 1 + (row >= 4).astype(jnp.int32)
        other = end * (row >= 4).astype(jnp.int32)
        slot = jnp.where(other == 1, 7 - slot, slot)
        column = lax.shift_right_logical(n, 3)
        obs = column * total_rows + ((8 * around - 4 + slot) & (total_rows - 1))
        total = jnp.zeros((1, lanes), jnp.float32)
        for t in range(index.shape[0]):
            cell = index[t, obs]
            y = lax.shift_right_logical(cell, 7) & (tile.ny - 1)
            values_row = tile.p[0][st, pl.ds(PAD + y, 1), :]
            total = total + jnp.where(lane == (cell & (lanes - 1)), values_row, 0.0) * weight[t, obs]
        at = column * 32 + ((around & 3) + other) * 8 + slot
        picked[pl.ds(at, 1), :] = total
        return carry

    lax.fori_loop(0, 8 * per, one, 0)
    ones = jnp.ones((values.shape[0], lanes), jnp.float32)
    values[...] = lax.dot_general(
        ones, picked[...], (((1,), (1,)), ((), ())), precision=HIGH, preferred_element_type=jnp.float32
    )


def prepare_kernel(chips, wells, rate, log_perm, value, var, noise, q_out, blocks, tables, q, sems):
    rows = log_perm.shape[2] // blocks.shape[0]
    copies = issue(
        [(log_perm.at[:, :, pl.ds(b * rows, rows), :], blocks.at[b]) for b in range(blocks.shape[0])],
        sems,
        0,
    )
    odd, chip, _ = position(chips)
    ny, nz = q.shape[1], q.shape[2]
    lane = lax.broadcasted_iota(jnp.int32, (1, nz), 1)
    q[...] = jnp.zeros_like(q)

    def one(n, carry):
        cell = wells[n]
        x = lax.shift_right_logical(cell, 14)
        y = lax.shift_right_logical(cell, 7) & (ny - 1)
        behind = jnp.where(odd == 1, chip * 8 + 11 - x, x - chip * 8 + 4) & (8 * chips - 1)
        where = (jnp.minimum(behind, q.shape[0] - 1), pl.ds(y, 1), slice(None))
        here = jnp.where(behind < q.shape[0], cell & (nz - 1), -1)
        q[where] = q[where] + jnp.where(lane == here, rate[n], 0.0)
        return carry

    lax.fori_loop(0, wells.shape[0], one, 0, unroll=4)
    copies += issue([(q, q_out)], sems, len(copies))
    groups, lanes = value.shape
    wide = lanes // groups
    half = noise.shape[0] // 2
    side = lax.broadcasted_iota(jnp.int32, (1, lanes), 1) // wide
    for g in range(groups):
        total = None
        for j in range(groups):
            where = pl.ds(j * lanes, lanes)
            parts = [noise[2 * n + c : 2 * n + c + 1, where] for c in range(2) for n in range(half)]
            parts += [value[pl.ds(j, 1), :], var[pl.ds(j, 1), :], jnp.ones((6, lanes), jnp.float32)]
            column = pltpu.roll(jnp.concatenate(parts, axis=0), (4 + wide * (j - g)) % lanes, 1)
            total = column if total is None else jnp.where(side == j, column, total)
        tables[g] = total
    drain(copies)


def solve_kernel(values, tables, columns, out, coef):
    groups = tables.shape[0]
    ens = columns.shape[0]
    half = ens // 2
    spaces = groups * 8
    parts = []
    for g in range(groups):
        sides = []
        for core in range(2):
            total = None
            for near in range(4):
                chip = (4 * g + near - core) % (4 * groups)
                row = values[pl.ds(2 * chip + core, half, stride=spaces), :]
                total = row if total is None else total + row
            sides.append(total)
        parts.append(sides)
    lanes = values.shape[1]
    near_lane = (lax.broadcasted_iota(jnp.int32, (half, lanes), 1) & 31) < 8
    ends = [values[pl.ds(at, half, stride=spaces), :] for at in (0, spaces - 1)]
    far = [pltpu.roll(end, lanes - 8, 1) for end in ends]
    for core in range(2):
        own, foreign = ends[core], far[1 - core]
        parts[0][core] = parts[0][core] - own + jnp.where(near_lane, own + foreign, 0.0)
    parts = [jnp.concatenate(sides, axis=0) for sides in parts]
    small = jnp.zeros((ens, ens), jnp.float32)
    right = jnp.zeros((ens, ens), jnp.float32)
    dims = (((1,), (1,)), ((), ()))
    for g in range(groups):
        predicted = parts[g]
        dev = predicted - jnp.mean(predicted, axis=0, keepdims=True)
        spread = INFLATION * tables[g, ens + 1 : ens + 2, :]
        resid = tables[g, ens : ens + 1, :] + jnp.sqrt(spread) * tables[g, 0:ens, :] - predicted
        scaled = dev / spread
        small = small + lax.dot_general(
            scaled, dev, dims, precision=HIGH, preferred_element_type=jnp.float32
        )
        right = right + lax.dot_general(
            scaled, resid, dims, precision=HIGH, preferred_element_type=jnp.float32
        )
    row = lax.broadcasted_iota(jnp.int32, (ens, ens), 0)
    col = lax.broadcasted_iota(jnp.int32, (ens, ens), 1)
    left = small + jnp.where(row == col, ens - 1.0, 0.0)
    for k in range(ens):
        pivot = left[k : k + 1, k : k + 1]
        left_row = left[k : k + 1, :] / pivot
        right_row = right[k : k + 1, :] / pivot
        factor = left[:, k : k + 1]
        here = row == k
        left = jnp.where(here, left_row, left - factor * left_row)
        right = jnp.where(here, right_row, right - factor * right_row)
    mixing = right - jnp.mean(right, axis=0, keepdims=True) + jnp.where(row == col, 1.0, 0.0)
    rows, wide = columns.shape[2], columns.shape[3]

    def natural(place):
        return 2 * place if place < half else 2 * (place - half) + 1

    for j in range(ens):
        for m in range(ens):
            at = natural(j) * ens + natural(m)
            coef[at] = jnp.broadcast_to(mixing[j : j + 1, m : m + 1], (8, wide))

    def one(n, carry):
        part = [columns[j, n] for j in range(ens)]
        for m in range(ens):
            for r0 in range(0, rows, 8):
                total = coef[m] * part[0][r0 : r0 + 8]
                for j in range(1, ens):
                    total = total + coef[j * ens + m] * part[j][r0 : r0 + 8]
                out[m, n, r0 : r0 + 8, :] = total
        return carry

    lax.fori_loop(0, columns.shape[1], one, 0)


def body(
    log_perm,
    saturation,
    pressure_init,
    wells,
    well_rate,
    obs_index,
    obs_weight,
    obs_value,
    obs_var,
    noise,
):
    members, width, ny, nz = log_perm.shape
    spaces = lax.axis_size("space")
    mems = lax.axis_size("mem")
    odd = lax.axis_index("space") % 2
    chips = spaces // 2
    devices = mems * spaces
    ens = members * mems
    grid = (ny, nz)
    f32 = jnp.float32

    def part(field, start, size):
        return lax.dynamic_slice_in_dim(field, start, size, axis=0)

    def plane(count):
        return pltpu.VMEM((count,) + grid, f32)

    def call(kernel, name, **more):
        return pl.pallas_call(
            functools.partial(kernel, chips) if kernel is not third_kernel else kernel,
            name=name,
            **more,
        )

    grant = pltpu.CompilerParams(vmem_limit_bytes=GRANT)
    other = part(log_perm, 1 - odd, 1)[0]
    swap_out = jnp.concatenate([other, saturation, pressure_init])
    swapped = lax.ppermute(swap_out, "space", [(i, i ^ 1) for i in range(spaces)])
    edge_out = jnp.concatenate([other, part(saturation, odd * 2, 2), part(pressure_init, odd, 3)])
    ends = spaces - 1
    edge_in = lax.ppermute(
        edge_out,
        "space",
        [(0, 0), (ends, ends)] + [(i, i + 1 if i % 2 else i - 1) for i in range(1, ends)],
    )
    sems = pltpu.SemaphoreType.DMA((16,))
    q, blocks, tables = call(
        prepare_kernel,
        "prepare",
        out_shape=(
            pltpu.HBM((12,) + grid, f32),
            pltpu.HBM((mems, members, width, ny // mems, nz), f32),
            jax.ShapeDtypeStruct((4, 16, nz), f32),
        ),
        in_specs=[SMEM, SMEM, FAR] + [VMEM] * 3,
        out_specs=(FAR, FAR, VMEM),
        scratch_shapes=[plane(12), sems],
        compiler_params=grant,
    )(wells, well_rate, log_perm, obs_value.reshape(4, nz), obs_var.reshape(4, nz), noise)
    scratch = tile_scratch(ny, nz) + [plane(8)]
    keep, send, perm_tile = call(
        first_kernel,
        "first",
        out_shape=(plane(PLANES), plane(8), pltpu.HBM((8,) + grid, f32)),
        in_specs=[FAR] * 4 + [VMEM],
        out_specs=(VMEM, VMEM, FAR),
        scratch_shapes=scratch + [plane(4), sems],
        compiler_params=pltpu.CompilerParams(vmem_limit_bytes=GRANT + 1_400_000),
    )(log_perm, saturation, pressure_init, q, near(swapped))
    onward = [(i, i + 2) for i in range(0, ends - 1, 2)] + [(ends - 1, ends)]
    onward += [(i, i - 2) for i in range(3, spaces, 2)] + [(1, 0)]
    back = [(b, a) for a, b in onward]
    got = lax.ppermute(send, "space", onward)
    keep, send, perm_edge = call(
        second_kernel,
        "second",
        out_shape=(plane(PLANES), plane(PLANES), pltpu.HBM((8,) + grid, f32)),
        in_specs=[FAR] * 3 + [VMEM] * 2,
        out_specs=(VMEM, VMEM, FAR),
        scratch_shapes=scratch + [plane(9), sems],
        compiler_params=grant,
    )(perm_tile, edge_in, q, near(keep), near(got))
    got = lax.ppermute(send, "space", back)
    columns = lax.all_to_all(blocks, "mem", 0, 0, tiled=True).reshape(ens, width, ny // mems, nz)
    keep, send = call(
        third_kernel,
        "third",
        out_shape=(plane(PLANES), plane(PLANES)),
        in_specs=[FAR] * 3 + [VMEM] * 2,
        out_specs=(VMEM,) * 2,
        scratch_shapes=scratch + [sems],
        compiler_params=grant,
    )(perm_tile, q, columns, near(keep), near(got))
    got = lax.ppermute(send, "space", onward)
    taps = obs_index.T.shape
    values = call(
        last_kernel,
        "last",
        out_shape=pltpu.HBM((devices, nz), f32),
        in_specs=[FAR] * 4 + [VMEM] * 2,
        out_specs=VMEM,
        scratch_shapes=scratch
        + [pltpu.SMEM(taps, jnp.int32), pltpu.SMEM(taps, f32), pltpu.VMEM((nz, nz), f32), sems],
        compiler_params=grant,
    )(perm_edge, q, obs_index.T, obs_weight.T, near(keep), near(got))
    values = lax.all_to_all(
        values.reshape(devices, 1, nz), ("mem", "space"), 0, 0, tiled=True
    ).reshape(devices, nz)
    return pl.pallas_call(
        solve_kernel,
        out_shape=jax.ShapeDtypeStruct(columns.shape, f32),
        in_specs=[VMEM] * 3,
        out_specs=VMEM,
        scratch_shapes=[pltpu.VMEM((ens**2, 8, nz), f32)],
        name="solve",
    )(values, tables, columns)


def solution(mesh):
    placed = (
        P("mem", "space", None, None),
        P("space", None, None),
        P("space", None, None),
        P(),
        P(),
        P(),
        P(),
        P(),
        P(),
        P(),
    )
    return jax.shard_map(
        body, mesh=mesh, in_specs=placed, out_specs=P(None, "space", "mem", None), check_vma=False
    )
```

```python
import functools

import jax
import jax.numpy as jnp
from jax import lax
from jax.experimental import pallas as pl
from jax.experimental.pallas import tpu as pltpu
from jax.sharding import PartitionSpec as P


INFLATION = 4.0
STEP = 0.1
PAD = 8
CHUNK = 32
HIGH = lax.Precision.HIGHEST
FAR = pl.BlockSpec(memory_space=pltpu.HBM)
SMEM = pl.BlockSpec(memory_space=pltpu.SMEM)
VMEM = pl.BlockSpec(memory_space=pltpu.VMEM)

S0, P0, S1, P1, S2, L2 = (0, 1), (2, 3, 4), (5, 6, 7), (8, 9, 10), 11, 12
PLANES = 13
GRANT = 56 << 20


def spot(row):
    return row + 1 + (row >= 4)


class Tile:
    def __init__(self, lam_a, lam_b, frac_a, frac_b, p_a, p_b, s_a, s_b, perm, q, q_row, cut):
        self.lam = (lam_a, lam_b)
        self.frac = (frac_a, frac_b)
        self.p = (p_a, p_b)
        self.s = (s_a, s_b)
        self.perm = perm
        self.q = q
        self.q_row = q_row
        self.ny = perm.shape[1]
        self.cut = cut

    def clear(self):
        for ref in self.lam + self.frac + self.p:
            tall, wide = ref.shape[1:]
            edge = jnp.zeros((PAD, wide), jnp.float32)
            for r in range(ref.shape[0]):
                ref[r, 0:PAD, :] = edge
                ref[r, tall - PAD : tall, :] = edge
            ref[5, :, :] = jnp.zeros((tall, wide), jnp.float32)

    def rows(self, first, last, fn):
        def one(row, carry):
            far = row >= 4
            st = row + 1 + far.astype(jnp.int32)
            joined = 1 - self.cut
            up = st + 1 + jnp.where(row == 3, joined, 0)
            down = st - 1 - jnp.where(row == 4, joined, 0)
            for y0 in range(0, self.ny, CHUNK):
                fn(row, st, up, down, y0)
            return carry

        lax.fori_loop(first, last + 1, one, 0)

    def props(self, level, first, last):
        def fn(row, st, up, down, y0):
            inner = pl.ds(y0, CHUNK)
            sat = self.s[level][st, inner, :]
            lam, frac = props(self.perm[row, inner, :], sat)
            self.lam[level][st, pl.ds(PAD + y0, CHUNK), :] = lam
            self.frac[level][st, pl.ds(PAD + y0, CHUNK), :] = frac

        self.rows(first, last, fn)

    def saturate(self, level, first, last):
        lam_r, frac_r, p_r = self.lam[level], self.frac[level], self.p[level]
        new = 1 - level
        lanes = lam_r.shape[2]
        lane = lax.broadcasted_iota(jnp.int32, (CHUNK, lanes), 1)
        is_first, is_last = lane == 0, lane == lanes - 1

        def fn(row, st, up, down, y0):
            inner = pl.ds(PAD + y0, CHUNK)
            lam, frac, press = lam_r[st, inner, :], frac_r[st, inner, :], p_r[st, inner, :]

            def face(index, where):
                flux = (lam + lam_r[index, where, :]) * (press - p_r[index, where, :])
                return flux * jnp.where(flux > 0.0, frac, frac_r[index, where, :])

            out = face(up, inner) + face(down, inner)
            out = out + face(st, pl.ds(PAD + y0 + 1, CHUNK))
            out = out + face(st, pl.ds(PAD + y0 - 1, CHUNK))
            flux = (lam + pltpu.roll(lam, lanes - 1, 1)) * (press - pltpu.roll(press, lanes - 1, 1))
            moved = flux * jnp.where(flux > 0.0, frac, pltpu.roll(frac, lanes - 1, 1))
            edge = jnp.maximum(lam * press, 0.0) * frac
            out = out + jnp.where(is_last, edge, moved)
            out = out + jnp.where(is_first, edge, pltpu.roll(-moved, 1, 1))
            q = self.q[self.q_row(row), pl.ds(y0, CHUNK), :]
            water = q * jnp.where(q > 0.0, 1.0, frac)
            sat = self.s[level][st, pl.ds(y0, CHUNK), :]
            sat = jnp.clip(sat + STEP * (water - out), 0.0, 1.0)
            self.s[new][st, pl.ds(y0, CHUNK), :] = sat
            lam, frac = props(self.perm[row, pl.ds(y0, CHUNK), :], sat)
            self.lam[new][st, inner, :] = lam
            self.frac[new][st, inner, :] = frac

        self.rows(first, last, fn)

    def pressure(self, level, first, last):
        new = 1 - level
        lam_r, p_r, out_r = self.lam[new], self.p[level], self.p[new]
        lanes = lam_r.shape[2]
        lane = lax.broadcasted_iota(jnp.int32, (CHUNK, lanes), 1)
        not_first, not_last = lane > 0, lane < lanes - 1

        def fn(row, st, up, down, y0):
            inner = pl.ds(PAD + y0, CHUNK)
            lam, press = lam_r[st, inner, :], p_r[st, inner, :]
            numer = press + self.q[self.q_row(row), pl.ds(y0, CHUNK), :]
            denom = jnp.ones_like(lam)
            for index, where in (
                (up, inner),
                (down, inner),
                (st, pl.ds(PAD + y0 + 1, CHUNK)),
                (st, pl.ds(PAD + y0 - 1, CHUNK)),
            ):
                trans = lam + lam_r[index, where, :]
                numer = numer + trans * p_r[index, where, :]
                denom = denom + trans
            for shift, mask in ((lanes - 1, not_last), (1, not_first)):
                trans = lam + jnp.where(mask, pltpu.roll(lam, shift, 1), 0.0)
                numer = numer + trans * jnp.where(mask, pltpu.roll(press, shift, 1), 0.0)
                denom = denom + trans
            out_r[st, inner, :] = numer / denom

        self.rows(first, last, fn)


def props(perm_half, sat):
    water = sat * sat
    oil = (1.0 - sat) * (1.0 - sat) * 0.25
    total = water + oil
    return perm_half * total, water / total


def near(array):
    return pltpu.with_memory_space_constraint(array, pltpu.VMEM)


def tile_scratch(ny, nz):
    tall = ny + 2 * PAD
    wide = [pltpu.VMEM((11, tall, nz), jnp.float32) for _ in range(6)]
    flat = [pltpu.VMEM((count, ny, nz), jnp.float32) for count in (11, 11, 12)]
    return wide + flat


def issue(pairs, sems, first):
    copies = []
    for n, (src, dst) in enumerate(pairs):
        copy = pltpu.make_async_copy(src, dst, sems.at[first + n])
        copy.start()
        copies.append(copy)
    return copies


def drain(copies):
    for copy in copies:
        copy.wait()


def move(pairs):
    tall = min(src.shape[0] for src, _ in pairs)

    def one(n, carry):
        where = pl.ds(pl.multiple_of(n * CHUNK, CHUNK), CHUNK)
        for src, dst in pairs:
            dst[where, :] = src[where, :]
        return carry

    lax.fori_loop(0, tall // CHUNK, one, 0)


def position(chips):
    place = lax.axis_index("space")
    odd, chip = place & 1, lax.shift_right_logical(place, 1)
    end = jnp.where(odd == 1, chips - 1, 0)
    return odd, chip, (chip == end).astype(jnp.int32)


def beyond(tile, row):
    return jnp.where(tile.cut == 1, 5, spot(row))


def give_early(tile, keep, send, send_early):
    pairs = []
    inner = pl.ds(PAD, tile.ny)
    sides = [(keep, lambda d: d)] + ([(send, lambda d: 7 - d)] if send_early else [])
    for out, row in sides:
        for d in range(2):
            pairs.append((tile.s[0].at[spot(row(d))], out.at[S0[d]]))
        for d in range(3):
            pairs.append((tile.p[0].at[spot(row(d)), inner], out.at[P0[d]]))
    return pairs


def give_late(tile, out, near, base):
    row, step = near
    inner = pl.ds(PAD, tile.ny)
    pairs = []
    for n, d in enumerate((1, 2, 3)):
        pairs.append((tile.s[1].at[spot(row + step * d)], out.at[S1[n] - base]))
    for n, d in enumerate((2, 3, 4)):
        st = beyond(tile, row + step * d) if d == 4 else spot(row + step * d)
        pairs.append((tile.p[1].at[st, inner], out.at[P1[n] - base]))
    return pairs


def give_last(tile, out, near, base):
    row, step = near
    inner = pl.ds(PAD, tile.ny)
    return [
        (tile.s[0].at[spot(row + step * 3)], out.at[S2 - base]),
        (tile.lam[0].at[beyond(tile, row + step * 4), inner], out.at[L2 - base]),
    ]


def take(tile, early, late, base_row, step):
    inner = pl.ds(PAD, tile.ny)
    start, s_next, p_next, last = [], [], [], []
    for d in range(2):
        start.append((early(S0[d]), tile.s[0].at[base_row + step * d]))
    for d in range(3):
        start.append((early(P0[d]), tile.p[0].at[base_row + step * d, inner]))
    for n, d in enumerate((1, 2, 3)):
        s_next.append((late(S1[n]), tile.s[1].at[base_row + step * d]))
    for n, d in enumerate((2, 3, 4)):
        p_next.append((late(P1[n]), tile.p[1].at[base_row + step * d, inner]))
    last.append((late(S2), tile.s[0].at[base_row + step * 3]))
    last.append((late(L2), tile.lam[0].at[base_row + step * 4, inner]))
    return start, s_next, p_next, last


def advance(tile, keep, send, send_early):
    base = 0 if send_early else S1[0]
    move(give_early(tile, keep, send, send_early))
    tile.saturate(0, 1, 6)
    tile.pressure(0, 2, 5)
    tile.saturate(1, 3, 4)
    pairs = []
    for out, near_row, at in ((send, (7, -1), base), (keep, (0, 1), 0)):
        pairs += give_late(tile, out, near_row, at) + give_last(tile, out, near_row, at)
    move(pairs)


def first_kernel(chips, log_perm, own_sat, own_press, q, swapped, keep, send, perm_out, *refs):
    odd, _, _ = position(chips)
    perm, raw, sems = refs[9:]
    tile = Tile(*refs[:8], perm, refs[8], lambda row: row + 4, jnp.int32(0))
    inner = pl.ds(PAD, tile.ny)

    def place(n):
        return jnp.where(odd == 1, 3 - n, n)

    pairs = [(log_perm.at[odd], raw)]
    for n in range(4):
        pairs.append((own_sat.at[place(n)], tile.s[0].at[spot(n)]))
        pairs.append((own_press.at[place(n)], tile.p[0].at[spot(n), inner]))
    copies = issue(pairs, sems, 0)
    q_copy = issue([(q, tile.q)], sems, len(pairs))
    tile.clear()
    pairs = []
    for n in range(4):
        pairs.append((swapped.at[4 + place(n)], tile.s[0].at[spot(4 + n)]))
        pairs.append((swapped.at[8 + place(n)], tile.p[0].at[spot(4 + n), inner]))
    move(pairs)

    def halve(src, base):
        def one(n, carry):
            for y0 in range(0, tile.ny, CHUNK):
                where = pl.ds(y0, CHUNK)
                perm[base + n, where, :] = 0.5 * jnp.exp(src[place(n), where, :])
            return carry

        lax.fori_loop(0, 4, one, 0)

    halve(swapped, 4)
    drain(copies)
    halve(raw, 0)
    perm_copy = issue([(perm, perm_out)], sems, 10)
    tile.props(0, 0, 7)
    drain(q_copy)
    advance(tile, keep, send, False)
    drain(perm_copy)


def fill(tile, sides, perm_copy, q_copy):
    tile.clear()
    groups = [sum((side[n] for side in sides), []) for n in range(4)]
    move(groups[0] + groups[1] + groups[2])
    drain(perm_copy)
    tile.props(0, 2, 5)
    tile.props(1, 0, 2)
    tile.props(1, 5, 7)
    drain(q_copy)
    tile.saturate(0, 3, 4)
    tile.pressure(0, 2, 5)
    move(groups[3])
    tile.props(0, 0, 0)
    tile.props(0, 7, 7)
    tile.saturate(1, 1, 6)
    tile.pressure(1, 0, 7)


def edge_q(cut):
    return lambda row: jnp.where((cut == 1) & (row >= 4), row, 7 - row)


def second_kernel(chips, perm_own, raw_in, q, kept, late_in, keep, send, perm_out, *refs):
    odd, _, end = position(chips)
    perm, raw, sems = refs[9:]
    tile = Tile(*refs[:8], perm, refs[8], edge_q(end), end)
    straight = odd ^ end

    def place(n, count):
        return jnp.where(straight == 1, n, count - 1 - n)

    def early(plane):
        if plane in S0:
            return raw.at[4 + place(plane, 2)]
        return raw.at[6 + place(plane - 2, 3)]

    copies = issue([(raw_in, raw)] + [(perm_own.at[3 - d], perm.at[d]) for d in range(4)], sems, 0)
    q_copy = issue([(q, tile.q)], sems, 5)
    drain(copies)

    def permeability(d, carry):
        for y0 in range(0, tile.ny, CHUNK):
            where = pl.ds(y0, CHUNK)
            perm[4 + d, where, :] = 0.5 * jnp.exp(raw[place(d, 4), where, :])
        return carry

    lax.fori_loop(0, 4, permeability, 0)
    perm_copy = issue([(perm, perm_out)], sems, 6)
    sides = (
        take(tile, lambda n: kept.at[n], lambda n: kept.at[n], 4, -1),
        take(tile, early, lambda n: late_in.at[n - S1[0]], 6, 1),
    )
    fill(tile, sides, [], q_copy)
    advance(tile, keep, send, True)
    drain(perm_copy)


def both_sides(tile, kept, got):
    return (
        take(tile, lambda n: kept.at[n], lambda n: kept.at[n], 4, -1),
        take(tile, lambda n: got.at[n], lambda n: got.at[n], 6, 1),
    )


def third_kernel(perm, q, columns, kept, got, keep, send, *refs):
    del columns
    tile = Tile(*refs[:8], refs[9], refs[8], lambda row: row + 4, jnp.int32(0))
    sems = refs[10]
    perm_copy = issue([(perm, tile.perm)], sems, 0)
    q_copy = issue([(q, tile.q)], sems, 1)
    fill(tile, both_sides(tile, kept, got), perm_copy, q_copy)
    advance(tile, keep, send, True)


def last_kernel(chips, perm, q, index_in, weight_in, kept, got, values, *refs):
    odd, chip, end = position(chips)
    tile = Tile(*refs[:8], refs[9], refs[8], edge_q(end), end)
    index, weight, picked, sems = refs[10:]
    perm_copy = issue([(perm, tile.perm)], sems, 0)
    q_copy = issue([(q, tile.q)], sems, 1)
    tables = issue([(index_in, index), (weight_in, weight)], sems, 2)
    fill(tile, both_sides(tile, kept, got), perm_copy, q_copy)
    drain(tables)
    around = (chip + odd) & (chips - 1)
    total_rows = 8 * chips
    per = index.shape[1] // total_rows
    lanes = kept.shape[2]
    lane = lax.broadcasted_iota(jnp.int32, (1, lanes), 1)
    picked[...] = jnp.zeros_like(picked)

    def one(n, carry):
        slot = n & 7
        row = jnp.where(odd == 1, slot, 7 - slot)
        st = row + 1 + (row >= 4).astype(jnp.int32)
        other = end * (row >= 4).astype(jnp.int32)
        slot = jnp.where(other == 1, 7 - slot, slot)
        column = lax.shift_right_logical(n, 3)
        obs = column * total_rows + ((8 * around - 4 + slot) & (total_rows - 1))
        total = jnp.zeros((1, lanes), jnp.float32)
        for t in range(index.shape[0]):
            cell = index[t, obs]
            y = lax.shift_right_logical(cell, 7) & (tile.ny - 1)
            values_row = tile.p[0][st, pl.ds(PAD + y, 1), :]
            total = total + jnp.where(lane == (cell & (lanes - 1)), values_row, 0.0) * weight[t, obs]
        at = column * 32 + ((around & 3) + other) * 8 + slot
        picked[pl.ds(at, 1), :] = total
        return carry

    lax.fori_loop(0, 8 * per, one, 0)
    ones = jnp.ones((values.shape[0], lanes), jnp.float32)
    values[...] = lax.dot_general(
        ones, picked[...], (((1,), (1,)), ((), ())), precision=HIGH, preferred_element_type=jnp.float32
    )


def prepare_kernel(chips, wells, rate, log_perm, value, var, noise, q_out, blocks, tables, q, held, sems):
    rows = log_perm.shape[2] // blocks.shape[0]
    count = blocks.shape[0]
    load = issue([(log_perm, held)], sems, count)
    odd, chip, _ = position(chips)
    ny, nz = q.shape[1], q.shape[2]
    lane = lax.broadcasted_iota(jnp.int32, (1, nz), 1)
    q[...] = jnp.zeros_like(q)

    def one(n, carry):
        cell = wells[n]
        x = lax.shift_right_logical(cell, 14)
        y = lax.shift_right_logical(cell, 7) & (ny - 1)
        behind = jnp.where(odd == 1, chip * 8 + 11 - x, x - chip * 8 + 4) & (8 * chips - 1)
        where = (jnp.minimum(behind, q.shape[0] - 1), pl.ds(y, 1), slice(None))
        here = jnp.where(behind < q.shape[0], cell & (nz - 1), -1)
        q[where] = q[where] + jnp.where(lane == here, rate[n], 0.0)
        return carry

    lax.fori_loop(0, wells.shape[0], one, 0, unroll=4)
    copies = issue([(q, q_out)], sems, count + 1)
    drain(load)
    copies += issue(
        [(held.at[:, :, pl.ds(b * rows, rows), :], blocks.at[b]) for b in range(count)], sems, 0
    )
    groups, lanes = value.shape
    wide = lanes // groups
    half = noise.shape[0] // 2
    side = lax.broadcasted_iota(jnp.int32, (1, lanes), 1) // wide
    for g in range(groups):
        total = None
        for j in range(groups):
            where = pl.ds(j * lanes, lanes)
            parts = [noise[2 * n + c : 2 * n + c + 1, where] for c in range(2) for n in range(half)]
            parts += [value[pl.ds(j, 1), :], var[pl.ds(j, 1), :], jnp.ones((6, lanes), jnp.float32)]
            column = pltpu.roll(jnp.concatenate(parts, axis=0), (4 + wide * (j - g)) % lanes, 1)
            total = column if total is None else jnp.where(side == j, column, total)
        tables[g] = total
    drain(copies)


def solve_kernel(values, tables, columns_in, out_to, coef, columns, out, sems):
    count = columns.shape[1]
    loads = issue([(columns_in.at[:, n], columns.at[:, n]) for n in range(count)], sems, 0)

    groups = tables.shape[0]
    ens = columns.shape[0]
    half = ens // 2
    spaces = groups * 8
    parts = []
    for g in range(groups):
        sides = []
        for core in range(2):
            total = None
            for near in range(4):
                chip = (4 * g + near - core) % (4 * groups)
                row = values[pl.ds(2 * chip + core, half, stride=spaces), :]
                total = row if total is None else total + row
            sides.append(total)
        parts.append(sides)
    lanes = values.shape[1]
    near_lane = (lax.broadcasted_iota(jnp.int32, (half, lanes), 1) & 31) < 8
    ends = [values[pl.ds(at, half, stride=spaces), :] for at in (0, spaces - 1)]
    far = [pltpu.roll(end, lanes - 8, 1) for end in ends]
    for core in range(2):
        own, foreign = ends[core], far[1 - core]
        parts[0][core] = parts[0][core] - own + jnp.where(near_lane, own + foreign, 0.0)
    parts = [jnp.concatenate(sides, axis=0) for sides in parts]
    small = jnp.zeros((ens, ens), jnp.float32)
    right = jnp.zeros((ens, ens), jnp.float32)
    dims = (((1,), (1,)), ((), ()))
    for g in range(groups):
        predicted = parts[g]
        dev = predicted - jnp.mean(predicted, axis=0, keepdims=True)
        spread = INFLATION * tables[g, ens + 1 : ens + 2, :]
        resid = tables[g, ens : ens + 1, :] + jnp.sqrt(spread) * tables[g, 0:ens, :] - predicted
        scaled = dev / spread
        small = small + lax.dot_general(
            scaled, dev, dims, precision=HIGH, preferred_element_type=jnp.float32
        )
        right = right + lax.dot_general(
            scaled, resid, dims, precision=HIGH, preferred_element_type=jnp.float32
        )
    row = lax.broadcasted_iota(jnp.int32, (ens, ens), 0)
    col = lax.broadcasted_iota(jnp.int32, (ens, ens), 1)
    left = small + jnp.where(row == col, ens - 1.0, 0.0)
    for k in range(ens):
        pivot = left[k : k + 1, k : k + 1]
        left_row = left[k : k + 1, :] / pivot
        right_row = right[k : k + 1, :] / pivot
        factor = left[:, k : k + 1]
        here = row == k
        left = jnp.where(here, left_row, left - factor * left_row)
        right = jnp.where(here, right_row, right - factor * right_row)
    mixing = right - jnp.mean(right, axis=0, keepdims=True) + jnp.where(row == col, 1.0, 0.0)
    rows, wide = columns.shape[2], columns.shape[3]

    def natural(place):
        return 2 * place if place < half else 2 * (place - half) + 1

    for j in range(ens):
        for m in range(ens):
            at = natural(j) * ens + natural(m)
            coef[at] = jnp.broadcast_to(mixing[j : j + 1, m : m + 1], (8, wide))

    stores = []
    for n in range(count):
        loads[n].wait()
        part = [columns[j, n] for j in range(ens)]
        for m in range(ens):
            for r0 in range(0, rows, 8):
                total = coef[m] * part[0][r0 : r0 + 8]
                for j in range(1, ens):
                    total = total + coef[j * ens + m] * part[j][r0 : r0 + 8]
                out[m, n, r0 : r0 + 8, :] = total
        stores += issue([(out.at[:, n], out_to.at[:, n])], sems, count + n)
    drain(stores)


def body(
    log_perm,
    saturation,
    pressure_init,
    wells,
    well_rate,
    obs_index,
    obs_weight,
    obs_value,
    obs_var,
    noise,
):
    members, width, ny, nz = log_perm.shape
    spaces = lax.axis_size("space")
    mems = lax.axis_size("mem")
    odd = lax.axis_index("space") % 2
    chips = spaces // 2
    devices = mems * spaces
    ens = members * mems
    grid = (ny, nz)
    f32 = jnp.float32

    def part(field, start, size):
        return lax.dynamic_slice_in_dim(field, start, size, axis=0)

    def plane(count):
        return pltpu.VMEM((count,) + grid, f32)

    def call(kernel, name, **more):
        return pl.pallas_call(
            functools.partial(kernel, chips) if kernel is not third_kernel else kernel,
            name=name,
            **more,
        )

    grant = pltpu.CompilerParams(vmem_limit_bytes=GRANT)
    other = part(log_perm, 1 - odd, 1)[0]
    swap_out = jnp.concatenate([other, saturation, pressure_init])
    swapped = lax.ppermute(swap_out, "space", [(i, i ^ 1) for i in range(spaces)])
    edge_out = jnp.concatenate([other, part(saturation, odd * 2, 2), part(pressure_init, odd, 3)])
    ends = spaces - 1
    edge_in = lax.ppermute(
        edge_out,
        "space",
        [(0, 0), (ends, ends)] + [(i, i + 1 if i % 2 else i - 1) for i in range(1, ends)],
    )
    sems = pltpu.SemaphoreType.DMA((16,))
    q, blocks, tables = call(
        prepare_kernel,
        "prepare",
        out_shape=(
            pltpu.HBM((12,) + grid, f32),
            pltpu.HBM((mems, members, width, ny // mems, nz), f32),
            jax.ShapeDtypeStruct((4, 16, nz), f32),
        ),
        in_specs=[SMEM, SMEM, FAR] + [VMEM] * 3,
        out_specs=(FAR, FAR, VMEM),
        scratch_shapes=[plane(12), pltpu.VMEM(log_perm.shape, f32), sems],
        compiler_params=grant,
    )(wells, well_rate, log_perm, obs_value.reshape(4, nz), obs_var.reshape(4, nz), noise)
    scratch = tile_scratch(ny, nz) + [plane(8)]
    keep, send, perm_tile = call(
        first_kernel,
        "first",
        out_shape=(plane(PLANES), plane(8), pltpu.HBM((8,) + grid, f32)),
        in_specs=[FAR] * 4 + [VMEM],
        out_specs=(VMEM, VMEM, FAR),
        scratch_shapes=scratch + [plane(4), sems],
        compiler_params=pltpu.CompilerParams(vmem_limit_bytes=GRANT + 1_400_000),
    )(log_perm, saturation, pressure_init, q, near(swapped))
    onward = [(i, i + 2) for i in range(0, ends - 1, 2)] + [(ends - 1, ends)]
    onward += [(i, i - 2) for i in range(3, spaces, 2)] + [(1, 0)]
    back = [(b, a) for a, b in onward]
    got = lax.ppermute(send, "space", onward)
    keep, send, perm_edge = call(
        second_kernel,
        "second",
        out_shape=(plane(PLANES), plane(PLANES), pltpu.HBM((8,) + grid, f32)),
        in_specs=[FAR] * 3 + [VMEM] * 2,
        out_specs=(VMEM, VMEM, FAR),
        scratch_shapes=scratch + [plane(9), sems],
        compiler_params=grant,
    )(perm_tile, edge_in, q, near(keep), near(got))
    got = lax.ppermute(send, "space", back)
    columns = lax.all_to_all(blocks, "mem", 0, 0, tiled=True).reshape(ens, width, ny // mems, nz)
    keep, send = call(
        third_kernel,
        "third",
        out_shape=(plane(PLANES), plane(PLANES)),
        in_specs=[FAR] * 3 + [VMEM] * 2,
        out_specs=(VMEM,) * 2,
        scratch_shapes=scratch + [sems],
        compiler_params=grant,
    )(perm_tile, q, columns, near(keep), near(got))
    got = lax.ppermute(send, "space", onward)
    taps = obs_index.T.shape
    values = call(
        last_kernel,
        "last",
        out_shape=pltpu.HBM((devices, nz), f32),
        in_specs=[FAR] * 4 + [VMEM] * 2,
        out_specs=VMEM,
        scratch_shapes=scratch
        + [pltpu.SMEM(taps, jnp.int32), pltpu.SMEM(taps, f32), pltpu.VMEM((nz, nz), f32), sems],
        compiler_params=grant,
    )(perm_edge, q, obs_index.T, obs_weight.T, near(keep), near(got))
    values = lax.all_to_all(
        values.reshape(devices, 1, nz), ("mem", "space"), 0, 0, tiled=True
    ).reshape(devices, nz)
    return pl.pallas_call(
        solve_kernel,
        out_shape=jax.ShapeDtypeStruct(columns.shape, f32),
        in_specs=[VMEM, VMEM, FAR],
        out_specs=FAR,
        scratch_shapes=[pltpu.VMEM((ens**2, 8, nz), f32)]
        + [pltpu.VMEM(columns.shape, f32) for _ in range(2)]
        + [sems],
        name="solve",
    )(values, tables, columns)


def solution(mesh):
    placed = (
        P("mem", "space", None, None),
        P("space", None, None),
        P("space", None, None),
        P(),
        P(),
        P(),
        P(),
        P(),
        P(),
        P(),
    )
    return jax.shard_map(
        body, mesh=mesh, in_specs=placed, out_specs=P(None, "space", "mem", None), check_vma=False
    )
```

```python
import functools

import jax
import jax.numpy as jnp
from jax import lax
from jax.experimental import pallas as pl
from jax.experimental.pallas import tpu as pltpu
from jax.sharding import PartitionSpec as P


INFLATION = 4.0
STEP = 0.1
PAD = 8
CHUNK = 32
HIGH = lax.Precision.HIGHEST
FAR = pl.BlockSpec(memory_space=pltpu.HBM)
SMEM = pl.BlockSpec(memory_space=pltpu.SMEM)
VMEM = pl.BlockSpec(memory_space=pltpu.VMEM)

S0, P0, S1, P1, S2, L2 = (0, 1), (2, 3, 4), (5, 6, 7), (8, 9, 10), 11, 12
PLANES = 13
GRANT = 56 << 20


def spot(row):
    return row + 1 + (row >= 4)


class Tile:
    def __init__(self, lam_a, lam_b, frac_a, frac_b, p_a, p_b, s_a, s_b, sides, perm, q, q_row, cut):
        self.lam = (lam_a, lam_b)
        self.frac = (frac_a, frac_b)
        self.p = (p_a, p_b)
        self.s = (s_a, s_b)
        self.sides = sides
        self.perm = perm
        self.q = q
        self.q_row = q_row
        self.ny = perm.shape[1]
        self.cut = cut

    def clear(self):
        for ref in self.lam + self.frac + self.p:
            tall, wide = ref.shape[1:]
            edge = jnp.zeros((PAD, wide), jnp.float32)
            for r in range(ref.shape[0]):
                ref[r, 0:PAD, :] = edge
                ref[r, tall - PAD : tall, :] = edge
            ref[5, :, :] = jnp.zeros((tall, wide), jnp.float32)

    def places(self, row):
        st = row + 1 + (row >= 4).astype(jnp.int32)
        joined = 1 - self.cut
        up = st + 1 + jnp.where(row == 3, joined, 0)
        down = st - 1 - jnp.where(row == 4, joined, 0)
        return st, up, down

    def rows(self, first, last, fn):
        def one(row, carry):
            for y0 in range(0, self.ny, CHUNK):
                fn(row, *self.places(row), y0)
            return carry

        lax.fori_loop(first, last + 1, one, 0)

    def run(self, phases, primed=False, then=None):
        def all_of(row, slot, which):
            for y0 in range(0, self.ny, CHUNK):
                which(row, *self.places(row), y0, slot)

        if not primed:
            all_of(jnp.int32(phases[0][0]), 0, phases[0][2])
        for phase, follower in zip(phases, phases[1:] + [then]):
            first, last, ahead, fn = phase

            def two(n, carry, first=first, ahead=ahead, fn=fn):
                row = first + 2 * n
                all_of(row + 1, 1, ahead)
                all_of(row, 0, fn)
                all_of(row + 2, 0, ahead)
                all_of(row + 1, 1, fn)
                return carry

            lax.fori_loop(0, (last - first) // 2, two, 0)
            all_of(jnp.int32(last), 1, ahead)
            all_of(jnp.int32(last - 1), 0, fn)
            if follower is not None:
                all_of(jnp.int32(follower[0]), 0, follower[2])
            all_of(jnp.int32(last), 1, fn)

    def props(self, level, first, last):
        def fn(row, st, up, down, y0):
            inner = pl.ds(y0, CHUNK)
            sat = self.s[level][st, inner, :]
            lam, frac = props(self.perm[row, inner, :], sat)
            self.lam[level][st, pl.ds(PAD + y0, CHUNK), :] = lam
            self.frac[level][st, pl.ds(PAD + y0, CHUNK), :] = frac

        self.rows(first, last, fn)

    def saturate(self, level, first, last):
        lam_r, frac_r, p_r = self.lam[level], self.frac[level], self.p[level]
        new = 1 - level
        lanes = lam_r.shape[2]
        lane = lax.broadcasted_iota(jnp.int32, (CHUNK, lanes), 1)
        is_first, is_last = lane == 0, lane == lanes - 1

        def ahead(row, st, up, down, y0, slot):
            inner = pl.ds(PAD + y0, CHUNK)
            lam, frac, press = lam_r[st, inner, :], frac_r[st, inner, :], p_r[st, inner, :]
            flux = (lam + pltpu.roll(lam, lanes - 1, 1)) * (press - pltpu.roll(press, lanes - 1, 1))
            moved = flux * jnp.where(flux > 0.0, frac, pltpu.roll(frac, lanes - 1, 1))
            edge = jnp.maximum(lam * press, 0.0) * frac
            out = jnp.where(is_last, edge, moved)
            out = out + jnp.where(is_first, edge, pltpu.roll(-moved, 1, 1))
            self.sides[2 * slot, pl.ds(y0, CHUNK), :] = out

        def fn(row, st, up, down, y0, slot):
            inner = pl.ds(PAD + y0, CHUNK)
            lam, frac, press = lam_r[st, inner, :], frac_r[st, inner, :], p_r[st, inner, :]

            def face(index, where):
                flux = (lam + lam_r[index, where, :]) * (press - p_r[index, where, :])
                return flux * jnp.where(flux > 0.0, frac, frac_r[index, where, :])

            out = face(up, inner) + face(down, inner)
            out = out + face(st, pl.ds(PAD + y0 + 1, CHUNK))
            out = out + face(st, pl.ds(PAD + y0 - 1, CHUNK))
            out = out + self.sides[2 * slot, pl.ds(y0, CHUNK), :]
            q = self.q[self.q_row(row), pl.ds(y0, CHUNK), :]
            water = q * jnp.where(q > 0.0, 1.0, frac)
            sat = self.s[level][st, pl.ds(y0, CHUNK), :]
            sat = jnp.clip(sat + STEP * (water - out), 0.0, 1.0)
            self.s[new][st, pl.ds(y0, CHUNK), :] = sat
            lam, frac = props(self.perm[row, pl.ds(y0, CHUNK), :], sat)
            self.lam[new][st, inner, :] = lam
            self.frac[new][st, inner, :] = frac

        return first, last, ahead, fn

    def pressure(self, level, first, last):
        new = 1 - level
        lam_r, p_r, out_r = self.lam[new], self.p[level], self.p[new]
        lanes = lam_r.shape[2]
        lane = lax.broadcasted_iota(jnp.int32, (CHUNK, lanes), 1)
        not_first, not_last = lane > 0, lane < lanes - 1

        def ahead(row, st, up, down, y0, slot):
            inner = pl.ds(PAD + y0, CHUNK)
            lam, press = lam_r[st, inner, :], p_r[st, inner, :]
            numer, denom = 0.0, 0.0
            for shift, mask in ((lanes - 1, not_last), (1, not_first)):
                trans = lam + jnp.where(mask, pltpu.roll(lam, shift, 1), 0.0)
                numer = numer + trans * jnp.where(mask, pltpu.roll(press, shift, 1), 0.0)
                denom = denom + trans
            self.sides[2 * slot, pl.ds(y0, CHUNK), :] = numer
            self.sides[2 * slot + 1, pl.ds(y0, CHUNK), :] = denom

        def fn(row, st, up, down, y0, slot):
            inner = pl.ds(PAD + y0, CHUNK)
            lam, press = lam_r[st, inner, :], p_r[st, inner, :]
            numer = press + self.q[self.q_row(row), pl.ds(y0, CHUNK), :]
            numer = numer + self.sides[2 * slot, pl.ds(y0, CHUNK), :]
            denom = 1.0 + self.sides[2 * slot + 1, pl.ds(y0, CHUNK), :]
            for index, where in (
                (up, inner),
                (down, inner),
                (st, pl.ds(PAD + y0 + 1, CHUNK)),
                (st, pl.ds(PAD + y0 - 1, CHUNK)),
            ):
                trans = lam + lam_r[index, where, :]
                numer = numer + trans * p_r[index, where, :]
                denom = denom + trans
            out_r[st, inner, :] = numer / denom

        return first, last, ahead, fn


def props(perm_half, sat):
    water = sat * sat
    oil = (1.0 - sat) * (1.0 - sat) * 0.25
    total = water + oil
    return perm_half * total, water / total


def near(array):
    return pltpu.with_memory_space_constraint(array, pltpu.VMEM)


def tile_scratch(ny, nz):
    tall = ny + 2 * PAD
    wide = [pltpu.VMEM((11, tall, nz), jnp.float32) for _ in range(6)]
    flat = [pltpu.VMEM((count, ny, nz), jnp.float32) for count in (11, 11, 4, 12)]
    return wide + flat


def issue(pairs, sems, first):
    copies = []
    for n, (src, dst) in enumerate(pairs):
        copy = pltpu.make_async_copy(src, dst, sems.at[first + n])
        copy.start()
        copies.append(copy)
    return copies


def drain(copies):
    for copy in copies:
        copy.wait()


def move(pairs):
    tall = min(src.shape[0] for src, _ in pairs)

    def one(n, carry):
        where = pl.ds(pl.multiple_of(n * CHUNK, CHUNK), CHUNK)
        for src, dst in pairs:
            dst[where, :] = src[where, :]
        return carry

    lax.fori_loop(0, tall // CHUNK, one, 0)


def position(chips):
    place = lax.axis_index("space")
    odd, chip = place & 1, lax.shift_right_logical(place, 1)
    end = jnp.where(odd == 1, chips - 1, 0)
    return odd, chip, (chip == end).astype(jnp.int32)


def beyond(tile, row):
    return jnp.where(tile.cut == 1, 5, spot(row))


def give_early(tile, keep, send, send_early):
    pairs = []
    inner = pl.ds(PAD, tile.ny)
    sides = [(keep, lambda d: d)] + ([(send, lambda d: 7 - d)] if send_early else [])
    for out, row in sides:
        for d in range(2):
            pairs.append((tile.s[0].at[spot(row(d))], out.at[S0[d]]))
        for d in range(3):
            pairs.append((tile.p[0].at[spot(row(d)), inner], out.at[P0[d]]))
    return pairs


def give_late(tile, out, near, base):
    row, step = near
    inner = pl.ds(PAD, tile.ny)
    pairs = []
    for n, d in enumerate((1, 2, 3)):
        pairs.append((tile.s[1].at[spot(row + step * d)], out.at[S1[n] - base]))
    for n, d in enumerate((2, 3, 4)):
        st = beyond(tile, row + step * d) if d == 4 else spot(row + step * d)
        pairs.append((tile.p[1].at[st, inner], out.at[P1[n] - base]))
    return pairs


def give_last(tile, out, near, base):
    row, step = near
    inner = pl.ds(PAD, tile.ny)
    return [
        (tile.s[0].at[spot(row + step * 3)], out.at[S2 - base]),
        (tile.lam[0].at[beyond(tile, row + step * 4), inner], out.at[L2 - base]),
    ]


def take(tile, early, late, base_row, step):
    inner = pl.ds(PAD, tile.ny)
    start, s_next, p_next, last = [], [], [], []
    for d in range(2):
        start.append((early(S0[d]), tile.s[0].at[base_row + step * d]))
    for d in range(3):
        start.append((early(P0[d]), tile.p[0].at[base_row + step * d, inner]))
    for n, d in enumerate((1, 2, 3)):
        s_next.append((late(S1[n]), tile.s[1].at[base_row + step * d]))
    for n, d in enumerate((2, 3, 4)):
        p_next.append((late(P1[n]), tile.p[1].at[base_row + step * d, inner]))
    last.append((late(S2), tile.s[0].at[base_row + step * 3]))
    last.append((late(L2), tile.lam[0].at[base_row + step * 4, inner]))
    return start, s_next, p_next, last


def advance(tile, keep, send, send_early, primed=True):
    base = 0 if send_early else S1[0]
    move(give_early(tile, keep, send, send_early))
    tile.run([tile.saturate(0, 1, 6), tile.pressure(0, 2, 5), tile.saturate(1, 3, 4)], primed)
    pairs = []
    for out, near_row, at in ((send, (7, -1), base), (keep, (0, 1), 0)):
        pairs += give_late(tile, out, near_row, at) + give_last(tile, out, near_row, at)
    move(pairs)


def first_kernel(chips, wells, rate, log_perm, own_sat, own_press, swapped, keep, send, perm_out, q_out, *refs):
    odd, _, _ = position(chips)
    perm, raw, sems = refs[10:]
    tile = Tile(*refs[:9], perm, refs[9], lambda row: row + 4, jnp.int32(0))
    inner = pl.ds(PAD, tile.ny)

    def place(n):
        return jnp.where(odd == 1, 3 - n, n)

    pairs = [(log_perm.at[odd], raw)]
    for n in range(4):
        pairs.append((own_sat.at[place(n)], tile.s[0].at[spot(n)]))
        pairs.append((own_press.at[place(n)], tile.p[0].at[spot(n), inner]))
    copies = issue(pairs, sems, 0)
    tile.clear()
    fill_sources(chips, wells, rate, tile.q)
    out_copies = issue([(tile.q, q_out)], sems, 9)
    pairs = []
    for n in range(4):
        pairs.append((swapped.at[4 + place(n)], tile.s[0].at[spot(4 + n)]))
        pairs.append((swapped.at[8 + place(n)], tile.p[0].at[spot(4 + n), inner]))
    move(pairs)

    def halve(src, base):
        def one(n, carry):
            for y0 in range(0, tile.ny, CHUNK):
                where = pl.ds(y0, CHUNK)
                perm[base + n, where, :] = 0.5 * jnp.exp(src[place(n), where, :])
            return carry

        lax.fori_loop(0, 4, one, 0)

    halve(swapped, 4)
    drain(copies)
    halve(raw, 0)
    out_copies += issue([(perm, perm_out)], sems, 10)
    tile.props(0, 0, 7)
    advance(tile, keep, send, False, False)
    drain(out_copies)


def fill(tile, sides, perm_copy, q_copy, then=None):
    tile.clear()
    groups = [sum((side[n] for side in sides), []) for n in range(4)]
    move(groups[0] + groups[1] + groups[2])
    drain(perm_copy)
    tile.props(0, 2, 5)
    tile.props(1, 0, 2)
    tile.props(1, 5, 7)
    drain(q_copy)
    move(groups[3])
    tile.props(0, 0, 0)
    tile.props(0, 7, 7)
    tile.run(
        [
            tile.saturate(0, 3, 4),
            tile.pressure(0, 2, 5),
            tile.saturate(1, 1, 6),
            tile.pressure(1, 0, 7),
        ],
        then=then,
    )


def edge_q(cut):
    return lambda row: jnp.where((cut == 1) & (row >= 4), row, 7 - row)


def second_kernel(chips, perm_own, raw_in, q, log_perm, value_in, var_in, noise_in, kept, late_in, keep, send, perm_out, blocks, tables, *refs):
    odd, _, end = position(chips)
    perm, raw, held, value, var, noise, sems = refs[10:]
    tile = Tile(*refs[:9], perm, refs[9], edge_q(end), end)
    straight = odd ^ end

    def place(n, count):
        return jnp.where(straight == 1, n, count - 1 - n)

    def early(plane):
        if plane in S0:
            return raw.at[4 + place(plane, 2)]
        return raw.at[6 + place(plane - 2, 3)]

    copies = issue([(raw_in, raw)] + [(perm_own.at[3 - d], perm.at[d]) for d in range(4)], sems, 0)
    q_copy = issue([(q, tile.q)], sems, 5)
    load = issue([(log_perm, held), (value_in, value), (var_in, var), (noise_in, noise)], sems, 7)
    drain(copies)

    def permeability(d, carry):
        for y0 in range(0, tile.ny, CHUNK):
            where = pl.ds(y0, CHUNK)
            perm[4 + d, where, :] = 0.5 * jnp.exp(raw[place(d, 4), where, :])
        return carry

    lax.fori_loop(0, 4, permeability, 0)
    perm_copy = issue([(perm, perm_out)], sems, 6)
    sides = (
        take(tile, lambda n: kept.at[n], lambda n: kept.at[n], 4, -1),
        take(tile, early, lambda n: late_in.at[n - S1[0]], 6, 1),
    )
    fill(tile, sides, [], q_copy, tile.saturate(0, 1, 6))
    drain(load)
    count = blocks.shape[0]
    rows = log_perm.shape[2] // count
    pieces = issue(
        [(held.at[:, :, pl.ds(b * rows, rows), :], blocks.at[b]) for b in range(count)], sems, 11
    )
    order_tables(value, var, noise, tables)
    advance(tile, keep, send, True)
    drain(perm_copy)
    drain(pieces)


def both_sides(tile, kept, got):
    return (
        take(tile, lambda n: kept.at[n], lambda n: kept.at[n], 4, -1),
        take(tile, lambda n: got.at[n], lambda n: got.at[n], 6, 1),
    )


def third_kernel(perm, q, columns, kept, got, keep, send, *refs):
    del columns
    tile = Tile(*refs[:9], refs[10], refs[9], lambda row: row + 4, jnp.int32(0))
    sems = refs[11]
    perm_copy = issue([(perm, tile.perm)], sems, 0)
    q_copy = issue([(q, tile.q)], sems, 1)
    fill(tile, both_sides(tile, kept, got), perm_copy, q_copy, tile.saturate(0, 1, 6))
    advance(tile, keep, send, True)


def last_kernel(chips, perm, q, index_in, weight_in, kept, got, values, *refs):
    odd, chip, end = position(chips)
    tile = Tile(*refs[:9], refs[10], refs[9], edge_q(end), end)
    index, weight, picked, sems = refs[11:]
    perm_copy = issue([(perm, tile.perm)], sems, 0)
    q_copy = issue([(q, tile.q)], sems, 1)
    tables = issue([(index_in, index), (weight_in, weight)], sems, 2)
    fill(tile, both_sides(tile, kept, got), perm_copy, q_copy)
    drain(tables)
    around = (chip + odd) & (chips - 1)
    total_rows = 8 * chips
    per = index.shape[1] // total_rows
    lanes = kept.shape[2]
    lane = lax.broadcasted_iota(jnp.int32, (1, lanes), 1)
    picked[...] = jnp.zeros_like(picked)

    def one(n, carry):
        slot = n & 7
        row = jnp.where(odd == 1, slot, 7 - slot)
        st = row + 1 + (row >= 4).astype(jnp.int32)
        other = end * (row >= 4).astype(jnp.int32)
        slot = jnp.where(other == 1, 7 - slot, slot)
        column = lax.shift_right_logical(n, 3)
        obs = column * total_rows + ((8 * around - 4 + slot) & (total_rows - 1))
        total = jnp.zeros((1, lanes), jnp.float32)
        for t in range(index.shape[0]):
            cell = index[t, obs]
            y = lax.shift_right_logical(cell, 7) & (tile.ny - 1)
            values_row = tile.p[0][st, pl.ds(PAD + y, 1), :]
            total = total + jnp.where(lane == (cell & (lanes - 1)), values_row, 0.0) * weight[t, obs]
        at = column * 32 + ((around & 3) + other) * 8 + slot
        picked[pl.ds(at, 1), :] = total
        return carry

    lax.fori_loop(0, 8 * per, one, 0, unroll=4)
    ones = jnp.ones((values.shape[0], lanes), jnp.float32)
    values[...] = lax.dot_general(
        ones, picked[...], (((1,), (1,)), ((), ())), precision=HIGH, preferred_element_type=jnp.float32
    )


def fill_sources(chips, wells, rate, q):
    odd, chip, _ = position(chips)
    ny, nz = q.shape[1], q.shape[2]
    lane = lax.broadcasted_iota(jnp.int32, (1, nz), 1)
    q[...] = jnp.zeros_like(q)

    def one(n, carry):
        cell = wells[n]
        x = lax.shift_right_logical(cell, 14)
        y = lax.shift_right_logical(cell, 7) & (ny - 1)
        behind = jnp.where(odd == 1, chip * 8 + 11 - x, x - chip * 8 + 4) & (8 * chips - 1)
        where = (jnp.minimum(behind, q.shape[0] - 1), pl.ds(y, 1), slice(None))
        here = jnp.where(behind < q.shape[0], cell & (nz - 1), -1)
        q[where] = q[where] + jnp.where(lane == here, rate[n], 0.0)
        return carry

    lax.fori_loop(0, wells.shape[0], one, 0, unroll=4)


def order_tables(value, var, noise, tables):
    groups, lanes = value.shape
    wide = lanes // groups
    half = noise.shape[0] // 2
    side = lax.broadcasted_iota(jnp.int32, (1, lanes), 1) // wide
    for g in range(groups):
        total = None
        for j in range(groups):
            where = pl.ds(j * lanes, lanes)
            parts = [noise[2 * n + c : 2 * n + c + 1, where] for c in range(2) for n in range(half)]
            parts += [value[pl.ds(j, 1), :], var[pl.ds(j, 1), :], jnp.ones((6, lanes), jnp.float32)]
            column = pltpu.roll(jnp.concatenate(parts, axis=0), (4 + wide * (j - g)) % lanes, 1)
            total = column if total is None else jnp.where(side == j, column, total)
        tables[g] = total


def solve_kernel(values, tables, columns_in, out_to, coef, columns, out, sems):
    count = columns.shape[1]
    loads = issue([(columns_in.at[:, n], columns.at[:, n]) for n in range(count)], sems, 0)

    groups = tables.shape[0]
    ens = columns.shape[0]
    half = ens // 2
    spaces = groups * 8
    parts = []
    for g in range(groups):
        sides = []
        for core in range(2):
            total = None
            for near in range(4):
                chip = (4 * g + near - core) % (4 * groups)
                row = values[pl.ds(2 * chip + core, half, stride=spaces), :]
                total = row if total is None else total + row
            sides.append(total)
        parts.append(sides)
    lanes = values.shape[1]
    near_lane = (lax.broadcasted_iota(jnp.int32, (half, lanes), 1) & 31) < 8
    ends = [values[pl.ds(at, half, stride=spaces), :] for at in (0, spaces - 1)]
    far = [pltpu.roll(end, lanes - 8, 1) for end in ends]
    for core in range(2):
        own, foreign = ends[core], far[1 - core]
        parts[0][core] = parts[0][core] - own + jnp.where(near_lane, own + foreign, 0.0)
    parts = [jnp.concatenate(sides, axis=0) for sides in parts]
    small = jnp.zeros((ens, ens), jnp.float32)
    right = jnp.zeros((ens, ens), jnp.float32)
    dims = (((1,), (1,)), ((), ()))
    for g in range(groups):
        predicted = parts[g]
        dev = predicted - jnp.mean(predicted, axis=0, keepdims=True)
        spread = INFLATION * tables[g, ens + 1 : ens + 2, :]
        resid = tables[g, ens : ens + 1, :] + jnp.sqrt(spread) * tables[g, 0:ens, :] - predicted
        scaled = dev / spread
        small = small + lax.dot_general(
            scaled, dev, dims, precision=HIGH, preferred_element_type=jnp.float32
        )
        right = right + lax.dot_general(
            scaled, resid, dims, precision=HIGH, preferred_element_type=jnp.float32
        )
    row = lax.broadcasted_iota(jnp.int32, (ens, ens), 0)
    col = lax.broadcasted_iota(jnp.int32, (ens, ens), 1)
    left = small + jnp.where(row == col, ens - 1.0, 0.0)
    for k in range(ens):
        pivot = left[k : k + 1, k : k + 1]
        left_row = left[k : k + 1, :] / pivot
        right_row = right[k : k + 1, :] / pivot
        factor = left[:, k : k + 1]
        here = row == k
        left = jnp.where(here, left_row, left - factor * left_row)
        right = jnp.where(here, right_row, right - factor * right_row)
    mixing = right - jnp.mean(right, axis=0, keepdims=True) + jnp.where(row == col, 1.0, 0.0)
    rows, wide = columns.shape[2], columns.shape[3]

    def natural(place):
        return 2 * place if place < half else 2 * (place - half) + 1

    for j in range(ens):
        for m in range(ens):
            at = natural(j) * ens + natural(m)
            coef[at] = jnp.broadcast_to(mixing[j : j + 1, m : m + 1], (8, wide))

    stores = []
    for n in range(count):
        loads[n].wait()
        part = [columns[j, n] for j in range(ens)]
        for m in range(ens):
            for r0 in range(0, rows, 8):
                total = coef[m] * part[0][r0 : r0 + 8]
                for j in range(1, ens):
                    total = total + coef[j * ens + m] * part[j][r0 : r0 + 8]
                out[m, n, r0 : r0 + 8, :] = total
        stores += issue([(out.at[:, n], out_to.at[:, n])], sems, count + n)
    drain(stores)


def body(
    log_perm,
    saturation,
    pressure_init,
    wells,
    well_rate,
    obs_index,
    obs_weight,
    obs_value,
    obs_var,
    noise,
):
    members, width, ny, nz = log_perm.shape
    spaces = lax.axis_size("space")
    mems = lax.axis_size("mem")
    odd = lax.axis_index("space") % 2
    chips = spaces // 2
    devices = mems * spaces
    ens = members * mems
    grid = (ny, nz)
    f32 = jnp.float32

    def part(field, start, size):
        return lax.dynamic_slice_in_dim(field, start, size, axis=0)

    def plane(count):
        return pltpu.VMEM((count,) + grid, f32)

    def call(kernel, name, **more):
        return pl.pallas_call(
            functools.partial(kernel, chips) if kernel is not third_kernel else kernel,
            name=name,
            **more,
        )

    grant = pltpu.CompilerParams(vmem_limit_bytes=GRANT)
    other = part(log_perm, 1 - odd, 1)[0]
    swap_out = jnp.concatenate([other, saturation, pressure_init])
    swapped = lax.ppermute(swap_out, "space", [(i, i ^ 1) for i in range(spaces)])
    edge_out = jnp.concatenate([other, part(saturation, odd * 2, 2), part(pressure_init, odd, 3)])
    ends = spaces - 1
    edge_in = lax.ppermute(
        edge_out,
        "space",
        [(0, 0), (ends, ends)] + [(i, i + 1 if i % 2 else i - 1) for i in range(1, ends)],
    )
    sems = pltpu.SemaphoreType.DMA((16,))
    scratch = tile_scratch(ny, nz) + [plane(8)]
    keep, send, perm_tile, q = call(
        first_kernel,
        "first",
        out_shape=(
            plane(PLANES),
            plane(8),
            pltpu.HBM((8,) + grid, f32),
            pltpu.HBM((12,) + grid, f32),
        ),
        in_specs=[SMEM] * 2 + [FAR] * 3 + [VMEM],
        out_specs=(VMEM, VMEM, FAR, FAR),
        scratch_shapes=scratch + [plane(4), sems],
        compiler_params=pltpu.CompilerParams(vmem_limit_bytes=GRANT + 1_400_000),
    )(wells, well_rate, log_perm, saturation, pressure_init, near(swapped))
    onward = [(i, i + 2) for i in range(0, ends - 1, 2)] + [(ends - 1, ends)]
    onward += [(i, i - 2) for i in range(3, spaces, 2)] + [(1, 0)]
    back = [(b, a) for a, b in onward]
    got = lax.ppermute(send, "space", onward)
    small = (obs_value.reshape(4, nz), obs_var.reshape(4, nz), noise)
    keep, send, perm_edge, blocks, tables = call(
        second_kernel,
        "second",
        out_shape=(
            plane(PLANES),
            plane(PLANES),
            pltpu.HBM((8,) + grid, f32),
            pltpu.HBM((mems, members, width, ny // mems, nz), f32),
            jax.ShapeDtypeStruct((4, 16, nz), f32),
        ),
        in_specs=[FAR] * 7 + [VMEM] * 2,
        out_specs=(VMEM, VMEM, FAR, FAR, VMEM),
        scratch_shapes=scratch
        + [plane(9), pltpu.VMEM(log_perm.shape, f32)]
        + [pltpu.VMEM(table.shape, f32) for table in small]
        + [sems],
        compiler_params=grant,
    )(perm_tile, edge_in, q, log_perm, *small, near(keep), near(got))
    got = lax.ppermute(send, "space", back)
    columns = lax.all_to_all(blocks, "mem", 0, 0, tiled=True).reshape(ens, width, ny // mems, nz)
    keep, send = call(
        third_kernel,
        "third",
        out_shape=(plane(PLANES), plane(PLANES)),
        in_specs=[FAR] * 3 + [VMEM] * 2,
        out_specs=(VMEM,) * 2,
        scratch_shapes=scratch + [sems],
        compiler_params=grant,
    )(perm_tile, q, columns, near(keep), near(got))
    got = lax.ppermute(send, "space", onward)
    taps = obs_index.T.shape
    values = call(
        last_kernel,
        "last",
        out_shape=pltpu.HBM((devices, nz), f32),
        in_specs=[FAR] * 4 + [VMEM] * 2,
        out_specs=VMEM,
        scratch_shapes=scratch
        + [pltpu.SMEM(taps, jnp.int32), pltpu.SMEM(taps, f32), pltpu.VMEM((nz, nz), f32), sems],
        compiler_params=grant,
    )(perm_edge, q, obs_index.T, obs_weight.T, near(keep), near(got))
    values = lax.all_to_all(
        values.reshape(devices, 1, nz), ("mem", "space"), 0, 0, tiled=True
    ).reshape(devices, nz)
    return pl.pallas_call(
        solve_kernel,
        out_shape=jax.ShapeDtypeStruct(columns.shape, f32),
        in_specs=[VMEM, VMEM, FAR],
        out_specs=FAR,
        scratch_shapes=[pltpu.VMEM((ens**2, 8, nz), f32)]
        + [pltpu.VMEM(columns.shape, f32) for _ in range(2)]
        + [sems],
        name="solve",
    )(values, tables, columns)


def solution(mesh):
    placed = (
        P("mem", "space", None, None),
        P("space", None, None),
        P("space", None, None),
        P(),
        P(),
        P(),
        P(),
        P(),
        P(),
        P(),
    )
    return jax.shard_map(
        body, mesh=mesh, in_specs=placed, out_specs=P(None, "space", "mem", None), check_vma=False
    )
```

```python
import functools

import jax
import jax.numpy as jnp
from jax import lax
from jax.experimental import pallas as pl
from jax.experimental.pallas import tpu as pltpu
from jax.sharding import PartitionSpec as P


INFLATION = 4.0
STEP = 0.1
PAD = 8
CHUNK = 32
HIGH = lax.Precision.HIGHEST
FAR = pl.BlockSpec(memory_space=pltpu.HBM)
SMEM = pl.BlockSpec(memory_space=pltpu.SMEM)
VMEM = pl.BlockSpec(memory_space=pltpu.VMEM)

S0, P0, S1, P1, S2, L2 = (0, 1), (2, 3, 4), (5, 6, 7), (8, 9, 10), 11, 12
PLANES = 13
GRANT = 56 << 20


def spot(row):
    return row + 1 + (row >= 4)


class Tile:
    def __init__(self, lam_a, lam_b, frac_a, frac_b, p_a, p_b, s_a, s_b, sides, steps, perm, q, q_row, cut):
        self.lam = (lam_a, lam_b)
        self.frac = (frac_a, frac_b)
        self.p = (p_a, p_b)
        self.s = (s_a, s_b)
        self.sides = sides
        self.steps = steps
        self.perm = perm
        self.q = q
        self.q_row = q_row
        self.ny = perm.shape[1]
        self.cut = cut

    def clear(self):
        for ref in self.lam + self.frac + self.p:
            tall, wide = ref.shape[1:]
            edge = jnp.zeros((PAD, wide), jnp.float32)
            for r in range(ref.shape[0]):
                ref[r, 0:PAD, :] = edge
                ref[r, tall - PAD : tall, :] = edge
            ref[5, :, :] = jnp.zeros((tall, wide), jnp.float32)

    def places(self, row):
        st = row + 1 + (row >= 4).astype(jnp.int32)
        joined = 1 - self.cut
        up = st + 1 + jnp.where(row == 3, joined, 0)
        down = st - 1 - jnp.where(row == 4, joined, 0)
        return st, up, down

    def rows(self, first, last, fn):
        def one(row, carry):
            for y0 in range(0, self.ny, CHUNK):
                fn(row, *self.places(row), y0)
            return carry

        lax.fori_loop(first, last + 1, one, 0)

    def run(self, phases, primed=False, then=None):
        def all_of(row, slot, which):
            for y0 in range(0, self.ny, CHUNK):
                which(row, *self.places(row), y0, slot)

        if not primed:
            all_of(jnp.int32(phases[0][0]), 0, phases[0][2])
        for phase, follower in zip(phases, phases[1:] + [then]):
            first, last, ahead, fn = phase

            def two(n, carry, first=first, ahead=ahead, fn=fn):
                row = first + 2 * n
                all_of(row + 1, 1, ahead)
                all_of(row, 0, fn)
                all_of(row + 2, 0, ahead)
                all_of(row + 1, 1, fn)
                return carry

            lax.fori_loop(0, (last - first) // 2, two, 0)
            all_of(jnp.int32(last), 1, ahead)
            all_of(jnp.int32(last - 1), 0, fn)
            if follower is not None:
                all_of(jnp.int32(follower[0]), 0, follower[2])
            all_of(jnp.int32(last), 1, fn)

    def props(self, level, first, last):
        def fn(row, st, up, down, y0):
            inner = pl.ds(y0, CHUNK)
            sat = self.s[level][st, inner, :]
            lam, frac = props(self.perm[row, inner, :], sat)
            self.lam[level][st, pl.ds(PAD + y0, CHUNK), :] = lam
            self.frac[level][st, pl.ds(PAD + y0, CHUNK), :] = frac

        self.rows(first, last, fn)

    def saturate(self, level, first, last):
        lam_r, frac_r, p_r = self.lam[level], self.frac[level], self.p[level]
        new = 1 - level
        lanes = lam_r.shape[2]
        lane = lax.broadcasted_iota(jnp.int32, (CHUNK, lanes), 1)
        is_first, is_last = lane == 0, lane == lanes - 1

        def ahead(row, st, up, down, y0, slot):
            inner = pl.ds(PAD + y0, CHUNK)
            lam, frac, press = lam_r[st, inner, :], frac_r[st, inner, :], p_r[st, inner, :]
            flux = (lam + pltpu.roll(lam, lanes - 1, 1)) * (press - pltpu.roll(press, lanes - 1, 1))
            moved = flux * jnp.where(flux > 0.0, frac, pltpu.roll(frac, lanes - 1, 1))
            edge = jnp.maximum(lam * press, 0.0) * frac
            out = jnp.where(is_last, edge, moved)
            out = out + jnp.where(is_first, edge, pltpu.roll(-moved, 1, 1))
            self.sides[2 * slot, pl.ds(y0, CHUNK), :] = out
            low = 0 if y0 == 0 else PAD + y0
            here = pl.ds(low, PAD + y0 + CHUNK - low)
            after = pl.ds(low + 1, PAD + y0 + CHUNK - low)
            flux = (lam_r[st, here, :] + lam_r[st, after, :]) * (p_r[st, here, :] - p_r[st, after, :])
            self.steps[slot, here, :] = flux * jnp.where(
                flux > 0.0, frac_r[st, here, :], frac_r[st, after, :]
            )

        def fn(row, st, up, down, y0, slot):
            inner = pl.ds(PAD + y0, CHUNK)
            lam, frac, press = lam_r[st, inner, :], frac_r[st, inner, :], p_r[st, inner, :]

            def face(index, where):
                flux = (lam + lam_r[index, where, :]) * (press - p_r[index, where, :])
                return flux * jnp.where(flux > 0.0, frac, frac_r[index, where, :])

            out = face(up, inner) + face(down, inner)
            out = out + self.steps[slot, inner, :] - self.steps[slot, pl.ds(PAD + y0 - 1, CHUNK), :]
            out = out + self.sides[2 * slot, pl.ds(y0, CHUNK), :]
            q = self.q[self.q_row(row), pl.ds(y0, CHUNK), :]
            water = q * jnp.where(q > 0.0, 1.0, frac)
            sat = self.s[level][st, pl.ds(y0, CHUNK), :]
            sat = jnp.clip(sat + STEP * (water - out), 0.0, 1.0)
            self.s[new][st, pl.ds(y0, CHUNK), :] = sat
            lam, frac = props(self.perm[row, pl.ds(y0, CHUNK), :], sat)
            self.lam[new][st, inner, :] = lam
            self.frac[new][st, inner, :] = frac

        return first, last, ahead, fn

    def pressure(self, level, first, last):
        new = 1 - level
        lam_r, p_r, out_r = self.lam[new], self.p[level], self.p[new]
        lanes = lam_r.shape[2]
        lane = lax.broadcasted_iota(jnp.int32, (CHUNK, lanes), 1)
        not_first, not_last = lane > 0, lane < lanes - 1

        def ahead(row, st, up, down, y0, slot):
            inner = pl.ds(PAD + y0, CHUNK)
            lam, press = lam_r[st, inner, :], p_r[st, inner, :]
            numer, denom = 0.0, 0.0
            for shift, mask in ((lanes - 1, not_last), (1, not_first)):
                trans = lam + jnp.where(mask, pltpu.roll(lam, shift, 1), 0.0)
                numer = numer + trans * jnp.where(mask, pltpu.roll(press, shift, 1), 0.0)
                denom = denom + trans
            self.sides[2 * slot, pl.ds(y0, CHUNK), :] = numer
            self.sides[2 * slot + 1, pl.ds(y0, CHUNK), :] = denom

        def fn(row, st, up, down, y0, slot):
            inner = pl.ds(PAD + y0, CHUNK)
            lam, press = lam_r[st, inner, :], p_r[st, inner, :]
            numer = press + self.q[self.q_row(row), pl.ds(y0, CHUNK), :]
            numer = numer + self.sides[2 * slot, pl.ds(y0, CHUNK), :]
            denom = 1.0 + self.sides[2 * slot + 1, pl.ds(y0, CHUNK), :]
            for index, where in (
                (up, inner),
                (down, inner),
                (st, pl.ds(PAD + y0 + 1, CHUNK)),
                (st, pl.ds(PAD + y0 - 1, CHUNK)),
            ):
                trans = lam + lam_r[index, where, :]
                numer = numer + trans * p_r[index, where, :]
                denom = denom + trans
            out_r[st, inner, :] = numer / denom

        return first, last, ahead, fn


def props(perm_half, sat):
    water = sat * sat
    oil = (1.0 - sat) * (1.0 - sat) * 0.25
    total = water + oil
    return perm_half * total, water / total


def near(array):
    return pltpu.with_memory_space_constraint(array, pltpu.VMEM)


def tile_scratch(ny, nz):
    tall = ny + 2 * PAD
    wide = [pltpu.VMEM((11, tall, nz), jnp.float32) for _ in range(6)]
    flat = [pltpu.VMEM((count, ny, nz), jnp.float32) for count in (11, 11, 4, 12)]
    flat.insert(3, pltpu.VMEM((2, ny + PAD, nz), jnp.float32))
    return wide + flat


def issue(pairs, sems, first):
    copies = []
    for n, (src, dst) in enumerate(pairs):
        copy = pltpu.make_async_copy(src, dst, sems.at[first + n])
        copy.start()
        copies.append(copy)
    return copies


def drain(copies):
    for copy in copies:
        copy.wait()


def move(pairs):
    tall = min(src.shape[0] for src, _ in pairs)

    def one(n, carry):
        where = pl.ds(pl.multiple_of(n * CHUNK, CHUNK), CHUNK)
        for src, dst in pairs:
            dst[where, :] = src[where, :]
        return carry

    lax.fori_loop(0, tall // CHUNK, one, 0)


def position(chips):
    place = lax.axis_index("space")
    odd, chip = place & 1, lax.shift_right_logical(place, 1)
    end = jnp.where(odd == 1, chips - 1, 0)
    return odd, chip, (chip == end).astype(jnp.int32)


def beyond(tile, row):
    return jnp.where(tile.cut == 1, 5, spot(row))


def give_early(tile, keep, send, send_early):
    pairs = []
    inner = pl.ds(PAD, tile.ny)
    sides = [(keep, lambda d: d)] + ([(send, lambda d: 7 - d)] if send_early else [])
    for out, row in sides:
        for d in range(2):
            pairs.append((tile.s[0].at[spot(row(d))], out.at[S0[d]]))
        for d in range(3):
            pairs.append((tile.p[0].at[spot(row(d)), inner], out.at[P0[d]]))
    return pairs


def give_late(tile, out, near, base):
    row, step = near
    inner = pl.ds(PAD, tile.ny)
    pairs = []
    for n, d in enumerate((1, 2, 3)):
        pairs.append((tile.s[1].at[spot(row + step * d)], out.at[S1[n] - base]))
    for n, d in enumerate((2, 3, 4)):
        st = beyond(tile, row + step * d) if d == 4 else spot(row + step * d)
        pairs.append((tile.p[1].at[st, inner], out.at[P1[n] - base]))
    return pairs


def give_last(tile, out, near, base):
    row, step = near
    inner = pl.ds(PAD, tile.ny)
    return [
        (tile.s[0].at[spot(row + step * 3)], out.at[S2 - base]),
        (tile.lam[0].at[beyond(tile, row + step * 4), inner], out.at[L2 - base]),
    ]


def take(tile, early, late, base_row, step):
    inner = pl.ds(PAD, tile.ny)
    start, s_next, p_next, last = [], [], [], []
    for d in range(2):
        start.append((early(S0[d]), tile.s[0].at[base_row + step * d]))
    for d in range(3):
        start.append((early(P0[d]), tile.p[0].at[base_row + step * d, inner]))
    for n, d in enumerate((1, 2, 3)):
        s_next.append((late(S1[n]), tile.s[1].at[base_row + step * d]))
    for n, d in enumerate((2, 3, 4)):
        p_next.append((late(P1[n]), tile.p[1].at[base_row + step * d, inner]))
    last.append((late(S2), tile.s[0].at[base_row + step * 3]))
    last.append((late(L2), tile.lam[0].at[base_row + step * 4, inner]))
    return start, s_next, p_next, last


def advance(tile, keep, send, send_early, primed=True):
    base = 0 if send_early else S1[0]
    move(give_early(tile, keep, send, send_early))
    tile.run([tile.saturate(0, 1, 6), tile.pressure(0, 2, 5), tile.saturate(1, 3, 4)], primed)
    pairs = []
    for out, near_row, at in ((send, (7, -1), base), (keep, (0, 1), 0)):
        pairs += give_late(tile, out, near_row, at) + give_last(tile, out, near_row, at)
    move(pairs)


def first_kernel(chips, wells, rate, log_perm, own_sat, own_press, swapped, keep, send, perm_out, q_out, *refs):
    odd, _, _ = position(chips)
    perm, raw, sems = refs[11:]
    tile = Tile(*refs[:10], perm, refs[10], lambda row: row + 4, jnp.int32(0))
    inner = pl.ds(PAD, tile.ny)

    def place(n):
        return jnp.where(odd == 1, 3 - n, n)

    pairs = [(log_perm.at[odd], raw)]
    for n in range(4):
        pairs.append((own_sat.at[place(n)], tile.s[0].at[spot(n)]))
        pairs.append((own_press.at[place(n)], tile.p[0].at[spot(n), inner]))
    copies = issue(pairs, sems, 0)
    tile.clear()
    fill_sources(chips, wells, rate, tile.q)
    out_copies = issue([(tile.q, q_out)], sems, 9)
    pairs = []
    for n in range(4):
        pairs.append((swapped.at[4 + place(n)], tile.s[0].at[spot(4 + n)]))
        pairs.append((swapped.at[8 + place(n)], tile.p[0].at[spot(4 + n), inner]))
    move(pairs)

    def halve(src, base):
        def one(n, carry):
            for y0 in range(0, tile.ny, CHUNK):
                where = pl.ds(y0, CHUNK)
                perm[base + n, where, :] = 0.5 * jnp.exp(src[place(n), where, :])
            return carry

        lax.fori_loop(0, 4, one, 0)

    halve(swapped, 4)
    drain(copies)
    halve(raw, 0)
    out_copies += issue([(perm, perm_out)], sems, 10)
    tile.props(0, 0, 7)
    advance(tile, keep, send, False, False)
    drain(out_copies)


def fill(tile, sides, perm_copy, q_copy, then=None):
    tile.clear()
    groups = [sum((side[n] for side in sides), []) for n in range(4)]
    move(groups[0] + groups[1] + groups[2])
    drain(perm_copy)
    tile.props(0, 2, 5)
    tile.props(1, 0, 2)
    tile.props(1, 5, 7)
    drain(q_copy)
    move(groups[3])
    tile.props(0, 0, 0)
    tile.props(0, 7, 7)
    tile.run(
        [
            tile.saturate(0, 3, 4),
            tile.pressure(0, 2, 5),
            tile.saturate(1, 1, 6),
            tile.pressure(1, 0, 7),
        ],
        then=then,
    )


def edge_q(cut):
    return lambda row: jnp.where((cut == 1) & (row >= 4), row, 7 - row)


def second_kernel(chips, perm_own, raw_in, q, log_perm, value_in, var_in, noise_in, kept, late_in, keep, send, perm_out, blocks, tables, *refs):
    odd, _, end = position(chips)
    perm, raw, held, value, var, noise, sems = refs[11:]
    tile = Tile(*refs[:10], perm, refs[10], edge_q(end), end)
    straight = odd ^ end

    def place(n, count):
        return jnp.where(straight == 1, n, count - 1 - n)

    def early(plane):
        if plane in S0:
            return raw.at[4 + place(plane, 2)]
        return raw.at[6 + place(plane - 2, 3)]

    copies = issue([(raw_in, raw)] + [(perm_own.at[3 - d], perm.at[d]) for d in range(4)], sems, 0)
    q_copy = issue([(q, tile.q)], sems, 5)
    load = issue([(log_perm, held), (value_in, value), (var_in, var), (noise_in, noise)], sems, 7)
    drain(copies)

    def permeability(d, carry):
        for y0 in range(0, tile.ny, CHUNK):
            where = pl.ds(y0, CHUNK)
            perm[4 + d, where, :] = 0.5 * jnp.exp(raw[place(d, 4), where, :])
        return carry

    lax.fori_loop(0, 4, permeability, 0)
    perm_copy = issue([(perm, perm_out)], sems, 6)
    sides = (
        take(tile, lambda n: kept.at[n], lambda n: kept.at[n], 4, -1),
        take(tile, early, lambda n: late_in.at[n - S1[0]], 6, 1),
    )
    fill(tile, sides, [], q_copy, tile.saturate(0, 1, 6))
    drain(load)
    count = blocks.shape[0]
    rows = log_perm.shape[2] // count
    pieces = issue(
        [(held.at[:, :, pl.ds(b * rows, rows), :], blocks.at[b]) for b in range(count)], sems, 11
    )
    order_tables(value, var, noise, tables)
    advance(tile, keep, send, True)
    drain(perm_copy)
    drain(pieces)


def both_sides(tile, kept, got):
    return (
        take(tile, lambda n: kept.at[n], lambda n: kept.at[n], 4, -1),
        take(tile, lambda n: got.at[n], lambda n: got.at[n], 6, 1),
    )


def third_kernel(perm, q, columns, kept, got, keep, send, *refs):
    del columns
    tile = Tile(*refs[:10], refs[11], refs[10], lambda row: row + 4, jnp.int32(0))
    sems = refs[12]
    perm_copy = issue([(perm, tile.perm)], sems, 0)
    q_copy = issue([(q, tile.q)], sems, 1)
    fill(tile, both_sides(tile, kept, got), perm_copy, q_copy, tile.saturate(0, 1, 6))
    advance(tile, keep, send, True)


def last_kernel(chips, perm, q, index_in, weight_in, kept, got, values, *refs):
    odd, chip, end = position(chips)
    tile = Tile(*refs[:10], refs[11], refs[10], edge_q(end), end)
    index, weight, picked, sems = refs[12:]
    perm_copy = issue([(perm, tile.perm)], sems, 0)
    q_copy = issue([(q, tile.q)], sems, 1)
    tables = issue([(index_in, index), (weight_in, weight)], sems, 2)
    fill(tile, both_sides(tile, kept, got), perm_copy, q_copy)
    drain(tables)
    around = (chip + odd) & (chips - 1)
    total_rows = 8 * chips
    per = index.shape[1] // total_rows
    lanes = kept.shape[2]
    lane = lax.broadcasted_iota(jnp.int32, (1, lanes), 1)
    picked[...] = jnp.zeros_like(picked)

    def one(n, carry):
        slot = n & 7
        row = jnp.where(odd == 1, slot, 7 - slot)
        st = row + 1 + (row >= 4).astype(jnp.int32)
        other = end * (row >= 4).astype(jnp.int32)
        slot = jnp.where(other == 1, 7 - slot, slot)
        column = lax.shift_right_logical(n, 3)
        obs = column * total_rows + ((8 * around - 4 + slot) & (total_rows - 1))
        total = jnp.zeros((1, lanes), jnp.float32)
        for t in range(index.shape[0]):
            cell = index[t, obs]
            y = lax.shift_right_logical(cell, 7) & (tile.ny - 1)
            values_row = tile.p[0][st, pl.ds(PAD + y, 1), :]
            total = total + jnp.where(lane == (cell & (lanes - 1)), values_row, 0.0) * weight[t, obs]
        at = column * 32 + ((around & 3) + other) * 8 + slot
        picked[pl.ds(at, 1), :] = total
        return carry

    lax.fori_loop(0, 8 * per, one, 0, unroll=4)
    ones = jnp.ones((values.shape[0], lanes), jnp.float32)
    values[...] = lax.dot_general(
        ones, picked[...], (((1,), (1,)), ((), ())), precision=HIGH, preferred_element_type=jnp.float32
    )


def fill_sources(chips, wells, rate, q):
    odd, chip, _ = position(chips)
    ny, nz = q.shape[1], q.shape[2]
    lane = lax.broadcasted_iota(jnp.int32, (1, nz), 1)
    q[...] = jnp.zeros_like(q)

    def one(n, carry):
        cell = wells[n]
        x = lax.shift_right_logical(cell, 14)
        y = lax.shift_right_logical(cell, 7) & (ny - 1)
        behind = jnp.where(odd == 1, chip * 8 + 11 - x, x - chip * 8 + 4) & (8 * chips - 1)
        where = (jnp.minimum(behind, q.shape[0] - 1), pl.ds(y, 1), slice(None))
        here = jnp.where(behind < q.shape[0], cell & (nz - 1), -1)
        q[where] = q[where] + jnp.where(lane == here, rate[n], 0.0)
        return carry

    lax.fori_loop(0, wells.shape[0], one, 0, unroll=4)


def order_tables(value, var, noise, tables):
    groups, lanes = value.shape
    wide = lanes // groups
    half = noise.shape[0] // 2
    side = lax.broadcasted_iota(jnp.int32, (1, lanes), 1) // wide
    for g in range(groups):
        total = None
        for j in range(groups):
            where = pl.ds(j * lanes, lanes)
            parts = [noise[2 * n + c : 2 * n + c + 1, where] for c in range(2) for n in range(half)]
            parts += [value[pl.ds(j, 1), :], var[pl.ds(j, 1), :], jnp.ones((6, lanes), jnp.float32)]
            column = pltpu.roll(jnp.concatenate(parts, axis=0), (4 + wide * (j - g)) % lanes, 1)
            total = column if total is None else jnp.where(side == j, column, total)
        tables[g] = total


def solve_kernel(values, tables, columns_in, out_to, coef, columns, out, sems):
    count = columns.shape[1]
    loads = issue([(columns_in.at[:, n], columns.at[:, n]) for n in range(count)], sems, 0)

    groups = tables.shape[0]
    ens = columns.shape[0]
    half = ens // 2
    spaces = groups * 8
    parts = []
    for g in range(groups):
        sides = []
        for core in range(2):
            total = None
            for near in range(4):
                chip = (4 * g + near - core) % (4 * groups)
                row = values[pl.ds(2 * chip + core, half, stride=spaces), :]
                total = row if total is None else total + row
            sides.append(total)
        parts.append(sides)
    lanes = values.shape[1]
    near_lane = (lax.broadcasted_iota(jnp.int32, (half, lanes), 1) & 31) < 8
    ends = [values[pl.ds(at, half, stride=spaces), :] for at in (0, spaces - 1)]
    far = [pltpu.roll(end, lanes - 8, 1) for end in ends]
    for core in range(2):
        own, foreign = ends[core], far[1 - core]
        parts[0][core] = parts[0][core] - own + jnp.where(near_lane, own + foreign, 0.0)
    parts = [jnp.concatenate(sides, axis=0) for sides in parts]
    small = jnp.zeros((ens, ens), jnp.float32)
    right = jnp.zeros((ens, ens), jnp.float32)
    dims = (((1,), (1,)), ((), ()))
    for g in range(groups):
        predicted = parts[g]
        dev = predicted - jnp.mean(predicted, axis=0, keepdims=True)
        spread = INFLATION * tables[g, ens + 1 : ens + 2, :]
        resid = tables[g, ens : ens + 1, :] + jnp.sqrt(spread) * tables[g, 0:ens, :] - predicted
        scaled = dev / spread
        small = small + lax.dot_general(
            scaled, dev, dims, precision=HIGH, preferred_element_type=jnp.float32
        )
        right = right + lax.dot_general(
            scaled, resid, dims, precision=HIGH, preferred_element_type=jnp.float32
        )
    row = lax.broadcasted_iota(jnp.int32, (ens, ens), 0)
    col = lax.broadcasted_iota(jnp.int32, (ens, ens), 1)
    left = small + jnp.where(row == col, ens - 1.0, 0.0)
    for k in range(ens):
        pivot = left[k : k + 1, k : k + 1]
        left_row = left[k : k + 1, :] / pivot
        right_row = right[k : k + 1, :] / pivot
        factor = left[:, k : k + 1]
        here = row == k
        left = jnp.where(here, left_row, left - factor * left_row)
        right = jnp.where(here, right_row, right - factor * right_row)
    mixing = right - jnp.mean(right, axis=0, keepdims=True) + jnp.where(row == col, 1.0, 0.0)
    rows, wide = columns.shape[2], columns.shape[3]

    def natural(place):
        return 2 * place if place < half else 2 * (place - half) + 1

    for j in range(ens):
        for m in range(ens):
            at = natural(j) * ens + natural(m)
            coef[at] = jnp.broadcast_to(mixing[j : j + 1, m : m + 1], (8, wide))

    stores = []
    for n in range(count):
        loads[n].wait()
        part = [columns[j, n] for j in range(ens)]
        for m in range(ens):
            for r0 in range(0, rows, 8):
                total = coef[m] * part[0][r0 : r0 + 8]
                for j in range(1, ens):
                    total = total + coef[j * ens + m] * part[j][r0 : r0 + 8]
                out[m, n, r0 : r0 + 8, :] = total
        stores += issue([(out.at[:, n], out_to.at[:, n])], sems, count + n)
    drain(stores)


def body(
    log_perm,
    saturation,
    pressure_init,
    wells,
    well_rate,
    obs_index,
    obs_weight,
    obs_value,
    obs_var,
    noise,
):
    members, width, ny, nz = log_perm.shape
    spaces = lax.axis_size("space")
    mems = lax.axis_size("mem")
    odd = lax.axis_index("space") % 2
    chips = spaces // 2
    devices = mems * spaces
    ens = members * mems
    grid = (ny, nz)
    f32 = jnp.float32

    def part(field, start, size):
        return lax.dynamic_slice_in_dim(field, start, size, axis=0)

    def plane(count):
        return pltpu.VMEM((count,) + grid, f32)

    def call(kernel, name, **more):
        return pl.pallas_call(
            functools.partial(kernel, chips) if kernel is not third_kernel else kernel,
            name=name,
            **more,
        )

    grant = pltpu.CompilerParams(vmem_limit_bytes=GRANT)
    other = part(log_perm, 1 - odd, 1)[0]
    swap_out = jnp.concatenate([other, saturation, pressure_init])
    swapped = lax.ppermute(swap_out, "space", [(i, i ^ 1) for i in range(spaces)])
    edge_out = jnp.concatenate([other, part(saturation, odd * 2, 2), part(pressure_init, odd, 3)])
    ends = spaces - 1
    edge_in = lax.ppermute(
        edge_out,
        "space",
        [(0, 0), (ends, ends)] + [(i, i + 1 if i % 2 else i - 1) for i in range(1, ends)],
    )
    sems = pltpu.SemaphoreType.DMA((16,))
    scratch = tile_scratch(ny, nz) + [plane(8)]
    keep, send, perm_tile, q = call(
        first_kernel,
        "first",
        out_shape=(
            plane(PLANES),
            plane(8),
            pltpu.HBM((8,) + grid, f32),
            pltpu.HBM((12,) + grid, f32),
        ),
        in_specs=[SMEM] * 2 + [FAR] * 3 + [VMEM],
        out_specs=(VMEM, VMEM, FAR, FAR),
        scratch_shapes=scratch + [plane(4), sems],
        compiler_params=pltpu.CompilerParams(vmem_limit_bytes=GRANT + 1_400_000),
    )(wells, well_rate, log_perm, saturation, pressure_init, near(swapped))
    onward = [(i, i + 2) for i in range(0, ends - 1, 2)] + [(ends - 1, ends)]
    onward += [(i, i - 2) for i in range(3, spaces, 2)] + [(1, 0)]
    back = [(b, a) for a, b in onward]
    got = lax.ppermute(send, "space", onward)
    small = (obs_value.reshape(4, nz), obs_var.reshape(4, nz), noise)
    keep, send, perm_edge, blocks, tables = call(
        second_kernel,
        "second",
        out_shape=(
            plane(PLANES),
            plane(PLANES),
            pltpu.HBM((8,) + grid, f32),
            pltpu.HBM((mems, members, width, ny // mems, nz), f32),
            jax.ShapeDtypeStruct((4, 16, nz), f32),
        ),
        in_specs=[FAR] * 7 + [VMEM] * 2,
        out_specs=(VMEM, VMEM, FAR, FAR, VMEM),
        scratch_shapes=scratch
        + [plane(9), pltpu.VMEM(log_perm.shape, f32)]
        + [pltpu.VMEM(table.shape, f32) for table in small]
        + [sems],
        compiler_params=grant,
    )(perm_tile, edge_in, q, log_perm, *small, near(keep), near(got))
    got = lax.ppermute(send, "space", back)
    columns = lax.all_to_all(blocks, "mem", 0, 0, tiled=True).reshape(ens, width, ny // mems, nz)
    keep, send = call(
        third_kernel,
        "third",
        out_shape=(plane(PLANES), plane(PLANES)),
        in_specs=[FAR] * 3 + [VMEM] * 2,
        out_specs=(VMEM,) * 2,
        scratch_shapes=scratch + [sems],
        compiler_params=grant,
    )(perm_tile, q, columns, near(keep), near(got))
    got = lax.ppermute(send, "space", onward)
    taps = obs_index.T.shape
    values = call(
        last_kernel,
        "last",
        out_shape=pltpu.HBM((devices, nz), f32),
        in_specs=[FAR] * 4 + [VMEM] * 2,
        out_specs=VMEM,
        scratch_shapes=scratch
        + [pltpu.SMEM(taps, jnp.int32), pltpu.SMEM(taps, f32), pltpu.VMEM((nz, nz), f32), sems],
        compiler_params=grant,
    )(perm_edge, q, obs_index.T, obs_weight.T, near(keep), near(got))
    values = lax.all_to_all(
        values.reshape(devices, 1, nz), ("mem", "space"), 0, 0, tiled=True
    ).reshape(devices, nz)
    return pl.pallas_call(
        solve_kernel,
        out_shape=jax.ShapeDtypeStruct(columns.shape, f32),
        in_specs=[VMEM, VMEM, FAR],
        out_specs=FAR,
        scratch_shapes=[pltpu.VMEM((ens**2, 8, nz), f32)]
        + [pltpu.VMEM(columns.shape, f32) for _ in range(2)]
        + [sems],
        name="solve",
    )(near(values), near(tables), columns)


def solution(mesh):
    placed = (
        P("mem", "space", None, None),
        P("space", None, None),
        P("space", None, None),
        P(),
        P(),
        P(),
        P(),
        P(),
        P(),
        P(),
    )
    return jax.shard_map(
        body, mesh=mesh, in_specs=placed, out_specs=P(None, "space", "mem", None), check_vma=False
    )
```

```python
import functools

import jax
import jax.numpy as jnp
from jax import lax
from jax.experimental import pallas as pl
from jax.experimental.pallas import tpu as pltpu
from jax.sharding import PartitionSpec as P


INFLATION = 4.0
STEP = 0.1
PAD = 8
CHUNK = 32
HALF = 16
HIGH = lax.Precision.HIGHEST
FAR = pl.BlockSpec(memory_space=pltpu.HBM)
SMEM = pl.BlockSpec(memory_space=pltpu.SMEM)
VMEM = pl.BlockSpec(memory_space=pltpu.VMEM)

S0, P0, S1, P1, S2, L2 = (0, 1), (2, 3, 4), (5, 6, 7), (8, 9, 10), 11, 12
PLANES = 13
GRANT = 56 << 20


def spot(row):
    return row + 1 + (row >= 4)


class Tile:
    def __init__(self, lam_a, lam_b, frac_a, frac_b, p_a, p_b, s_a, s_b, sides, steps, perm, q, q_row, cut):
        self.lam = (lam_a, lam_b)
        self.frac = (frac_a, frac_b)
        self.p = (p_a, p_b)
        self.s = (s_a, s_b)
        self.sides = sides
        self.steps = steps
        self.perm = perm
        self.q = q
        self.q_row = q_row
        self.ny = perm.shape[1]
        self.cut = cut

    def clear(self):
        for ref in self.lam + self.frac + self.p:
            tall, wide = ref.shape[1:]
            edge = jnp.zeros((PAD, wide), jnp.float32)
            for r in range(ref.shape[0]):
                ref[r, 0:PAD, :] = edge
                ref[r, tall - PAD : tall, :] = edge
            ref[5, :, :] = jnp.zeros((tall, wide), jnp.float32)

    def places(self, row):
        st = row + 1 + (row >= 4).astype(jnp.int32)
        joined = 1 - self.cut
        up = st + 1 + jnp.where(row == 3, joined, 0)
        down = st - 1 - jnp.where(row == 4, joined, 0)
        return st, up, down

    def rows(self, first, last, fn):
        def one(row, carry):
            for y0 in range(0, self.ny, CHUNK):
                fn(row, *self.places(row), y0)
            return carry

        lax.fori_loop(first, last + 1, one, 0)

    def run(self, phases, primed=False, then=None):
        def all_of(row, slot, which, chunk):
            for y0 in range(0, self.ny, chunk):
                which(row, *self.places(row), y0, slot)

        if not primed:
            all_of(jnp.int32(phases[0][0]), 0, phases[0][2], phases[0][4])
        for phase, follower in zip(phases, phases[1:] + [then]):
            first, last, ahead, fn, chunk = phase

            def two(n, carry, first=first, ahead=ahead, fn=fn, chunk=chunk):
                row = first + 2 * n
                all_of(row + 1, 1, ahead, chunk)
                all_of(row, 0, fn, chunk)
                all_of(row + 2, 0, ahead, chunk)
                all_of(row + 1, 1, fn, chunk)
                return carry

            lax.fori_loop(0, (last - first) // 2, two, 0)
            all_of(jnp.int32(last), 1, ahead, chunk)
            all_of(jnp.int32(last - 1), 0, fn, chunk)
            if follower is not None:
                all_of(jnp.int32(follower[0]), 0, follower[2], follower[4])
            all_of(jnp.int32(last), 1, fn, chunk)

    def props(self, level, first, last):
        def fn(row, st, up, down, y0):
            inner = pl.ds(y0, CHUNK)
            sat = self.s[level][st, inner, :]
            lam, frac = props(self.perm[row, inner, :], sat)
            self.lam[level][st, pl.ds(PAD + y0, CHUNK), :] = lam
            self.frac[level][st, pl.ds(PAD + y0, CHUNK), :] = frac

        self.rows(first, last, fn)

    def saturate(self, level, first, last):
        lam_r, frac_r, p_r = self.lam[level], self.frac[level], self.p[level]
        new = 1 - level
        lanes = lam_r.shape[2]
        lane = lax.broadcasted_iota(jnp.int32, (CHUNK, lanes), 1)
        is_first, is_last = lane == 0, lane == lanes - 1

        def ahead(row, st, up, down, y0, slot):
            inner = pl.ds(PAD + y0, CHUNK)
            lam, frac, press = lam_r[st, inner, :], frac_r[st, inner, :], p_r[st, inner, :]
            flux = (lam + pltpu.roll(lam, lanes - 1, 1)) * (press - pltpu.roll(press, lanes - 1, 1))
            moved = flux * jnp.where(flux > 0.0, frac, pltpu.roll(frac, lanes - 1, 1))
            edge = jnp.maximum(lam * press, 0.0) * frac
            out = jnp.where(is_last, edge, moved)
            out = out + jnp.where(is_first, edge, pltpu.roll(-moved, 1, 1))
            self.sides[2 * slot, pl.ds(y0, CHUNK), :] = out
            low = 0 if y0 == 0 else PAD + y0
            here = pl.ds(low, PAD + y0 + CHUNK - low)
            after = pl.ds(low + 1, PAD + y0 + CHUNK - low)
            flux = (lam_r[st, here, :] + lam_r[st, after, :]) * (p_r[st, here, :] - p_r[st, after, :])
            self.steps[slot, here, :] = flux * jnp.where(
                flux > 0.0, frac_r[st, here, :], frac_r[st, after, :]
            )

        def fn(row, st, up, down, y0, slot):
            inner = pl.ds(PAD + y0, CHUNK)
            lam, frac, press = lam_r[st, inner, :], frac_r[st, inner, :], p_r[st, inner, :]

            def face(index, where):
                flux = (lam + lam_r[index, where, :]) * (press - p_r[index, where, :])
                return flux * jnp.where(flux > 0.0, frac, frac_r[index, where, :])

            out = face(up, inner) + face(down, inner)
            out = out + self.steps[slot, inner, :] - self.steps[slot, pl.ds(PAD + y0 - 1, CHUNK), :]
            out = out + self.sides[2 * slot, pl.ds(y0, CHUNK), :]
            q = self.q[self.q_row(row), pl.ds(y0, CHUNK), :]
            water = q * jnp.where(q > 0.0, 1.0, frac)
            sat = self.s[level][st, pl.ds(y0, CHUNK), :]
            sat = jnp.clip(sat + STEP * (water - out), 0.0, 1.0)
            self.s[new][st, pl.ds(y0, CHUNK), :] = sat
            lam, frac = props(self.perm[row, pl.ds(y0, CHUNK), :], sat)
            self.lam[new][st, inner, :] = lam
            self.frac[new][st, inner, :] = frac

        return first, last, ahead, fn, CHUNK

    def pressure(self, level, first, last):
        new = 1 - level
        lam_r, p_r, out_r = self.lam[new], self.p[level], self.p[new]
        lanes = lam_r.shape[2]
        lane = lax.broadcasted_iota(jnp.int32, (HALF, lanes), 1)
        not_first, not_last = lane > 0, lane < lanes - 1

        def ahead(row, st, up, down, y0, slot):
            inner = pl.ds(PAD + y0, HALF)
            lam, press = lam_r[st, inner, :], p_r[st, inner, :]
            numer, denom = 0.0, 0.0
            for shift, mask in ((lanes - 1, not_last), (1, not_first)):
                trans = lam + jnp.where(mask, pltpu.roll(lam, shift, 1), 0.0)
                numer = numer + trans * jnp.where(mask, pltpu.roll(press, shift, 1), 0.0)
                denom = denom + trans
            self.sides[2 * slot, pl.ds(y0, HALF), :] = numer
            self.sides[2 * slot + 1, pl.ds(y0, HALF), :] = denom

        def fn(row, st, up, down, y0, slot):
            inner = pl.ds(PAD + y0, HALF)
            lam, press = lam_r[st, inner, :], p_r[st, inner, :]
            numer = press + self.q[self.q_row(row), pl.ds(y0, HALF), :]
            numer = numer + self.sides[2 * slot, pl.ds(y0, HALF), :]
            denom = 1.0 + self.sides[2 * slot + 1, pl.ds(y0, HALF), :]
            for index, where in (
                (up, inner),
                (down, inner),
                (st, pl.ds(PAD + y0 + 1, HALF)),
                (st, pl.ds(PAD + y0 - 1, HALF)),
            ):
                trans = lam + lam_r[index, where, :]
                numer = numer + trans * p_r[index, where, :]
                denom = denom + trans
            out_r[st, inner, :] = numer / denom

        return first, last, ahead, fn, HALF


def props(perm_half, sat):
    water = sat * sat
    oil = (1.0 - sat) * (1.0 - sat) * 0.25
    total = water + oil
    return perm_half * total, water / total


def near(array):
    return pltpu.with_memory_space_constraint(array, pltpu.VMEM)


def tile_scratch(ny, nz):
    tall = ny + 2 * PAD
    wide = [pltpu.VMEM((11, tall, nz), jnp.float32) for _ in range(6)]
    flat = [pltpu.VMEM((count, ny, nz), jnp.float32) for count in (11, 11, 4, 12)]
    flat.insert(3, pltpu.VMEM((2, ny + PAD, nz), jnp.float32))
    return wide + flat


def issue(pairs, sems, first):
    copies = []
    for n, (src, dst) in enumerate(pairs):
        copy = pltpu.make_async_copy(src, dst, sems.at[first + n])
        copy.start()
        copies.append(copy)
    return copies


def drain(copies):
    for copy in copies:
        copy.wait()


def move(pairs):
    tall = min(src.shape[0] for src, _ in pairs)

    def one(n, carry):
        where = pl.ds(pl.multiple_of(n * CHUNK, CHUNK), CHUNK)
        for src, dst in pairs:
            dst[where, :] = src[where, :]
        return carry

    lax.fori_loop(0, tall // CHUNK, one, 0)


def position(chips):
    place = lax.axis_index("space")
    odd, chip = place & 1, lax.shift_right_logical(place, 1)
    end = jnp.where(odd == 1, chips - 1, 0)
    return odd, chip, (chip == end).astype(jnp.int32)


def beyond(tile, row):
    return jnp.where(tile.cut == 1, 5, spot(row))


def give_early(tile, keep, send, send_early):
    pairs = []
    inner = pl.ds(PAD, tile.ny)
    sides = [(keep, lambda d: d)] + ([(send, lambda d: 7 - d)] if send_early else [])
    for out, row in sides:
        for d in range(2):
            pairs.append((tile.s[0].at[spot(row(d))], out.at[S0[d]]))
        for d in range(3):
            pairs.append((tile.p[0].at[spot(row(d)), inner], out.at[P0[d]]))
    return pairs


def give_late(tile, out, near, base):
    row, step = near
    inner = pl.ds(PAD, tile.ny)
    pairs = []
    for n, d in enumerate((1, 2, 3)):
        pairs.append((tile.s[1].at[spot(row + step * d)], out.at[S1[n] - base]))
    for n, d in enumerate((2, 3, 4)):
        st = beyond(tile, row + step * d) if d == 4 else spot(row + step * d)
        pairs.append((tile.p[1].at[st, inner], out.at[P1[n] - base]))
    return pairs


def give_last(tile, out, near, base):
    row, step = near
    inner = pl.ds(PAD, tile.ny)
    return [
        (tile.s[0].at[spot(row + step * 3)], out.at[S2 - base]),
        (tile.lam[0].at[beyond(tile, row + step * 4), inner], out.at[L2 - base]),
    ]


def take(tile, early, late, base_row, step):
    inner = pl.ds(PAD, tile.ny)
    start, s_next, p_next, last = [], [], [], []
    for d in range(2):
        start.append((early(S0[d]), tile.s[0].at[base_row + step * d]))
    for d in range(3):
        start.append((early(P0[d]), tile.p[0].at[base_row + step * d, inner]))
    for n, d in enumerate((1, 2, 3)):
        s_next.append((late(S1[n]), tile.s[1].at[base_row + step * d]))
    for n, d in enumerate((2, 3, 4)):
        p_next.append((late(P1[n]), tile.p[1].at[base_row + step * d, inner]))
    last.append((late(S2), tile.s[0].at[base_row + step * 3]))
    last.append((late(L2), tile.lam[0].at[base_row + step * 4, inner]))
    return start, s_next, p_next, last


def advance(tile, keep, send, send_early, primed=True):
    base = 0 if send_early else S1[0]
    move(give_early(tile, keep, send, send_early))
    tile.run([tile.saturate(0, 1, 6), tile.pressure(0, 2, 5), tile.saturate(1, 3, 4)], primed)
    pairs = []
    for out, near_row, at in ((send, (7, -1), base), (keep, (0, 1), 0)):
        pairs += give_late(tile, out, near_row, at) + give_last(tile, out, near_row, at)
    move(pairs)


def first_kernel(chips, wells, rate, log_perm, own_sat, own_press, swapped, keep, send, perm_out, q_out, *refs):
    odd, _, _ = position(chips)
    perm, raw, sems = refs[11:]
    tile = Tile(*refs[:10], perm, refs[10], lambda row: row + 4, jnp.int32(0))
    inner = pl.ds(PAD, tile.ny)

    def place(n):
        return jnp.where(odd == 1, 3 - n, n)

    pairs = [(log_perm.at[odd], raw)]
    for n in range(4):
        pairs.append((own_sat.at[place(n)], tile.s[0].at[spot(n)]))
        pairs.append((own_press.at[place(n)], tile.p[0].at[spot(n), inner]))
    copies = issue(pairs, sems, 0)
    tile.clear()
    fill_sources(chips, wells, rate, tile.q)
    out_copies = issue([(tile.q, q_out)], sems, 9)
    pairs = []
    for n in range(4):
        pairs.append((swapped.at[4 + place(n)], tile.s[0].at[spot(4 + n)]))
        pairs.append((swapped.at[8 + place(n)], tile.p[0].at[spot(4 + n), inner]))
    move(pairs)

    def halve(src, base):
        def one(n, carry):
            for y0 in range(0, tile.ny, CHUNK):
                where = pl.ds(y0, CHUNK)
                perm[base + n, where, :] = 0.5 * jnp.exp(src[place(n), where, :])
            return carry

        lax.fori_loop(0, 4, one, 0)

    halve(swapped, 4)
    drain(copies)
    halve(raw, 0)
    out_copies += issue([(perm, perm_out)], sems, 10)
    tile.props(0, 0, 7)
    advance(tile, keep, send, False, False)
    drain(out_copies)


def fill(tile, sides, q_copy, then=None):
    tile.props(0, 2, 5)
    tile.props(1, 0, 2)
    tile.props(1, 5, 7)
    drain(q_copy)
    move(sides[0][3] + sides[1][3])
    tile.props(0, 0, 0)
    tile.props(0, 7, 7)
    tile.run(
        [
            tile.saturate(0, 3, 4),
            tile.pressure(0, 2, 5),
            tile.saturate(1, 1, 6),
            tile.pressure(1, 0, 7),
        ],
        then=then,
    )


def edge_q(cut):
    return lambda row: jnp.where((cut == 1) & (row >= 4), row, 7 - row)


def second_kernel(chips, perm_own, raw_in, q, log_perm, value_in, var_in, noise_in, kept, late_in, keep, send, perm_out, perm_next, blocks, tables, *refs):
    odd, _, end = position(chips)
    perm, raw, held, value, var, noise, sems = refs[11:]
    tile = Tile(*refs[:10], perm, refs[10], edge_q(end), end)
    straight = odd ^ end

    def place(n, count):
        return jnp.where(straight == 1, n, count - 1 - n)

    def early(plane):
        if plane in S0:
            return raw.at[4 + place(plane, 2)]
        return raw.at[6 + place(plane - 2, 3)]

    copies = issue([(raw_in, raw)] + [(perm_own.at[3 - d], perm.at[d]) for d in range(4)], sems, 0)
    q_copy = issue([(q, tile.q)], sems, 5)
    load = issue(
        [(log_perm, held), (value_in, value), (var_in, var), (noise_in, noise), (perm_own, perm_next)],
        sems,
        7,
    )
    sides = (
        take(tile, lambda n: kept.at[n], lambda n: kept.at[n], 4, -1),
        take(tile, early, lambda n: late_in.at[n - S1[0]], 6, 1),
    )
    tile.clear()
    move(sides[0][0] + sides[0][1] + sides[0][2] + sides[1][1] + sides[1][2])
    drain(copies)
    move(sides[1][0])

    def permeability(d, carry):
        for y0 in range(0, tile.ny, CHUNK):
            where = pl.ds(y0, CHUNK)
            perm[4 + d, where, :] = 0.5 * jnp.exp(raw[place(d, 4), where, :])
        return carry

    lax.fori_loop(0, 4, permeability, 0)
    perm_copy = issue([(perm, perm_out)], sems, 6)
    fill(tile, sides, q_copy, tile.saturate(0, 1, 6))
    drain(load)
    count = blocks.shape[0]
    rows = log_perm.shape[2] // count
    pieces = issue(
        [(held.at[:, :, pl.ds(b * rows, rows), :], blocks.at[b]) for b in range(count)], sems, 12
    )
    order_tables(value, var, noise, tables)
    advance(tile, keep, send, True)
    drain(perm_copy)
    drain(pieces)


def both_sides(tile, kept, got):
    return (
        take(tile, lambda n: kept.at[n], lambda n: kept.at[n], 4, -1),
        take(tile, lambda n: got.at[n], lambda n: got.at[n], 6, 1),
    )


def gather(tile, kept, got):
    sides = both_sides(tile, kept, got)
    tile.clear()
    move(sum((side[n] for side in sides for n in range(3)), []))
    return sides


def third_kernel(q, columns, perm_later, perm, kept, got, keep, send, perm_next, *refs):
    del columns
    tile = Tile(*refs[:10], perm, refs[10], lambda row: row + 4, jnp.int32(0))
    sems = refs[11]
    q_copy = issue([(q, tile.q)], sems, 0)
    hand_on = issue([(perm_later, perm_next)], sems, 1)
    fill(tile, gather(tile, kept, got), q_copy, tile.saturate(0, 1, 6))
    advance(tile, keep, send, True)
    drain(hand_on)


def last_kernel(chips, q, index_in, weight_in, perm, kept, got, values, *refs):
    odd, chip, end = position(chips)
    tile = Tile(*refs[:10], perm, refs[10], edge_q(end), end)
    index, weight, picked, sems = refs[11:]
    q_copy = issue([(q, tile.q)], sems, 1)
    tables = issue([(index_in, index), (weight_in, weight)], sems, 2)
    fill(tile, gather(tile, kept, got), q_copy)
    drain(tables)
    around = (chip + odd) & (chips - 1)
    total_rows = 8 * chips
    per = index.shape[1] // total_rows
    lanes = kept.shape[2]
    lane = lax.broadcasted_iota(jnp.int32, (1, lanes), 1)
    picked[...] = jnp.zeros_like(picked)

    def one(n, carry):
        slot = n & 7
        row = jnp.where(odd == 1, slot, 7 - slot)
        st = row + 1 + (row >= 4).astype(jnp.int32)
        other = end * (row >= 4).astype(jnp.int32)
        slot = jnp.where(other == 1, 7 - slot, slot)
        column = lax.shift_right_logical(n, 3)
        obs = column * total_rows + ((8 * around - 4 + slot) & (total_rows - 1))
        total = jnp.zeros((1, lanes), jnp.float32)
        for t in range(index.shape[0]):
            cell = index[t, obs]
            y = lax.shift_right_logical(cell, 7) & (tile.ny - 1)
            values_row = tile.p[0][st, pl.ds(PAD + y, 1), :]
            total = total + jnp.where(lane == (cell & (lanes - 1)), values_row, 0.0) * weight[t, obs]
        at = column * 32 + ((around & 3) + other) * 8 + slot
        picked[pl.ds(at, 1), :] = total
        return carry

    lax.fori_loop(0, 8 * per, one, 0, unroll=4)
    ones = jnp.ones((values.shape[0], lanes), jnp.float32)
    values[...] = lax.dot_general(
        ones, picked[...], (((1,), (1,)), ((), ())), precision=HIGH, preferred_element_type=jnp.float32
    )


def fill_sources(chips, wells, rate, q):
    odd, chip, _ = position(chips)
    ny, nz = q.shape[1], q.shape[2]
    lane = lax.broadcasted_iota(jnp.int32, (1, nz), 1)
    q[...] = jnp.zeros_like(q)

    def one(n, carry):
        cell = wells[n]
        x = lax.shift_right_logical(cell, 14)
        y = lax.shift_right_logical(cell, 7) & (ny - 1)
        behind = jnp.where(odd == 1, chip * 8 + 11 - x, x - chip * 8 + 4) & (8 * chips - 1)
        where = (jnp.minimum(behind, q.shape[0] - 1), pl.ds(y, 1), slice(None))
        here = jnp.where(behind < q.shape[0], cell & (nz - 1), -1)
        q[where] = q[where] + jnp.where(lane == here, rate[n], 0.0)
        return carry

    lax.fori_loop(0, wells.shape[0], one, 0, unroll=4)


def order_tables(value, var, noise, tables):
    groups, lanes = value.shape
    wide = lanes // groups
    half = noise.shape[0] // 2
    side = lax.broadcasted_iota(jnp.int32, (1, lanes), 1) // wide
    for g in range(groups):
        total = None
        for j in range(groups):
            where = pl.ds(j * lanes, lanes)
            parts = [noise[2 * n + c : 2 * n + c + 1, where] for c in range(2) for n in range(half)]
            parts += [value[pl.ds(j, 1), :], var[pl.ds(j, 1), :], jnp.ones((6, lanes), jnp.float32)]
            column = pltpu.roll(jnp.concatenate(parts, axis=0), (4 + wide * (j - g)) % lanes, 1)
            total = column if total is None else jnp.where(side == j, column, total)
        tables[g] = total


def solve_kernel(values, tables, columns_in, out_to, coef, columns, out, sems):
    count = columns.shape[1]
    loads = issue([(columns_in.at[:, n], columns.at[:, n]) for n in range(count)], sems, 0)

    groups = tables.shape[0]
    ens = columns.shape[0]
    half = ens // 2
    spaces = groups * 8
    parts = []
    for g in range(groups):
        sides = []
        for core in range(2):
            total = None
            for near in range(4):
                chip = (4 * g + near - core) % (4 * groups)
                row = values[pl.ds(2 * chip + core, half, stride=spaces), :]
                total = row if total is None else total + row
            sides.append(total)
        parts.append(sides)
    lanes = values.shape[1]
    near_lane = (lax.broadcasted_iota(jnp.int32, (half, lanes), 1) & 31) < 8
    ends = [values[pl.ds(at, half, stride=spaces), :] for at in (0, spaces - 1)]
    far = [pltpu.roll(end, lanes - 8, 1) for end in ends]
    for core in range(2):
        own, foreign = ends[core], far[1 - core]
        parts[0][core] = parts[0][core] - own + jnp.where(near_lane, own + foreign, 0.0)
    parts = [jnp.concatenate(sides, axis=0) for sides in parts]
    small = jnp.zeros((ens, ens), jnp.float32)
    right = jnp.zeros((ens, ens), jnp.float32)
    dims = (((1,), (1,)), ((), ()))
    for g in range(groups):
        predicted = parts[g]
        dev = predicted - jnp.mean(predicted, axis=0, keepdims=True)
        spread = INFLATION * tables[g, ens + 1 : ens + 2, :]
        resid = tables[g, ens : ens + 1, :] + jnp.sqrt(spread) * tables[g, 0:ens, :] - predicted
        scaled = dev / spread
        small = small + lax.dot_general(
            scaled, dev, dims, precision=HIGH, preferred_element_type=jnp.float32
        )
        right = right + lax.dot_general(
            scaled, resid, dims, precision=HIGH, preferred_element_type=jnp.float32
        )
    row = lax.broadcasted_iota(jnp.int32, (ens, ens), 0)
    col = lax.broadcasted_iota(jnp.int32, (ens, ens), 1)
    left = small + jnp.where(row == col, ens - 1.0, 0.0)
    for k in range(ens):
        pivot = left[k : k + 1, k : k + 1]
        left_row = left[k : k + 1, :] / pivot
        right_row = right[k : k + 1, :] / pivot
        factor = left[:, k : k + 1]
        here = row == k
        left = jnp.where(here, left_row, left - factor * left_row)
        right = jnp.where(here, right_row, right - factor * right_row)
    mixing = right - jnp.mean(right, axis=0, keepdims=True) + jnp.where(row == col, 1.0, 0.0)
    rows, wide = columns.shape[2], columns.shape[3]

    def natural(place):
        return 2 * place if place < half else 2 * (place - half) + 1

    for j in range(ens):
        for m in range(ens):
            at = natural(j) * ens + natural(m)
            coef[at] = jnp.broadcast_to(mixing[j : j + 1, m : m + 1], (8, wide))

    stores = []
    for n in range(count):
        loads[n].wait()
        part = [columns[j, n] for j in range(ens)]
        for m in range(ens):
            for r0 in range(0, rows, 8):
                total = coef[m] * part[0][r0 : r0 + 8]
                for j in range(1, ens):
                    total = total + coef[j * ens + m] * part[j][r0 : r0 + 8]
                out[m, n, r0 : r0 + 8, :] = total
        stores += issue([(out.at[:, n], out_to.at[:, n])], sems, count + n)
    drain(stores)


def body(
    log_perm,
    saturation,
    pressure_init,
    wells,
    well_rate,
    obs_index,
    obs_weight,
    obs_value,
    obs_var,
    noise,
):
    members, width, ny, nz = log_perm.shape
    spaces = lax.axis_size("space")
    mems = lax.axis_size("mem")
    odd = lax.axis_index("space") % 2
    chips = spaces // 2
    devices = mems * spaces
    ens = members * mems
    grid = (ny, nz)
    f32 = jnp.float32

    def part(field, start, size):
        return lax.dynamic_slice_in_dim(field, start, size, axis=0)

    def plane(count):
        return pltpu.VMEM((count,) + grid, f32)

    def call(kernel, name, **more):
        return pl.pallas_call(
            functools.partial(kernel, chips) if kernel is not third_kernel else kernel,
            name=name,
            **more,
        )

    grant = pltpu.CompilerParams(vmem_limit_bytes=GRANT)
    other = part(log_perm, 1 - odd, 1)[0]
    swap_out = jnp.concatenate([other, saturation, pressure_init])
    swapped = lax.ppermute(swap_out, "space", [(i, i ^ 1) for i in range(spaces)])
    edge_out = jnp.concatenate([other, part(saturation, odd * 2, 2), part(pressure_init, odd, 3)])
    ends = spaces - 1
    edge_in = lax.ppermute(
        edge_out,
        "space",
        [(0, 0), (ends, ends)] + [(i, i + 1 if i % 2 else i - 1) for i in range(1, ends)],
    )
    sems = pltpu.SemaphoreType.DMA((16,))
    scratch = tile_scratch(ny, nz)
    keep, send, perm_tile, q = call(
        first_kernel,
        "first",
        out_shape=(
            plane(PLANES),
            plane(8),
            pltpu.HBM((8,) + grid, f32),
            pltpu.HBM((12,) + grid, f32),
        ),
        in_specs=[SMEM] * 2 + [FAR] * 3 + [VMEM],
        out_specs=(VMEM, VMEM, FAR, FAR),
        scratch_shapes=scratch + [plane(8), plane(4), sems],
        compiler_params=pltpu.CompilerParams(vmem_limit_bytes=GRANT + 1_400_000),
    )(wells, well_rate, log_perm, saturation, pressure_init, near(swapped))
    onward = [(i, i + 2) for i in range(0, ends - 1, 2)] + [(ends - 1, ends)]
    onward += [(i, i - 2) for i in range(3, spaces, 2)] + [(1, 0)]
    back = [(b, a) for a, b in onward]
    got = lax.ppermute(send, "space", onward)
    small = (obs_value.reshape(4, nz), obs_var.reshape(4, nz), noise)
    keep, send, perm_edge, perm_tile, blocks, tables = call(
        second_kernel,
        "second",
        out_shape=(
            plane(PLANES),
            plane(PLANES),
            pltpu.HBM((8,) + grid, f32),
            plane(8),
            pltpu.HBM((mems, members, width, ny // mems, nz), f32),
            jax.ShapeDtypeStruct((4, 16, nz), f32),
        ),
        in_specs=[FAR] * 7 + [VMEM] * 2,
        out_specs=(VMEM, VMEM, FAR, VMEM, FAR, VMEM),
        scratch_shapes=scratch
        + [plane(8), plane(9), pltpu.VMEM(log_perm.shape, f32)]
        + [pltpu.VMEM(table.shape, f32) for table in small]
        + [sems],
        compiler_params=grant,
    )(perm_tile, edge_in, q, log_perm, *small, near(keep), near(got))
    got = lax.ppermute(send, "space", back)
    columns = lax.all_to_all(blocks, "mem", 0, 0, tiled=True).reshape(ens, width, ny // mems, nz)
    keep, send, perm_edge = call(
        third_kernel,
        "third",
        out_shape=(plane(PLANES), plane(PLANES), plane(8)),
        in_specs=[FAR] * 3 + [VMEM] * 3,
        out_specs=(VMEM,) * 3,
        scratch_shapes=scratch + [sems],
        compiler_params=grant,
    )(q, columns, perm_edge, near(perm_tile), near(keep), near(got))
    got = lax.ppermute(send, "space", onward)
    taps = obs_index.T.shape
    values = call(
        last_kernel,
        "last",
        out_shape=pltpu.HBM((devices, nz), f32),
        in_specs=[FAR] * 3 + [VMEM] * 3,
        out_specs=VMEM,
        scratch_shapes=scratch
        + [pltpu.SMEM(taps, jnp.int32), pltpu.SMEM(taps, f32), pltpu.VMEM((nz, nz), f32), sems],
        compiler_params=grant,
    )(q, obs_index.T, obs_weight.T, near(perm_edge), near(keep), near(got))
    values = lax.all_to_all(
        values.reshape(devices, 1, nz), ("mem", "space"), 0, 0, tiled=True
    ).reshape(devices, nz)
    return pl.pallas_call(
        solve_kernel,
        out_shape=jax.ShapeDtypeStruct(columns.shape, f32),
        in_specs=[VMEM, VMEM, FAR],
        out_specs=FAR,
        scratch_shapes=[pltpu.VMEM((ens**2, 8, nz), f32)]
        + [pltpu.VMEM(columns.shape, f32) for _ in range(2)]
        + [sems],
        name="solve",
    )(near(values), near(tables), columns)


def solution(mesh):
    placed = (
        P("mem", "space", None, None),
        P("space", None, None),
        P("space", None, None),
        P(),
        P(),
        P(),
        P(),
        P(),
        P(),
        P(),
    )
    return jax.shard_map(
        body, mesh=mesh, in_specs=placed, out_specs=P(None, "space", "mem", None), check_vma=False
    )
```

```python
import functools

import jax
import jax.numpy as jnp
from jax import lax
from jax.experimental import pallas as pl
from jax.experimental.pallas import tpu as pltpu
from jax.sharding import PartitionSpec as P


INFLATION = 4.0
STEP = 0.1
PAD = 8
CHUNK = 32
HALF = 16
HIGH = lax.Precision.HIGHEST
FAR = pl.BlockSpec(memory_space=pltpu.HBM)
SMEM = pl.BlockSpec(memory_space=pltpu.SMEM)
VMEM = pl.BlockSpec(memory_space=pltpu.VMEM)

S0, P0, S1, P1, S2, L2 = (0, 1), (2, 3, 4), (5, 6, 7), (8, 9, 10), 11, 12
PLANES = 13
GRANT = 56 << 20


def spot(row):
    return row + 1 + (row >= 4)


class Tile:
    def __init__(self, lam_a, lam_b, frac_a, frac_b, p_a, p_b, s_a, s_b, sides, steps, perm, q, q_row, cut):
        self.lam = (lam_a, lam_b)
        self.frac = (frac_a, frac_b)
        self.p = (p_a, p_b)
        self.s = (s_a, s_b)
        self.sides = sides
        self.steps = steps
        self.perm = perm
        self.q = q
        self.q_row = q_row
        self.ny = perm.shape[1]
        self.cut = cut

    def clear(self):
        for ref in self.lam + self.frac + self.p:
            tall, wide = ref.shape[1:]
            edge = jnp.zeros((PAD, wide), jnp.float32)
            for r in range(ref.shape[0]):
                ref[r, 0:PAD, :] = edge
                ref[r, tall - PAD : tall, :] = edge
            ref[5, :, :] = jnp.zeros((tall, wide), jnp.float32)

    def places(self, row):
        st = row + 1 + (row >= 4).astype(jnp.int32)
        joined = 1 - self.cut
        up = st + 1 + jnp.where(row == 3, joined, 0)
        down = st - 1 - jnp.where(row == 4, joined, 0)
        return st, up, down

    def rows(self, first, last, fn):
        def one(row, carry):
            for y0 in range(0, self.ny, CHUNK):
                fn(row, *self.places(row), y0)
            return carry

        lax.fori_loop(first, last + 1, one, 0)

    def run(self, phases, primed=False, then=None):
        def all_of(row, slot, which, chunk):
            for y0 in range(0, self.ny, chunk):
                which(row, *self.places(row), y0, slot)

        if not primed:
            all_of(jnp.int32(phases[0][0]), 0, phases[0][2], phases[0][4])
        for phase, follower in zip(phases, phases[1:] + [then]):
            first, last, ahead, fn, chunk = phase

            def two(n, carry, first=first, ahead=ahead, fn=fn, chunk=chunk):
                row = first + 2 * n
                all_of(row + 1, 1, ahead, chunk)
                all_of(row, 0, fn, chunk)
                all_of(row + 2, 0, ahead, chunk)
                all_of(row + 1, 1, fn, chunk)
                return carry

            lax.fori_loop(0, (last - first) // 2, two, 0)
            all_of(jnp.int32(last), 1, ahead, chunk)
            all_of(jnp.int32(last - 1), 0, fn, chunk)
            if follower is not None:
                all_of(jnp.int32(follower[0]), 0, follower[2], follower[4])
            all_of(jnp.int32(last), 1, fn, chunk)

    def props(self, level, first, last):
        def fn(row, st, up, down, y0):
            inner = pl.ds(y0, CHUNK)
            sat = self.s[level][st, inner, :]
            lam, frac = props(self.perm[row, inner, :], sat)
            self.lam[level][st, pl.ds(PAD + y0, CHUNK), :] = lam
            self.frac[level][st, pl.ds(PAD + y0, CHUNK), :] = frac

        self.rows(first, last, fn)

    def saturate(self, level, first, last):
        lam_r, frac_r, p_r = self.lam[level], self.frac[level], self.p[level]
        new = 1 - level
        lanes = lam_r.shape[2]
        lane = lax.broadcasted_iota(jnp.int32, (CHUNK, lanes), 1)
        is_first, is_last = lane == 0, lane == lanes - 1

        def ahead(row, st, up, down, y0, slot):
            inner = pl.ds(PAD + y0, CHUNK)
            lam, frac, press = lam_r[st, inner, :], frac_r[st, inner, :], p_r[st, inner, :]
            flux = (lam + pltpu.roll(lam, lanes - 1, 1)) * (press - pltpu.roll(press, lanes - 1, 1))
            moved = flux * jnp.where(flux > 0.0, frac, pltpu.roll(frac, lanes - 1, 1))
            edge = jnp.maximum(lam * press, 0.0) * frac
            out = jnp.where(is_last, edge, moved)
            out = out + jnp.where(is_first, edge, pltpu.roll(-moved, 1, 1))
            self.sides[2 * slot, pl.ds(y0, CHUNK), :] = out
            low = 0 if y0 == 0 else PAD + y0
            here = pl.ds(low, PAD + y0 + CHUNK - low)
            after = pl.ds(low + 1, PAD + y0 + CHUNK - low)
            flux = (lam_r[st, here, :] + lam_r[st, after, :]) * (p_r[st, here, :] - p_r[st, after, :])
            self.steps[slot, here, :] = flux * jnp.where(
                flux > 0.0, frac_r[st, here, :], frac_r[st, after, :]
            )

        def fn(row, st, up, down, y0, slot):
            inner = pl.ds(PAD + y0, CHUNK)
            lam, frac, press = lam_r[st, inner, :], frac_r[st, inner, :], p_r[st, inner, :]

            def face(index, where):
                flux = (lam + lam_r[index, where, :]) * (press - p_r[index, where, :])
                return flux * jnp.where(flux > 0.0, frac, frac_r[index, where, :])

            out = face(up, inner) + face(down, inner)
            out = out + self.steps[slot, inner, :] - self.steps[slot, pl.ds(PAD + y0 - 1, CHUNK), :]
            out = out + self.sides[2 * slot, pl.ds(y0, CHUNK), :]
            q = self.q[self.q_row(row), pl.ds(y0, CHUNK), :]
            water = q * jnp.where(q > 0.0, 1.0, frac)
            sat = self.s[level][st, pl.ds(y0, CHUNK), :]
            sat = jnp.clip(sat + STEP * (water - out), 0.0, 1.0)
            self.s[new][st, pl.ds(y0, CHUNK), :] = sat
            lam, frac = props(self.perm[row, pl.ds(y0, CHUNK), :], sat)
            self.lam[new][st, inner, :] = lam
            self.frac[new][st, inner, :] = frac

        return first, last, ahead, fn, CHUNK

    def pressure(self, level, first, last):
        new = 1 - level
        lam_r, p_r, out_r = self.lam[new], self.p[level], self.p[new]
        lanes = lam_r.shape[2]
        lane = lax.broadcasted_iota(jnp.int32, (HALF, lanes), 1)
        not_first, not_last = lane > 0, lane < lanes - 1

        def ahead(row, st, up, down, y0, slot):
            inner = pl.ds(PAD + y0, HALF)
            lam, press = lam_r[st, inner, :], p_r[st, inner, :]
            numer, denom = 0.0, 0.0
            for shift, mask in ((lanes - 1, not_last), (1, not_first)):
                trans = lam + jnp.where(mask, pltpu.roll(lam, shift, 1), 0.0)
                numer = numer + trans * jnp.where(mask, pltpu.roll(press, shift, 1), 0.0)
                denom = denom + trans
            self.sides[2 * slot, pl.ds(y0, HALF), :] = numer
            self.sides[2 * slot + 1, pl.ds(y0, HALF), :] = denom

        def fn(row, st, up, down, y0, slot):
            inner = pl.ds(PAD + y0, HALF)
            lam, press = lam_r[st, inner, :], p_r[st, inner, :]
            numer = press + self.q[self.q_row(row), pl.ds(y0, HALF), :]
            numer = numer + self.sides[2 * slot, pl.ds(y0, HALF), :]
            denom = 1.0 + self.sides[2 * slot + 1, pl.ds(y0, HALF), :]
            for index, where in (
                (up, inner),
                (down, inner),
                (st, pl.ds(PAD + y0 + 1, HALF)),
                (st, pl.ds(PAD + y0 - 1, HALF)),
            ):
                trans = lam + lam_r[index, where, :]
                numer = numer + trans * p_r[index, where, :]
                denom = denom + trans
            out_r[st, inner, :] = numer / denom

        return first, last, ahead, fn, HALF


def props(perm_half, sat):
    water = sat * sat
    oil = (1.0 - sat) * (1.0 - sat) * 0.25
    total = water + oil
    return perm_half * total, water / total


def near(array):
    return pltpu.with_memory_space_constraint(array, pltpu.VMEM)


def tile_scratch(ny, nz):
    tall = ny + 2 * PAD
    wide = [pltpu.VMEM((11, tall, nz), jnp.float32) for _ in range(6)]
    flat = [pltpu.VMEM((count, ny, nz), jnp.float32) for count in (11, 11, 4, 12)]
    flat.insert(3, pltpu.VMEM((2, ny + PAD, nz), jnp.float32))
    return wide + flat


def issue(pairs, sems, first):
    copies = []
    for n, (src, dst) in enumerate(pairs):
        copy = pltpu.make_async_copy(src, dst, sems.at[first + n])
        copy.start()
        copies.append(copy)
    return copies


def drain(copies):
    for copy in copies:
        copy.wait()


def move(pairs):
    tall = min(src.shape[0] for src, _ in pairs)

    def one(n, carry):
        where = pl.ds(pl.multiple_of(n * CHUNK, CHUNK), CHUNK)
        for src, dst in pairs:
            dst[where, :] = src[where, :]
        return carry

    lax.fori_loop(0, tall // CHUNK, one, 0)


def position(chips):
    place = lax.axis_index("space")
    odd, chip = place & 1, lax.shift_right_logical(place, 1)
    end = jnp.where(odd == 1, chips - 1, 0)
    return odd, chip, (chip == end).astype(jnp.int32)


def beyond(tile, row):
    return jnp.where(tile.cut == 1, 5, spot(row))


def give_early(tile, keep, send, send_early):
    pairs = []
    inner = pl.ds(PAD, tile.ny)
    sides = [(keep, lambda d: d)] + ([(send, lambda d: 7 - d)] if send_early else [])
    for out, row in sides:
        for d in range(2):
            pairs.append((tile.s[0].at[spot(row(d))], out.at[S0[d]]))
        for d in range(3):
            pairs.append((tile.p[0].at[spot(row(d)), inner], out.at[P0[d]]))
    return pairs


def give_late(tile, out, near, base):
    row, step = near
    inner = pl.ds(PAD, tile.ny)
    pairs = []
    for n, d in enumerate((1, 2, 3)):
        pairs.append((tile.s[1].at[spot(row + step * d)], out.at[S1[n] - base]))
    for n, d in enumerate((2, 3, 4)):
        st = beyond(tile, row + step * d) if d == 4 else spot(row + step * d)
        pairs.append((tile.p[1].at[st, inner], out.at[P1[n] - base]))
    return pairs


def give_last(tile, out, near, base):
    row, step = near
    inner = pl.ds(PAD, tile.ny)
    return [
        (tile.s[0].at[spot(row + step * 3)], out.at[S2 - base]),
        (tile.lam[0].at[beyond(tile, row + step * 4), inner], out.at[L2 - base]),
    ]


def take(tile, early, late, base_row, step):
    inner = pl.ds(PAD, tile.ny)
    start, s_next, p_next, last = [], [], [], []
    for d in range(2):
        start.append((early(S0[d]), tile.s[0].at[base_row + step * d]))
    for d in range(3):
        start.append((early(P0[d]), tile.p[0].at[base_row + step * d, inner]))
    for n, d in enumerate((1, 2, 3)):
        s_next.append((late(S1[n]), tile.s[1].at[base_row + step * d]))
    for n, d in enumerate((2, 3, 4)):
        p_next.append((late(P1[n]), tile.p[1].at[base_row + step * d, inner]))
    last.append((late(S2), tile.s[0].at[base_row + step * 3]))
    last.append((late(L2), tile.lam[0].at[base_row + step * 4, inner]))
    return start, s_next, p_next, last


def advance(tile, keep, send, send_early, primed=True):
    base = 0 if send_early else S1[0]
    move(give_early(tile, keep, send, send_early))
    tile.run([tile.saturate(0, 1, 6), tile.pressure(0, 2, 5), tile.saturate(1, 3, 4)], primed)
    pairs = []
    for out, near_row, at in ((send, (7, -1), base), (keep, (0, 1), 0)):
        pairs += give_late(tile, out, near_row, at) + give_last(tile, out, near_row, at)
    move(pairs)


def first_kernel(chips, wells, rate, log_perm, own_sat, own_press, swapped, keep, send, perm, q_out, *refs):
    odd, _, _ = position(chips)
    raw, sems = refs[11:]
    tile = Tile(*refs[:10], perm, refs[10], lambda row: row + 4, jnp.int32(0))
    inner = pl.ds(PAD, tile.ny)

    def place(n):
        return jnp.where(odd == 1, 3 - n, n)

    pairs = [(log_perm.at[odd], raw)]
    for n in range(4):
        pairs.append((own_sat.at[place(n)], tile.s[0].at[spot(n)]))
        pairs.append((own_press.at[place(n)], tile.p[0].at[spot(n), inner]))
    copies = issue(pairs, sems, 0)
    tile.clear()
    fill_sources(chips, wells, rate, tile.q)
    out_copies = issue([(tile.q, q_out)], sems, 9)
    pairs = []
    for n in range(4):
        pairs.append((swapped.at[4 + place(n)], tile.s[0].at[spot(4 + n)]))
        pairs.append((swapped.at[8 + place(n)], tile.p[0].at[spot(4 + n), inner]))
    move(pairs)

    def halve(src, base):
        def one(n, carry):
            for y0 in range(0, tile.ny, CHUNK):
                where = pl.ds(y0, CHUNK)
                perm[base + n, where, :] = 0.5 * jnp.exp(src[place(n), where, :])
            return carry

        lax.fori_loop(0, 4, one, 0)

    halve(swapped, 4)
    drain(copies)
    halve(raw, 0)
    tile.props(0, 0, 7)
    advance(tile, keep, send, False, False)
    drain(out_copies)


def fill(tile, sides, q_copy, then=None):
    tile.props(0, 2, 5)
    tile.props(1, 0, 2)
    tile.props(1, 5, 7)
    drain(q_copy)
    move(sides[0][3] + sides[1][3])
    tile.props(0, 0, 0)
    tile.props(0, 7, 7)
    tile.run(
        [
            tile.saturate(0, 3, 4),
            tile.pressure(0, 2, 5),
            tile.saturate(1, 1, 6),
            tile.pressure(1, 0, 7),
        ],
        then=then,
    )


def edge_q(cut):
    return lambda row: jnp.where((cut == 1) & (row >= 4), row, 7 - row)


def second_kernel(
    chips, q, log_perm, value_in, var_in, noise_in, perm_own, raw, kept, late_in,
    keep, send, perm_out, blocks, tables, *refs
):
    odd, _, end = position(chips)
    perm, held, value, var, noise, sems = refs[11:]
    tile = Tile(*refs[:10], perm, refs[10], edge_q(end), end)
    straight = odd ^ end

    def place(n, count):
        return jnp.where(straight == 1, n, count - 1 - n)

    def early(plane):
        if plane in S0:
            return raw.at[4 + place(plane, 2)]
        return raw.at[6 + place(plane - 2, 3)]

    q_copy = issue([(q, tile.q)], sems, 5)
    load = issue(
        [(log_perm, held), (value_in, value), (var_in, var), (noise_in, noise)], sems, 7
    )
    sides = (
        take(tile, lambda n: kept.at[n], lambda n: kept.at[n], 4, -1),
        take(tile, early, lambda n: late_in.at[n - S1[0]], 6, 1),
    )
    tile.clear()
    move(sum((side[n] for side in sides for n in range(3)), []))

    def permeability(d, carry):
        for y0 in range(0, tile.ny, CHUNK):
            where = pl.ds(y0, CHUNK)
            perm[3 - d, where, :] = perm_own[d, where, :]
            perm[4 + d, where, :] = 0.5 * jnp.exp(raw[place(d, 4), where, :])
        return carry

    lax.fori_loop(0, 4, permeability, 0)
    perm_copy = issue([(perm, perm_out)], sems, 6)
    fill(tile, sides, q_copy, tile.saturate(0, 1, 6))
    drain(load)
    count = blocks.shape[0]
    rows = log_perm.shape[2] // count
    pieces = issue(
        [(held.at[:, :, pl.ds(b * rows, rows), :], blocks.at[b]) for b in range(count)], sems, 12
    )
    order_tables(value, var, noise, tables)
    advance(tile, keep, send, True)
    drain(perm_copy)
    drain(pieces)


def both_sides(tile, kept, got):
    return (
        take(tile, lambda n: kept.at[n], lambda n: kept.at[n], 4, -1),
        take(tile, lambda n: got.at[n], lambda n: got.at[n], 6, 1),
    )


def gather(tile, kept, got):
    sides = both_sides(tile, kept, got)
    tile.clear()
    move(sum((side[n] for side in sides for n in range(3)), []))
    return sides


def third_kernel(q, columns, perm_later, perm, kept, got, keep, send, perm_next, *refs):
    del columns
    tile = Tile(*refs[:10], perm, refs[10], lambda row: row + 4, jnp.int32(0))
    sems = refs[11]
    q_copy = issue([(q, tile.q)], sems, 0)
    hand_on = issue([(perm_later, perm_next)], sems, 1)
    fill(tile, gather(tile, kept, got), q_copy, tile.saturate(0, 1, 6))
    advance(tile, keep, send, True)
    drain(hand_on)


def last_kernel(chips, q, index_in, weight_in, perm, kept, got, values, *refs):
    odd, chip, end = position(chips)
    tile = Tile(*refs[:10], perm, refs[10], edge_q(end), end)
    index, weight, picked, sems = refs[11:]
    q_copy = issue([(q, tile.q)], sems, 1)
    tables = issue([(index_in, index), (weight_in, weight)], sems, 2)
    fill(tile, gather(tile, kept, got), q_copy)
    drain(tables)
    around = (chip + odd) & (chips - 1)
    total_rows = 8 * chips
    per = index.shape[1] // total_rows
    lanes = kept.shape[2]
    lane = lax.broadcasted_iota(jnp.int32, (1, lanes), 1)
    picked[...] = jnp.zeros_like(picked)

    def one(n, carry):
        slot = n & 7
        row = jnp.where(odd == 1, slot, 7 - slot)
        st = row + 1 + (row >= 4).astype(jnp.int32)
        other = end * (row >= 4).astype(jnp.int32)
        slot = jnp.where(other == 1, 7 - slot, slot)
        column = lax.shift_right_logical(n, 3)
        obs = column * total_rows + ((8 * around - 4 + slot) & (total_rows - 1))
        total = jnp.zeros((1, lanes), jnp.float32)
        for t in range(index.shape[0]):
            cell = index[t, obs]
            y = lax.shift_right_logical(cell, 7) & (tile.ny - 1)
            values_row = tile.p[0][st, pl.ds(PAD + y, 1), :]
            total = total + jnp.where(lane == (cell & (lanes - 1)), values_row, 0.0) * weight[t, obs]
        at = column * 32 + ((around & 3) + other) * 8 + slot
        picked[pl.ds(at, 1), :] = total
        return carry

    lax.fori_loop(0, 8 * per, one, 0, unroll=4)
    ones = jnp.ones((values.shape[0], lanes), jnp.float32)
    values[...] = lax.dot_general(
        ones, picked[...], (((1,), (1,)), ((), ())), precision=HIGH, preferred_element_type=jnp.float32
    )


def fill_sources(chips, wells, rate, q):
    odd, chip, _ = position(chips)
    ny, nz = q.shape[1], q.shape[2]
    lane = lax.broadcasted_iota(jnp.int32, (1, nz), 1)
    q[...] = jnp.zeros_like(q)

    def one(n, carry):
        cell = wells[n]
        x = lax.shift_right_logical(cell, 14)
        y = lax.shift_right_logical(cell, 7) & (ny - 1)
        behind = jnp.where(odd == 1, chip * 8 + 11 - x, x - chip * 8 + 4) & (8 * chips - 1)
        where = (jnp.minimum(behind, q.shape[0] - 1), pl.ds(y, 1), slice(None))
        here = jnp.where(behind < q.shape[0], cell & (nz - 1), -1)
        q[where] = q[where] + jnp.where(lane == here, rate[n], 0.0)
        return carry

    lax.fori_loop(0, wells.shape[0], one, 0, unroll=4)


def order_tables(value, var, noise, tables):
    groups, lanes = value.shape
    wide = lanes // groups
    half = noise.shape[0] // 2
    side = lax.broadcasted_iota(jnp.int32, (1, lanes), 1) // wide
    for g in range(groups):
        total = None
        for j in range(groups):
            where = pl.ds(j * lanes, lanes)
            parts = [noise[2 * n + c : 2 * n + c + 1, where] for c in range(2) for n in range(half)]
            parts += [value[pl.ds(j, 1), :], var[pl.ds(j, 1), :], jnp.ones((6, lanes), jnp.float32)]
            column = pltpu.roll(jnp.concatenate(parts, axis=0), (4 + wide * (j - g)) % lanes, 1)
            total = column if total is None else jnp.where(side == j, column, total)
        tables[g] = total


def solve_kernel(values, tables, columns_in, out_to, coef, columns, out, sems):
    count = columns.shape[1]
    loads = issue([(columns_in.at[:, n], columns.at[:, n]) for n in range(count)], sems, 0)

    groups = tables.shape[0]
    ens = columns.shape[0]
    half = ens // 2
    spaces = groups * 8
    parts = []
    for g in range(groups):
        sides = []
        for core in range(2):
            total = None
            for near in range(4):
                chip = (4 * g + near - core) % (4 * groups)
                row = values[pl.ds(2 * chip + core, half, stride=spaces), :]
                total = row if total is None else total + row
            sides.append(total)
        parts.append(sides)
    lanes = values.shape[1]
    near_lane = (lax.broadcasted_iota(jnp.int32, (half, lanes), 1) & 31) < 8
    ends = [values[pl.ds(at, half, stride=spaces), :] for at in (0, spaces - 1)]
    far = [pltpu.roll(end, lanes - 8, 1) for end in ends]
    for core in range(2):
        own, foreign = ends[core], far[1 - core]
        parts[0][core] = parts[0][core] - own + jnp.where(near_lane, own + foreign, 0.0)
    parts = [jnp.concatenate(sides, axis=0) for sides in parts]
    small = jnp.zeros((ens, ens), jnp.float32)
    right = jnp.zeros((ens, ens), jnp.float32)
    dims = (((1,), (1,)), ((), ()))
    for g in range(groups):
        predicted = parts[g]
        dev = predicted - jnp.mean(predicted, axis=0, keepdims=True)
        spread = INFLATION * tables[g, ens + 1 : ens + 2, :]
        resid = tables[g, ens : ens + 1, :] + jnp.sqrt(spread) * tables[g, 0:ens, :] - predicted
        scaled = dev / spread
        small = small + lax.dot_general(
            scaled, dev, dims, precision=HIGH, preferred_element_type=jnp.float32
        )
        right = right + lax.dot_general(
            scaled, resid, dims, precision=HIGH, preferred_element_type=jnp.float32
        )
    row = lax.broadcasted_iota(jnp.int32, (ens, ens), 0)
    col = lax.broadcasted_iota(jnp.int32, (ens, ens), 1)
    left = small + jnp.where(row == col, ens - 1.0, 0.0)
    for k in range(ens):
        pivot = left[k : k + 1, k : k + 1]
        left_row = left[k : k + 1, :] / pivot
        right_row = right[k : k + 1, :] / pivot
        factor = left[:, k : k + 1]
        here = row == k
        left = jnp.where(here, left_row, left - factor * left_row)
        right = jnp.where(here, right_row, right - factor * right_row)
    mixing = right - jnp.mean(right, axis=0, keepdims=True) + jnp.where(row == col, 1.0, 0.0)
    rows, wide = columns.shape[2], columns.shape[3]

    def natural(place):
        return 2 * place if place < half else 2 * (place - half) + 1

    for j in range(ens):
        for m in range(ens):
            at = natural(j) * ens + natural(m)
            coef[at] = jnp.broadcast_to(mixing[j : j + 1, m : m + 1], (8, wide))

    stores = []
    for n in range(count):
        loads[n].wait()
        part = [columns[j, n] for j in range(ens)]
        for m in range(ens):
            for r0 in range(0, rows, 8):
                total = coef[m] * part[0][r0 : r0 + 8]
                for j in range(1, ens):
                    total = total + coef[j * ens + m] * part[j][r0 : r0 + 8]
                out[m, n, r0 : r0 + 8, :] = total
        stores += issue([(out.at[:, n], out_to.at[:, n])], sems, count + n)
    drain(stores)


def body(
    log_perm,
    saturation,
    pressure_init,
    wells,
    well_rate,
    obs_index,
    obs_weight,
    obs_value,
    obs_var,
    noise,
):
    members, width, ny, nz = log_perm.shape
    spaces = lax.axis_size("space")
    mems = lax.axis_size("mem")
    odd = lax.axis_index("space") % 2
    chips = spaces // 2
    devices = mems * spaces
    ens = members * mems
    grid = (ny, nz)
    f32 = jnp.float32

    def part(field, start, size):
        return lax.dynamic_slice_in_dim(field, start, size, axis=0)

    def plane(count):
        return pltpu.VMEM((count,) + grid, f32)

    def call(kernel, name, **more):
        return pl.pallas_call(
            functools.partial(kernel, chips) if kernel is not third_kernel else kernel,
            name=name,
            **more,
        )

    grant = pltpu.CompilerParams(vmem_limit_bytes=GRANT)
    other = part(log_perm, 1 - odd, 1)[0]
    swap_out = jnp.concatenate([other, saturation, pressure_init])
    swapped = lax.ppermute(swap_out, "space", [(i, i ^ 1) for i in range(spaces)])
    edge_out = jnp.concatenate([other, part(saturation, odd * 2, 2), part(pressure_init, odd, 3)])
    ends = spaces - 1
    edge_in = lax.ppermute(
        edge_out,
        "space",
        [(0, 0), (ends, ends)] + [(i, i + 1 if i % 2 else i - 1) for i in range(1, ends)],
    )
    sems = pltpu.SemaphoreType.DMA((16,))
    scratch = tile_scratch(ny, nz)
    keep, send, perm_tile, q = call(
        first_kernel,
        "first",
        out_shape=(
            plane(PLANES),
            plane(8),
            plane(8),
            pltpu.HBM((12,) + grid, f32),
        ),
        in_specs=[SMEM] * 2 + [FAR] * 3 + [VMEM],
        out_specs=(VMEM, VMEM, VMEM, FAR),
        scratch_shapes=scratch + [plane(4), sems],
        compiler_params=pltpu.CompilerParams(vmem_limit_bytes=GRANT + 1_400_000),
    )(wells, well_rate, log_perm, saturation, pressure_init, near(swapped))
    onward = [(i, i + 2) for i in range(0, ends - 1, 2)] + [(ends - 1, ends)]
    onward += [(i, i - 2) for i in range(3, spaces, 2)] + [(1, 0)]
    back = [(b, a) for a, b in onward]
    got = lax.ppermute(send, "space", onward)
    small = (obs_value.reshape(4, nz), obs_var.reshape(4, nz), noise)
    keep, send, perm_edge, blocks, tables = call(
        second_kernel,
        "second",
        out_shape=(
            plane(PLANES),
            plane(PLANES),
            pltpu.HBM((8,) + grid, f32),
            pltpu.HBM((mems, members, width, ny // mems, nz), f32),
            jax.ShapeDtypeStruct((4, 16, nz), f32),
        ),
        in_specs=[FAR] * 5 + [VMEM] * 4,
        out_specs=(VMEM, VMEM, FAR, FAR, VMEM),
        scratch_shapes=scratch
        + [plane(8), pltpu.VMEM(log_perm.shape, f32)]
        + [pltpu.VMEM(table.shape, f32) for table in small]
        + [sems],
        compiler_params=grant,
    )(q, log_perm, *small, near(perm_tile), near(edge_in), near(keep), near(got))
    got = lax.ppermute(send, "space", back)
    columns = lax.all_to_all(blocks, "mem", 0, 0, tiled=True).reshape(ens, width, ny // mems, nz)
    keep, send, perm_edge = call(
        third_kernel,
        "third",
        out_shape=(plane(PLANES), plane(PLANES), plane(8)),
        in_specs=[FAR] * 3 + [VMEM] * 3,
        out_specs=(VMEM,) * 3,
        scratch_shapes=scratch + [sems],
        compiler_params=grant,
    )(q, columns, perm_edge, near(perm_tile), near(keep), near(got))
    got = lax.ppermute(send, "space", onward)
    taps = obs_index.T.shape
    values = call(
        last_kernel,
        "last",
        out_shape=pltpu.HBM((devices, nz), f32),
        in_specs=[FAR] * 3 + [VMEM] * 3,
        out_specs=VMEM,
        scratch_shapes=scratch
        + [pltpu.SMEM(taps, jnp.int32), pltpu.SMEM(taps, f32), pltpu.VMEM((nz, nz), f32), sems],
        compiler_params=grant,
    )(q, obs_index.T, obs_weight.T, near(perm_edge), near(keep), near(got))
    values = lax.all_to_all(
        values.reshape(devices, 1, nz), ("mem", "space"), 0, 0, tiled=True
    ).reshape(devices, nz)
    return pl.pallas_call(
        solve_kernel,
        out_shape=jax.ShapeDtypeStruct(columns.shape, f32),
        in_specs=[VMEM, VMEM, FAR],
        out_specs=FAR,
        scratch_shapes=[pltpu.VMEM((ens**2, 8, nz), f32)]
        + [pltpu.VMEM(columns.shape, f32) for _ in range(2)]
        + [sems],
        name="solve",
    )(near(values), near(tables), columns)


def solution(mesh):
    placed = (
        P("mem", "space", None, None),
        P("space", None, None),
        P("space", None, None),
        P(),
        P(),
        P(),
        P(),
        P(),
        P(),
        P(),
    )
    return jax.shard_map(
        body, mesh=mesh, in_specs=placed, out_specs=P(None, "space", "mem", None), check_vma=False
    )
```
